32 devices in a mesh: ctx: 32 (over z, y, x, core).
Axes of the slice: x: 2, y: 2, z: 4, core: 2. Of those that a mesh axis runs over, the one named last changes fastest.
Arguments:
- tokens: bfloat16 [16384, 1536], P('ctx'), may hold values from -6 to 6
- cotangent: bfloat16 [16384, 1536], P('ctx'), may hold values from -6 to 6
- doc_lengths: int32 [8], replicated, may hold values from 1 to 8192, 16384 in all
- adapter_ids: int32 [8], replicated, may hold values from 0 to 7
- w_query: bfloat16 [1536, 1536], P('ctx'), may hold values from -0.15625 to 0.15625
- w_keyval: bfloat16 [1536, 256], P('ctx'), may hold values from -0.15625 to 0.15625
- w_output: bfloat16 [1536, 1536], P('ctx'), may hold values from -2.5 to 2.5
- w_gateup: bfloat16 [1536, 9216], P('ctx'), may hold values from -0.15625 to 0.15625
- w_down: bfloat16 [4608, 1536], P('ctx'), may hold values from -0.09375 to 0.09375
- gain_attn: float32 [1536], replicated, may hold values from 0.25 to 1.75
- gain_mlp: float32 [1536], replicated, may hold values from 0.25 to 1.75
- query_a: bfloat16 [1536, 128], replicated, may hold values from -0.15625 to 0.15625
- query_b: bfloat16 [128, 1536], replicated, may hold values from -0.75 to 0.75
- keyval_a: bfloat16 [1536, 128], replicated, may hold values from -0.15625 to 0.15625
- keyval_b: bfloat16 [128, 256], replicated, may hold values from -0.75 to 0.75
- output_a: bfloat16 [1536, 128], replicated, may hold values from -0.15625 to 0.15625
- output_b: bfloat16 [128, 1536], replicated, may hold values from -0.75 to 0.75
- gateup_a: bfloat16 [1536, 128], replicated, may hold values from -0.15625 to 0.15625
- gateup_b: bfloat16 [128, 9216], replicated, may hold values from -0.75 to 0.75
- down_a: bfloat16 [4608, 128], replicated, may hold values from -0.09375 to 0.09375
- down_b: bfloat16 [128, 1536], replicated, may hold values from -0.75 to 0.75
Outputs:
- out: bfloat16 [16384, 1536], P('ctx')
- grad_tokens: bfloat16 [16384, 1536], P('ctx')
- grad_query_a: float32 [1536, 128], replicated
- grad_query_b: float32 [128, 1536], replicated
- grad_keyval_a: float32 [1536, 128], replicated
- grad_keyval_b: float32 [128, 256], replicated
- grad_output_a: float32 [1536, 128], replicated
- grad_output_b: float32 [128, 1536], replicated
- grad_gateup_a: float32 [1536, 128], replicated
- grad_gateup_b: float32 [128, 9216], replicated
- grad_down_a: float32 [4608, 128], replicated
- grad_down_b: float32 [128, 1536], replicated
The draws below stay inside these ranges and needn't reach their ends.
Inputs may be any that keep to these rules, and one draw needn't show every extreme that they name: `doc_lengths`: the documents follow one another over all 16384 positions; the longest has exactly 8192 tokens.
All inputs are finite; a program needn't handle non-finite values.
Results may differ from the reference program's by a relative error of at most 0.015.
Values may be sent and summed in bfloat16 or wider, within the bound.
A program may use at most 320 MiB of HBM per device.

```python
import math
import jax
import jax.numpy as jnp
import numpy as np
from jax import lax

D = 1536
HEADS = 12
HD = 128
QW = 1536
FF = 4608
WINDOW = 1024
RANK = 16
ADAPTERS = 8
AR = 128
TOK_DEV = 512
TOKENS = 16384
REACH = 4
DOC_MOST = 8192
DOCS = 8
N_CTX = 32


def plant(array, key, least, high):
    longest = array.shape.index(max(array.shape))
    spots = []
    for shift in (0, 1):
        where = [jax.random.randint(jax.random.fold_in(key, axis), (), 0, length) for axis, length in enumerate(array.shape)]
        where[longest] = (where[longest] + shift) % array.shape[longest]
        spots.append(tuple(where))
    return array.at[spots[0]].set(least).at[spots[1]].set(high)


def block_scale(own_key, dims, shards, least, largest):
    factor_of, own = 1.0, jax.random.fold_in(own_key, 6)
    for axis_at, blocks in shards:
        steps = jnp.exp(jax.random.uniform(jax.random.fold_in(own, axis_at), (blocks,), jnp.float32, least / len(shards), largest / len(shards)))
        factor_of = factor_of * jnp.repeat(steps, dims[axis_at] // blocks).reshape([-1 if axis == axis_at else 1 for axis in range(len(dims))])
    return factor_of


def split_up(amount, total, most, lean):
    loads = [(1 << 20) // math.isqrt(standing ** lean) + 1 for standing in range(2, amount + 1)]
    surplus, counts = total - most - (amount - 1), [1] * (amount - 1)
    while surplus > 0:
        candidates = [i for i in range(amount - 1) if counts[i] < most]
        pool, budget = sum([loads[i] for i in candidates]), surplus
        for i in candidates:
            extra = min(most - counts[i], max(1, budget * loads[i] // pool), surplus)
            counts[i] = counts[i] + extra
            surplus = surplus - extra
    return np.array([most] + counts)


def ragged(stream_key, count, total, limit, skew):
    if count == 2:
        one = jax.random.randint(stream_key, (), max(1, total - limit), min(limit, total - 1) + 1)
        return jnp.stack([one, total - one])
    sizes = jnp.asarray(split_up(count, total, limit, skew), jnp.int32)
    twos = (count - 1) // 2
    source_of, sink = sizes[1:1 + 2 * twos:2], sizes[2:2 + 2 * twos:2]
    room = jnp.minimum(source_of - 1, limit - sink)
    moved = jax.random.randint(jax.random.fold_in(stream_key, 1), (twos,), 0, 1 << 20) % (room + 1)
    sizes = sizes.at[1:1 + 2 * twos:2].set(source_of - moved).at[2:2 + 2 * twos:2].set(sink + moved)
    return sizes[jax.random.permutation(jax.random.fold_in(stream_key, 2), count)]


def gaussian(rng, dims, scale, most, shards=(), held_as=jnp.bfloat16):
    drawn = scale * jax.random.normal(rng, dims, jnp.float32)
    if shards:
        drawn = drawn * block_scale(rng, dims, shards, -0.22, 0.18)
    return jnp.clip(drawn, -most, most).astype(held_as)


def setup_inputs(seed: int = 0) -> dict:
    arg_keys = jax.random.split(jax.random.key(seed), 22)
    return {
        "tokens": gaussian(arg_keys[0], (TOKENS, D), 1.0, 6.0, ((0, 32),)),
        "cotangent": gaussian(arg_keys[1], (TOKENS, D), 1.0, 6.0, ((0, 32),)),
        "doc_lengths": ragged(arg_keys[2], DOCS, TOKENS, DOC_MOST, 2).astype(jnp.int32),
        "adapter_ids": plant(jax.random.randint(arg_keys[3], (DOCS,), 0, ADAPTERS), jax.random.fold_in(arg_keys[3], 1), 0, ADAPTERS - 1).astype(jnp.int32),
        "w_query": gaussian(arg_keys[4], (D, QW), D ** -0.5, 0.15625, ((0, 32),)),
        "w_keyval": gaussian(arg_keys[5], (D, 2 * HD), D ** -0.5, 0.15625, ((0, 32),)),
        "w_output": gaussian(arg_keys[6], (QW, D), (max(1, QW // 256)) ** -0.5, 2.5, ((0, 32),)),
        "w_gateup": gaussian(arg_keys[7], (D, 2 * FF), D ** -0.5, 0.15625, ((0, 32),)),
        "w_down": gaussian(arg_keys[8], (FF, D), FF ** -0.5, 0.09375, ((0, 32),)),
        "gain_attn": jnp.clip(1.0 + 0.15 * jax.random.normal(arg_keys[9], (D,), jnp.float32), 0.25, 1.75),
        "gain_mlp": jnp.clip(1.0 + 0.15 * jax.random.normal(arg_keys[10], (D,), jnp.float32), 0.25, 1.75),
        "query_a": gaussian(arg_keys[11], (D, AR), D ** -0.5, 0.15625),
        "query_b": gaussian(arg_keys[12], (AR, QW), (4 * RANK) ** -0.5, 0.75),
        "keyval_a": gaussian(arg_keys[13], (D, AR), D ** -0.5, 0.15625),
        "keyval_b": gaussian(arg_keys[14], (AR, 2 * HD), (4 * RANK) ** -0.5, 0.75),
        "output_a": gaussian(arg_keys[15], (QW, AR), QW ** -0.5, 0.15625),
        "output_b": gaussian(arg_keys[16], (AR, D), (4 * RANK) ** -0.5, 0.75),
        "gateup_a": gaussian(arg_keys[17], (D, AR), D ** -0.5, 0.15625),
        "gateup_b": gaussian(arg_keys[18], (AR, 2 * FF), (4 * RANK) ** -0.5, 0.75),
        "down_a": gaussian(arg_keys[19], (FF, AR), FF ** -0.5, 0.09375),
        "down_b": gaussian(arg_keys[20], (AR, D), (4 * RANK) ** -0.5, 0.75),
    }


HIGH = lax.Precision.HIGHEST
NORM_EPS = 1e-06
MASKED = -1e+30

@jax.custom_vjp
def low(v):
    return lax.optimization_barrier(v.astype(jnp.bfloat16)).astype(jnp.float32)

@jax.custom_vjp
def low_back(v):
    return v

def low_keep(v):
    return (low(v), None)

def low_pass(kept, grad):
    return (grad,)

def back_keep(v):
    return (v, None)

def back_low(kept, grad):
    return (low(grad),)
low.defvjp(low_keep, low_pass)
low_back.defvjp(back_keep, back_low)

def to_natural(stored):
    width = stored.shape[-1]
    halves = stored.reshape(N_CTX, 2, TOK_DEV // 2, width)
    return jnp.concatenate([halves[:, 0], halves[::-1, 1]], axis=0).reshape(-1, width)

def to_stored(natural):
    width = natural.shape[-1]
    blocks = natural.reshape(2, N_CTX, TOK_DEV // 2, width)
    return jnp.stack([blocks[0], blocks[1][::-1]], axis=1).reshape(-1, width)

def segment_of(doc_lengths, positions):
    starts = jnp.cumsum(doc_lengths) - doc_lengths
    return lax.optimization_barrier(jnp.sum((starts[None, :] <= positions[:, None]).astype(jnp.int32), axis=1)) - 1

def adapter_mask(doc_lengths, adapter_ids, positions):
    segment = segment_of(doc_lengths, positions)
    owner = segment[:, None] == jnp.arange(doc_lengths.shape[0], dtype=jnp.int32)[None, :]
    chosen = lax.optimization_barrier(jnp.sum(jnp.where(owner, adapter_ids[None, :], 0), axis=1))
    columns = jnp.arange(ADAPTERS * RANK, dtype=jnp.int32) // RANK
    return (segment, (columns[None, :] == chosen[:, None]).astype(jnp.float32))

def rms_scale(values, gain):
    return values * lax.rsqrt(lax.optimization_barrier(jnp.mean(values * values, axis=-1, keepdims=True)) + NORM_EPS) * gain

def adapted(inputs, weight, down_part, up_part, mask):
    main = jnp.dot(inputs, weight, precision=HIGH)
    inner = low_back(low(jnp.dot(inputs, down_part, precision=HIGH) * mask))
    return main + jnp.dot(inner, up_part, precision=HIGH)

def attend_all(query, keyval, segment, positions):
    width = TOK_DEV // 2
    reach = REACH
    span = (reach + 1) * width
    pad_keys = jnp.concatenate([jnp.zeros((reach * width, 2 * HD), keyval.dtype), keyval], axis=0)
    pad_seg = jnp.concatenate([jnp.full((reach * width,), -1, jnp.int32), segment])
    pad_pos = jnp.concatenate([jnp.arange(-reach * width, 0, dtype=jnp.int32), positions])

    def one_block(index):
        start = index * width
        keys = lax.dynamic_slice_in_dim(pad_keys, start, span, 0)
        key_seg = lax.dynamic_slice_in_dim(pad_seg, start, span, 0)
        key_pos = lax.dynamic_slice_in_dim(pad_pos, start, span, 0)
        rows = lax.dynamic_slice_in_dim(query, start, width, 0)
        query_seg = lax.dynamic_slice_in_dim(segment, start, width, 0)
        query_pos = lax.dynamic_slice_in_dim(positions, start, width, 0)
        allowed = (key_pos[None, :] <= query_pos[:, None]) & (query_pos[:, None] - key_pos[None, :] < WINDOW) & (key_seg[None, :] == query_seg[:, None])
        heads = rows.reshape(width, HEADS, HD)
        scores = jnp.einsum('rhd,kd->rhk', heads, keys[:, :HD], precision=HIGH) * HD ** (-0.5)
        scores = jnp.where(allowed[:, None, :], low_back(scores), MASKED)
        prob = low(jax.nn.softmax(scores, axis=-1))
        mixed = jnp.einsum('rhk,kd->rhd', prob, keys[:, HD:], precision=HIGH)
        return mixed.reshape(width, HEADS * HD)
    blocks = lax.map(jax.checkpoint(one_block), jnp.arange(TOKENS // width, dtype=jnp.int32))
    return blocks.reshape(TOKENS, HEADS * HD)

def block_forward(resid, frozen, gain_attn, gain_mlp, adapt, mask, segment, positions):
    w_query, w_keyval, w_output, w_gateup, w_down = frozen
    query_a, query_b, keyval_a, keyval_b, output_a, output_b, gateup_a, gateup_b, down_a, down_b = adapt
    act_one = low(rms_scale(resid, gain_attn))
    query = low_back(low(adapted(act_one, w_query, query_a, query_b, mask)))
    keyval = low_back(low(adapted(act_one, w_keyval, keyval_a, keyval_b, mask)))
    attention = low_back(low(attend_all(query, keyval, segment, positions)))
    middle = resid + low_back(adapted(attention, w_output, output_a, output_b, mask))
    act_two = low(rms_scale(middle, gain_mlp))
    gate_up = low_back(adapted(act_two, w_gateup, gateup_a, gateup_b, mask))
    hidden = low(jax.nn.gelu(gate_up[:, :FF]) * gate_up[:, FF:])
    return middle + low_back(adapted(hidden, w_down, down_a, down_b, mask))

def reference(tokens, cotangent, doc_lengths, adapter_ids, w_query, w_keyval, w_output, w_gateup, w_down, gain_attn, gain_mlp, query_a, query_b, keyval_a, keyval_b, output_a, output_b, gateup_a, gateup_b, down_a, down_b):
    positions = jnp.arange(TOKENS, dtype=jnp.int32)
    segment, mask = adapter_mask(doc_lengths, adapter_ids, positions)
    resid = to_natural(tokens.astype(jnp.float32))
    grad_out = to_natural(cotangent.astype(jnp.float32))
    frozen = tuple((weight.astype(jnp.float32) for weight in (w_query, w_keyval, w_output, w_gateup, w_down)))
    adapters = tuple((part.astype(jnp.float32) for part in (query_a, query_b, keyval_a, keyval_b, output_a, output_b, gateup_a, gateup_b, down_a, down_b)))

    def forward(inputs, adapt):
        return block_forward(inputs, frozen, gain_attn, gain_mlp, adapt, mask, segment, positions)
    result, pull = jax.vjp(forward, resid, adapters)
    grad_inputs, grads = pull(grad_out)
    return (to_stored(result).astype(jnp.bfloat16), to_stored(grad_inputs).astype(jnp.bfloat16), grads[0], grads[1], grads[2], grads[3], grads[4], grads[5], grads[6], grads[7], grads[8], grads[9])
```

```python
import functools

import jax
import jax.numpy as jnp
from jax import lax
from jax.experimental import pallas as pl
from jax.experimental.pallas import tpu as pltpu
from jax.sharding import PartitionSpec as P

HEADS = 12
HD = 128
FF = 4608
WINDOW = 1024
RANK = 16
ADAPTERS = 8


NORM_EPS = 1e-06
MASKED = -1e30
MESH = pl.DeviceIdType.MESH

ORD_A = (4, 3, 1, 2, 0)
ORD_A2 = (4, 3, 2, 1, 0)
ORD_B = (4, 1, 2, 3, 0)
ORD_B2 = (4, 2, 1, 3, 0)
ORD_C = (4, 2, 3, 1, 0)
ORD_C2 = (4, 1, 3, 2, 0)
LAGS = (0, 1, 2, 4, 6)


def gather_units():
    units = [
        [(0, 0, 6, ORD_A), (0, 6, 5, ORD_C), (0, 11, 1, ORD_B), (1, 0, 2, ORD_B)],
        [(2, 0, 5, ORD_A), (2, 5, 4, ORD_C), (2, 9, 3, ORD_B)],
    ]
    sets = ((ORD_A, ORD_C, ORD_B), (ORD_A2, ORD_C2, ORD_B2))
    for i in range(3):
        first, second, third = sets[i % 2]
        units.append([(4, 4 * i, 2, first), (4, 4 * i + 2, 1, second), (4, 4 * i + 3, 1, third)])
    for i in range(12):
        first, second, third = sets[i % 2]
        units.append(
            [(3, 3 * i, 3, first), (3, 36 + 3 * i, 2, second), (3, 36 + 3 * i + 2, 1, third)]
        )
    return units


def gather_kernel(parts, events, *refs):
    count = 5
    src, dst = refs[:count], refs[count : 2 * count]
    send_sem, recv_sem, own_sem = refs[2 * count :]
    me = lax.axis_index("ctx")
    bits = [(me // (1 << b)) % 2 for b in range(5)]
    barrier = pltpu.get_barrier_semaphore()
    for b in range(5):
        pl.semaphore_signal(barrier, 1, device_id=flip(me, bits, b), device_id_type=MESH)
    pl.semaphore_wait(barrier, 5)
    own = []
    for w in range(count):
        copy = pltpu.make_async_copy(
            src[w], dst[w].at[bits[4], bits[3], bits[2], bits[1], bits[0]], own_sem.at[w]
        )
        copy.start()
        own.append(copy)

    def exchange(p, k):
        w, tile, tiles, order = parts[p]
        bit, have = order[k], order[:k]
        where = tuple(pl.ds(0, 2) if b in have else bits[b] for b in (4, 3, 2, 1, 0))
        cols = pl.ds(tile * 128, tiles * 128)
        there = dst[w].at[where + (slice(None), cols)]
        return pltpu.make_async_remote_copy(
            there if k else src[w].at[:, cols],
            there,
            send_sem.at[p, k],
            recv_sem.at[p, k],
            device_id=flip(me, bits, bit),
            device_id_type=MESH,
        )

    waited = set()
    for p, k in events:
        if k:
            if parts[p][0] not in waited:
                waited.add(parts[p][0])
                own[parts[p][0]].wait()
            exchange(p, k - 1).wait_recv()
        exchange(p, k).start()
    for p in range(len(parts)):
        exchange(p, 4).wait_recv()
    for p in range(len(parts)):
        for k in range(5):
            exchange(p, k).wait_send()


def gather_weights(weights):
    units = gather_units()
    parts = [part for unit in units for part in unit]
    unit_of = [i for i, unit in enumerate(units) for part in unit]
    events = sorted(
        ((unit_of[p] + LAGS[k], -k, p, k) for p in range(len(parts)) for k in range(5))
    )
    events = [(p, k) for _, _, p, k in events]
    out = pl.pallas_call(
        functools.partial(gather_kernel, parts, events),
        out_shape=[jax.ShapeDtypeStruct((2,) * 5 + w.shape, w.dtype) for w in weights],
        in_specs=[pl.BlockSpec(memory_space=pl.ANY)] * len(weights),
        out_specs=[pl.BlockSpec(memory_space=pl.ANY)] * len(weights),
        scratch_shapes=[
            pltpu.SemaphoreType.DMA((len(parts), 5)),
            pltpu.SemaphoreType.DMA((len(parts), 5)),
            pltpu.SemaphoreType.DMA((len(weights),)),
        ],
        compiler_params=pltpu.CompilerParams(collective_id=0, has_side_effects=True),
    )(*weights)
    return [x.reshape(-1, x.shape[-1]) for x in out]


def flip(me, bits, b):
    return (me+(1-2*bits[b])*(1<<b),)
def reduce_kernel(rows, in_ref, out_ref, r0, r1, r2, r3, r4, ssem, rsem):
    rb=(r0,r1,r2,r3,r4)
    me=lax.axis_index("ctx")
    bits=[(me//(1<<b))%2 for b in range(5)]
    bar=pltpu.get_barrier_semaphore()
    for b in range(5):
        pl.semaphore_signal(bar,1,device_id=flip(me,bits,b),device_id_type=MESH)
    pl.semaphore_wait(bar,5)
    t=rows//16
    a=round(t*3/7); bb=round(t*3/14)
    classes=[(0,a*16,ORD_A),(a*16,bb*16,ORD_B),((a+bb)*16,rows-(a+bb)*16,ORD_C)]
    def rs(cl,s):
        r0_,n,order=classes[cl]
        red=order[::-1]
        bit=red[s]; done=red[:s]
        rem=[b for b in (4,3,2,1,0) if b not in done]
        src=in_ref if s==0 else rb[s-1]
        idx=tuple((1-bits[b]) if b==bit else slice(None) for b in rem)
        return pltpu.make_async_remote_copy(src.at[idx+(pl.ds(r0_,n),)],rb[s].at[(slice(None),)*(4-s)+(pl.ds(r0_,n),)],ssem.at[cl,s],rsem.at[cl,s],device_id=flip(me,bits,bit),device_id_type=MESH)
    def add(cl,s):
        r0_,n,order=classes[cl]
        red=order[::-1]
        bit=red[s]; done=red[:s]
        rem=[b for b in (4,3,2,1,0) if b not in done]
        src=in_ref if s==0 else rb[s-1]
        rs_=pl.ds(r0_,n)
        nd=4-s
        def body(j,_):
            ds=[(j//(1<<(nd-1-i)))%2 for i in range(nd)]
            it=iter(ds)
            si=tuple(bits[b] if b==bit else next(it) for b in rem)
            v=src[si+(rs_,)].astype(jnp.float32)+rb[s][tuple(ds)+(rs_,)].astype(jnp.float32)
            rb[s][tuple(ds)+(rs_,)]=v.astype(jnp.bfloat16)
            return 0
        lax.fori_loop(0,1<<nd,body,0)
    def ag(cl,k):
        r0_,n,order=classes[cl]
        bit=order[k]; have=order[:k]
        idx=tuple(slice(None) if b in have else bits[b] for b in (4,3,2,1,0))+(pl.ds(r0_,n),)
        src=out_ref.at[idx] if k else rb[4].at[pl.ds(r0_,n)]
        return pltpu.make_async_remote_copy(src,out_ref.at[idx],ssem.at[cl,5+k],rsem.at[cl,5+k],device_id=flip(me,bits,bit),device_id_type=MESH)
    for cl in range(3): rs(cl,0).start()
    for s in range(5):
        for cl in range(3):
            rs(cl,s).wait_recv()
            add(cl,s)
            if s<4: rs(cl,s+1).start()
            else:
                ag(cl,0).start()
                r0_,n,_=classes[cl]
                out_ref[bits[4],bits[3],bits[2],bits[1],bits[0],pl.ds(r0_,n)]=rb[4][pl.ds(r0_,n)]
    for k in range(1,5):
        for cl in range(3):
            ag(cl,k-1).wait_recv()
            ag(cl,k).start()
    for cl in range(3): ag(cl,4).wait_recv()
    for cl in range(3):
        for s in range(5):
            rs(cl,s).wait_send(); ag(cl,s).wait_send()
def reduce_packed(x, cid=1):
    import functools
    rows=x.shape[5]
    return pl.pallas_call(functools.partial(reduce_kernel,rows),
        out_shape=jax.ShapeDtypeStruct(x.shape,x.dtype),
        in_specs=[pl.BlockSpec(memory_space=pltpu.VMEM)],out_specs=pl.BlockSpec(memory_space=pltpu.VMEM),
        scratch_shapes=[pltpu.VMEM((2,)*(4-s)+(rows,128),jnp.bfloat16) for s in range(5)]+[pltpu.SemaphoreType.DMA((3,10)),pltpu.SemaphoreType.DMA((3,10))],
        compiler_params=pltpu.CompilerParams(collective_id=cid,has_side_effects=True,vmem_limit_bytes=40<<20))(x)
def pack(grads):
    ps=[g.reshape(g.shape[0]//16,16,g.shape[1]//128,128).transpose(0,2,1,3).reshape(-1,128).astype(jnp.bfloat16) for g in grads]
    n=sum(p.shape[0] for p in ps); tot=-(-n//512)*512
    if tot>n: ps.append(jnp.zeros((tot-n,128),jnp.bfloat16))
    return jnp.concatenate(ps,0).reshape((2,)*5+(tot//32,128))
def unpack(x,shapes):
    x=x.reshape(-1,128); out=[]; o=0
    for r,c in shapes:
        n=r*c//128
        out.append(x[o:o+n].reshape(r//16,c//128,16,128).transpose(0,2,1,3).reshape(r,c).astype(jnp.float32)); o+=n
    return out


def shifted(x, axis, by):
    size = lax.axis_size(axis)
    pairs = [(i, i + by) for i in range(size) if 0 <= i + by < size]
    return lax.ppermute(x, axis, pairs)


def segment_of(doc_lengths, positions):
    starts = jnp.cumsum(doc_lengths) - doc_lengths
    return jnp.sum((starts[None, :] <= positions[:, None]).astype(jnp.int32), axis=1) - 1


def adapter_mask(doc_lengths, adapter_ids, positions):
    segment = segment_of(doc_lengths, positions)
    owner = segment[:, None] == jnp.arange(doc_lengths.shape[0], dtype=jnp.int32)[None, :]
    chosen = jnp.sum(jnp.where(owner, adapter_ids[None, :], 0), axis=1)
    columns = jnp.arange(ADAPTERS * RANK, dtype=jnp.int32) // RANK
    return (segment, (columns[None, :] == chosen[:, None]).astype(jnp.float32))


def rms_scale(values, gain):
    return values * lax.rsqrt(jnp.mean(values * values, axis=-1, keepdims=True) + NORM_EPS) * gain


def by_rows(left, right):
    return lax.dot_general(
        left, right, (((0,), (0,)), ((), ())), preferred_element_type=jnp.float32
    )


def by_cols(left, right):
    return lax.dot_general(
        left, right, (((1,), (1,)), ((), ())), preferred_element_type=jnp.float32
    )


def adapted(inputs, weight, down_part, up_part, mask):
    inner = (jnp.dot(inputs, down_part, preferred_element_type=jnp.float32) * mask).astype(
        jnp.bfloat16
    )
    return (
        jnp.dot(inputs, weight, preferred_element_type=jnp.float32)
        + jnp.dot(inner, up_part, preferred_element_type=jnp.float32),
        inner,
    )


def adapter_back(grad_out, inputs, inner, up_part, mask):
    grad_up = by_rows(inner, grad_out)
    grad_inner = (by_cols(grad_out, up_part) * mask).astype(jnp.bfloat16)
    return (by_rows(inputs, grad_inner), grad_up, grad_inner)


def owner_of(block, count, width):
    device_of = jnp.where(block < count, block, 2 * count - 1 - block)
    return (device_of, jnp.where(block < count, 0, width))


def key_block(table, first_device, block, count, width):
    device_of, row_in = owner_of(block, count, width)
    piece = lax.dynamic_slice(
        table, (device_of - first_device, row_in, jnp.int32(0)), (1, width, table.shape[2])
    )
    return piece[0]


def block_scores(query, keys, allowed):
    rows = query.shape[0]
    heads = query.reshape(rows, HEADS, HD)
    raw = jnp.einsum(
        "rhd,kd->rhk", heads, keys[:, :HD], preferred_element_type=jnp.float32
    ) * HD ** (-0.5)
    return jnp.where(allowed[:, None, :], raw, MASKED)


def attend_forward(query, keys, allowed):
    scores = block_scores(query, keys, allowed)
    top = jnp.max(scores, axis=-1, keepdims=True)
    total = jnp.sum(jnp.exp(scores - top), axis=-1, keepdims=True)
    log_total = top + jnp.log(total)
    weights = jnp.exp(scores - log_total).astype(jnp.bfloat16)
    mixed = jnp.einsum("rhk,kd->rhd", weights, keys[:, HD:], preferred_element_type=jnp.float32)
    return (mixed.reshape(query.shape[0], -1), log_total)


def attend_backward(query, keys, allowed, log_total, grad_out):
    rows = query.shape[0]
    prob = jnp.exp(block_scores(query, keys, allowed) - log_total)
    grad_heads = grad_out.reshape(rows, HEADS, HD)
    grad_prob = jnp.einsum(
        "rhd,kd->rhk", grad_heads, keys[:, HD:], preferred_element_type=jnp.float32
    )
    delta = jnp.sum(prob * grad_prob, axis=-1, keepdims=True)
    grad_scores = (prob * (grad_prob - delta)).astype(jnp.bfloat16)
    scale = HD ** (-0.5)
    grad_query = (
        jnp.einsum("rhk,kd->rhd", grad_scores, keys[:, :HD], preferred_element_type=jnp.float32)
        * scale
    )
    grad_key = (
        jnp.einsum(
            "rhk,rhd->kd",
            grad_scores,
            query.reshape(rows, HEADS, HD),
            preferred_element_type=jnp.float32,
        )
        * scale
    )
    grad_value = jnp.einsum(
        "rhk,rhd->kd", prob.astype(jnp.bfloat16), grad_heads, preferred_element_type=jnp.float32
    )
    return (grad_query.reshape(rows, -1), jnp.concatenate([grad_key, grad_value], axis=1))


def local(
    tokens,
    cotangent,
    doc_lengths,
    adapter_ids,
    w_query,
    w_keyval,
    w_output,
    w_gateup,
    w_down,
    gain_attn,
    gain_mlp,
    query_a,
    query_b,
    keyval_a,
    keyval_b,
    output_a,
    output_b,
    gateup_a,
    gateup_b,
    down_a,
    down_b,
):
    count = lax.axis_size("ctx")
    device = lax.axis_index("ctx")
    local_rows = tokens.shape[0]
    width = local_rows // 2
    reach = (WINDOW + width - 1) // width
    key_width = w_keyval.shape[1]
    half_rows = jnp.arange(width, dtype=jnp.int32)
    own_blocks = (device, 2 * count - 1 - device)
    positions = jnp.concatenate(
        [own_blocks[0] * width + half_rows, own_blocks[1] * width + half_rows]
    )
    segment, mask = adapter_mask(doc_lengths, adapter_ids, positions)
    resid = tokens.astype(jnp.float32)
    act_one = rms_scale(resid, gain_attn).astype(jnp.bfloat16)
    own = count == 32 and w_query.shape[0] % 16 == 0
    weights = (w_query, w_keyval, w_output, w_gateup, w_down)
    if own:
        full = gather_weights(weights)
    else:
        full = [lax.all_gather(w, "ctx", axis=0, tiled=True) for w in weights]
    full_query, full_keyval, full_output, full_gateup, full_down = full
    query_full, inner_query = adapted(act_one, full_query, query_a, query_b, mask)
    keyval_full, inner_keyval = adapted(act_one, full_keyval, keyval_a, keyval_b, mask)
    query = query_full.astype(jnp.bfloat16)
    keyval = keyval_full.astype(jnp.bfloat16)
    stacked = [keyval]
    for offset in range(1, reach + 1):
        later = shifted(keyval, "ctx", -offset)
        prior = shifted(keyval, "ctx", offset)
        stacked = [prior] + stacked + [later]
    table = jnp.stack(stacked)
    first_device = device - reach
    kept = []
    mixed_parts = []
    for which in range(2):
        block = own_blocks[which]
        key_blocks = [block - reach + step for step in range(reach + 1)]
        keys = jnp.concatenate(
            [key_block(table, first_device, entry, count, width) for entry in key_blocks], axis=0
        )
        key_pos = jnp.concatenate([entry * width + half_rows for entry in key_blocks])
        key_seg = segment_of(doc_lengths, key_pos)
        query_pos = positions[which * width : (which + 1) * width]
        query_seg = segment[which * width : (which + 1) * width]
        allowed = (
            (key_pos[None, :] <= query_pos[:, None])
            & (query_pos[:, None] - key_pos[None, :] < WINDOW)
            & (key_seg[None, :] == query_seg[:, None])
        )
        mixed, log_total = attend_forward(query[which * width : (which + 1) * width], keys, allowed)
        kept.append((key_blocks, keys, allowed, log_total))
        mixed_parts.append(mixed)
    attention = jnp.concatenate(mixed_parts, axis=0).astype(jnp.bfloat16)
    branch_one, inner_output = adapted(attention, full_output, output_a, output_b, mask)
    middle = resid + branch_one
    act_two = rms_scale(middle, gain_mlp).astype(jnp.bfloat16)
    gate_up, inner_gateup = adapted(act_two, full_gateup, gateup_a, gateup_b, mask)
    gate = gate_up[:, :FF]
    upper = gate_up[:, FF:]
    hidden = (jax.nn.gelu(gate) * upper).astype(jnp.bfloat16)
    down_main = jnp.dot(
        hidden,
        full_down,
        preferred_element_type=jnp.float32,
    )
    inner_down = (jnp.dot(hidden, down_a, preferred_element_type=jnp.float32) * mask).astype(
        jnp.bfloat16
    )
    result = middle + (down_main + jnp.dot(inner_down, down_b, preferred_element_type=jnp.float32))
    grad_down_a, grad_down_b, d_inner_down = adapter_back(
        cotangent, hidden, inner_down, down_b, mask
    )
    grad_hidden = by_cols(cotangent, full_down) + by_cols(
        d_inner_down, down_a
    )

    def gated(gate_part, up_part):
        return jax.nn.gelu(gate_part) * up_part

    unused, pull_glu = jax.vjp(gated, gate, upper)
    grad_gate, grad_up = pull_glu(grad_hidden)
    grad_gateup = jnp.concatenate([grad_gate, grad_up], axis=1).astype(jnp.bfloat16)
    grad_gateup_a, grad_gateup_b, d_inner_gateup = adapter_back(
        grad_gateup, act_two, inner_gateup, gateup_b, mask
    )
    grad_act_two = by_cols(grad_gateup, full_gateup) + by_cols(d_inner_gateup, gateup_a)
    unused, pull_two = jax.vjp(lambda values: rms_scale(values, gain_mlp), middle)
    grad_middle = cotangent.astype(jnp.float32) + pull_two(grad_act_two)[0]
    grad_branch = grad_middle.astype(jnp.bfloat16)
    grad_output_a, grad_output_b, d_inner_output = adapter_back(
        grad_branch, attention, inner_output, output_b, mask
    )
    grad_attention = (by_cols(grad_branch, full_output) + by_cols(d_inner_output, output_a)).astype(
        jnp.bfloat16
    )
    query_grads = []
    key_grads = []
    for which in range(2):
        key_blocks, keys, allowed, log_total = kept[which]
        rows_query = query[which * width : (which + 1) * width]
        rows_grad = grad_attention[which * width : (which + 1) * width]
        grad_rows, grad_keys = attend_backward(rows_query, keys, allowed, log_total, rows_grad)
        query_grads.append(grad_rows)
        for step, entry in enumerate(key_blocks):
            key_grads.append((entry, grad_keys[step * width : (step + 1) * width]))
    grad_query = jnp.concatenate(query_grads, axis=0).astype(jnp.bfloat16)
    slots = jnp.zeros((2 * reach + 1, local_rows, key_width), jnp.float32)
    for entry, piece in key_grads:
        device_of, row_in = owner_of(entry, count, width)
        slot = device_of - first_device
        current = lax.dynamic_slice(slots, (slot, row_in, jnp.int32(0)), (1, width, key_width))
        slots = lax.dynamic_update_slice(slots, current + piece[None], (slot, row_in, jnp.int32(0)))
    grad_keyval_full = slots[reach]
    for offset in range(1, reach + 1):
        from_lower = shifted(slots[reach + offset].astype(jnp.bfloat16), "ctx", offset).astype(
            jnp.float32
        )
        from_upper = shifted(slots[reach - offset].astype(jnp.bfloat16), "ctx", -offset).astype(
            jnp.float32
        )
        grad_keyval_full = grad_keyval_full + from_lower + from_upper
    grad_keyval = grad_keyval_full.astype(jnp.bfloat16)
    grad_query_a, grad_query_b, d_inner_query = adapter_back(
        grad_query, act_one, inner_query, query_b, mask
    )
    grad_keyval_a, grad_keyval_b, d_inner_keyval = adapter_back(
        grad_keyval, act_one, inner_keyval, keyval_b, mask
    )
    grad_act_one = (
        by_cols(grad_query, full_query)
        + by_cols(grad_keyval, full_keyval)
        + by_cols(d_inner_query, query_a)
        + by_cols(d_inner_keyval, keyval_a)
    )
    unused, pull_one = jax.vjp(lambda values: rms_scale(values, gain_attn), resid)
    grad_tokens = (grad_middle + pull_one(grad_act_one)[0]).astype(jnp.bfloat16)
    partial = (
                        grad_query_a,
            grad_query_b,
            grad_keyval_a,
            grad_keyval_b,
            grad_output_a,
            grad_output_b,
            grad_gateup_a,
            grad_gateup_b,
            grad_down_a,
            grad_down_b,
    )
    if own:
        sums = unpack(reduce_packed(pack(partial)), [g.shape for g in partial])
    else:
        sums = lax.psum(partial, "ctx")
    return (
        result.astype(jnp.bfloat16),
        grad_tokens,
        sums[0],
        sums[1],
        sums[2],
        sums[3],
        sums[4],
        sums[5],
        sums[6],
        sums[7],
        sums[8],
        sums[9],
    )


def solution(mesh):
    in_specs = (
        P("ctx", None),
        P("ctx", None),
        P(),
        P(),
        P("ctx", None),
        P("ctx", None),
        P("ctx", None),
        P("ctx", None),
        P("ctx", None),
        P(),
        P(),
        P(),
        P(),
        P(),
        P(),
        P(),
        P(),
        P(),
        P(),
        P(),
        P(),
    )
    out_specs = (P("ctx", None), P("ctx", None), P(), P(), P(), P(), P(), P(), P(), P(), P(), P())
    return jax.shard_map(local, mesh=mesh, in_specs=in_specs, out_specs=out_specs, check_vma=False)
```

```python
import functools

import jax
import jax.numpy as jnp
from jax import lax
from jax.experimental import pallas as pl
from jax.experimental.pallas import tpu as pltpu
from jax.sharding import PartitionSpec as P

HEADS = 12
HD = 128
FF = 4608
WINDOW = 1024
RANK = 16
ADAPTERS = 8


NORM_EPS = 1e-06
MASKED = -1e30


MESH = pl.DeviceIdType.MESH
bf16 = jnp.bfloat16
f32 = jnp.float32
NN = (((1,), (0,)), ((), ()))
NT = (((1,), (1,)), ((), ()))
TN = (((0,), (0,)), ((), ()))
VMEM = pl.BlockSpec(memory_space=pltpu.VMEM)
HBM = pl.BlockSpec(memory_space=pl.ANY)
ORD_A = (4, 3, 1, 2, 0)
ORD_A2 = (4, 3, 2, 1, 0)
ORD_B = (4, 1, 2, 3, 0)
ORD_B2 = (4, 2, 1, 3, 0)
ORD_C = (4, 2, 3, 1, 0)
ORD_C2 = (4, 1, 3, 2, 0)
LAGS = (0, 1, 2, 4, 6)


def shifted(x, axis, by):
    size = lax.axis_size(axis)
    pairs = [(i, i + by) for i in range(size) if 0 <= i + by < size]
    return lax.ppermute(x, axis, pairs)


def segment_of(doc_lengths, positions):
    starts = jnp.cumsum(doc_lengths) - doc_lengths
    return jnp.sum((starts[None, :] <= positions[:, None]).astype(jnp.int32), axis=1) - 1


def adapter_mask(doc_lengths, adapter_ids, positions):
    segment = segment_of(doc_lengths, positions)
    owner = segment[:, None] == jnp.arange(doc_lengths.shape[0], dtype=jnp.int32)[None, :]
    chosen = jnp.sum(jnp.where(owner, adapter_ids[None, :], 0), axis=1)
    columns = jnp.arange(ADAPTERS * RANK, dtype=jnp.int32) // RANK
    return (segment, (columns[None, :] == chosen[:, None]).astype(jnp.float32))


def rms_scale(values, gain):
    return values * lax.rsqrt(jnp.mean(values * values, axis=-1, keepdims=True) + NORM_EPS) * gain


def by_rows(left, right):
    return lax.dot_general(
        left, right, (((0,), (0,)), ((), ())), preferred_element_type=jnp.float32
    )


def by_cols(left, right):
    return lax.dot_general(
        left, right, (((1,), (1,)), ((), ())), preferred_element_type=jnp.float32
    )


def adapted(inputs, weight, down_part, up_part, mask):
    inner = (jnp.dot(inputs, down_part, preferred_element_type=jnp.float32) * mask).astype(
        jnp.bfloat16
    )
    return (
        jnp.dot(inputs, weight, preferred_element_type=jnp.float32)
        + jnp.dot(inner, up_part, preferred_element_type=jnp.float32),
        inner,
    )


def adapter_back(grad_out, inputs, inner, up_part, mask):
    grad_up = by_rows(inner, grad_out)
    grad_inner = (by_cols(grad_out, up_part) * mask).astype(jnp.bfloat16)
    return (by_rows(inputs, grad_inner), grad_up, grad_inner)


def owner_of(block, count, width):
    device_of = jnp.where(block < count, block, 2 * count - 1 - block)
    return (device_of, jnp.where(block < count, 0, width))


def key_block(table, first_device, block, count, width):
    device_of, row_in = owner_of(block, count, width)
    piece = lax.dynamic_slice(
        table, (device_of - first_device, row_in, jnp.int32(0)), (1, width, table.shape[2])
    )
    return piece[0]


def block_scores(query, keys, allowed):
    rows = query.shape[0]
    heads = query.reshape(rows, HEADS, HD)
    raw = jnp.einsum(
        "rhd,kd->rhk", heads, keys[:, :HD], preferred_element_type=jnp.float32
    ) * HD ** (-0.5)
    return jnp.where(allowed[:, None, :], raw, MASKED)


def attend_forward(query, keys, allowed):
    scores = block_scores(query, keys, allowed)
    top = jnp.max(scores, axis=-1, keepdims=True)
    total = jnp.sum(jnp.exp(scores - top), axis=-1, keepdims=True)
    log_total = top + jnp.log(total)
    weights = jnp.exp(scores - log_total).astype(jnp.bfloat16)
    mixed = jnp.einsum("rhk,kd->rhd", weights, keys[:, HD:], preferred_element_type=jnp.float32)
    return (mixed.reshape(query.shape[0], -1), log_total)


def attend_backward(query, keys, allowed, log_total, grad_out):
    rows = query.shape[0]
    prob = jnp.exp(block_scores(query, keys, allowed) - log_total)
    grad_heads = grad_out.reshape(rows, HEADS, HD)
    grad_prob = jnp.einsum(
        "rhd,kd->rhk", grad_heads, keys[:, HD:], preferred_element_type=jnp.float32
    )
    delta = jnp.sum(prob * grad_prob, axis=-1, keepdims=True)
    grad_scores = (prob * (grad_prob - delta)).astype(jnp.bfloat16)
    scale = HD ** (-0.5)
    grad_query = (
        jnp.einsum("rhk,kd->rhd", grad_scores, keys[:, :HD], preferred_element_type=jnp.float32)
        * scale
    )
    grad_key = (
        jnp.einsum(
            "rhk,rhd->kd",
            grad_scores,
            query.reshape(rows, HEADS, HD),
            preferred_element_type=jnp.float32,
        )
        * scale
    )
    grad_value = jnp.einsum(
        "rhk,rhd->kd", prob.astype(jnp.bfloat16), grad_heads, preferred_element_type=jnp.float32
    )
    return (grad_query.reshape(rows, -1), jnp.concatenate([grad_key, grad_value], axis=1))


def local_native(
    tokens,
    cotangent,
    doc_lengths,
    adapter_ids,
    w_query,
    w_keyval,
    w_output,
    w_gateup,
    w_down,
    gain_attn,
    gain_mlp,
    query_a,
    query_b,
    keyval_a,
    keyval_b,
    output_a,
    output_b,
    gateup_a,
    gateup_b,
    down_a,
    down_b,
):
    count = lax.axis_size("ctx")
    device = lax.axis_index("ctx")
    local_rows = tokens.shape[0]
    width = local_rows // 2
    reach = (WINDOW + width - 1) // width
    key_width = w_keyval.shape[1]
    half_rows = jnp.arange(width, dtype=jnp.int32)
    own_blocks = (device, 2 * count - 1 - device)
    positions = jnp.concatenate(
        [own_blocks[0] * width + half_rows, own_blocks[1] * width + half_rows]
    )
    segment, mask = adapter_mask(doc_lengths, adapter_ids, positions)
    resid = tokens.astype(jnp.float32)
    act_one = rms_scale(resid, gain_attn).astype(jnp.bfloat16)
    full_query, full_keyval, full_output, full_gateup = (
        lax.all_gather(w_query, "ctx", axis=0, tiled=True),
        lax.all_gather(w_keyval, "ctx", axis=0, tiled=True),
        lax.all_gather(w_output, "ctx", axis=0, tiled=True),
        lax.all_gather(w_gateup, "ctx", axis=0, tiled=True),
    )
    query_full, inner_query = adapted(act_one, full_query, query_a, query_b, mask)
    keyval_full, inner_keyval = adapted(act_one, full_keyval, keyval_a, keyval_b, mask)
    query = query_full.astype(jnp.bfloat16)
    keyval = keyval_full.astype(jnp.bfloat16)
    stacked = [keyval]
    for offset in range(1, reach + 1):
        later = shifted(keyval, "ctx", -offset)
        prior = shifted(keyval, "ctx", offset)
        stacked = [prior] + stacked + [later]
    table = jnp.stack(stacked)
    first_device = device - reach
    kept = []
    mixed_parts = []
    for which in range(2):
        block = own_blocks[which]
        key_blocks = [block - reach + step for step in range(reach + 1)]
        keys = jnp.concatenate(
            [key_block(table, first_device, entry, count, width) for entry in key_blocks], axis=0
        )
        key_pos = jnp.concatenate([entry * width + half_rows for entry in key_blocks])
        key_seg = segment_of(doc_lengths, key_pos)
        query_pos = positions[which * width : (which + 1) * width]
        query_seg = segment[which * width : (which + 1) * width]
        allowed = (
            (key_pos[None, :] <= query_pos[:, None])
            & (query_pos[:, None] - key_pos[None, :] < WINDOW)
            & (key_seg[None, :] == query_seg[:, None])
        )
        mixed, log_total = attend_forward(query[which * width : (which + 1) * width], keys, allowed)
        kept.append((key_blocks, keys, allowed, log_total))
        mixed_parts.append(mixed)
    attention = jnp.concatenate(mixed_parts, axis=0).astype(jnp.bfloat16)
    branch_one, inner_output = adapted(attention, full_output, output_a, output_b, mask)
    middle = resid + branch_one
    act_two = rms_scale(middle, gain_mlp).astype(jnp.bfloat16)
    gate_up, inner_gateup = adapted(act_two, full_gateup, gateup_a, gateup_b, mask)
    gate = gate_up[:, :FF]
    upper = gate_up[:, FF:]
    hidden = (jax.nn.gelu(gate) * upper).astype(jnp.bfloat16)
    down_main = jnp.dot(
        hidden,
        lax.all_gather(w_down, "ctx", axis=0, tiled=True),
        preferred_element_type=jnp.float32,
    )
    inner_down = (jnp.dot(hidden, down_a, preferred_element_type=jnp.float32) * mask).astype(
        jnp.bfloat16
    )
    result = middle + (down_main + jnp.dot(inner_down, down_b, preferred_element_type=jnp.float32))
    grad_down_a, grad_down_b, d_inner_down = adapter_back(
        cotangent, hidden, inner_down, down_b, mask
    )
    grad_hidden = by_cols(cotangent, lax.all_gather(w_down, "ctx", axis=0, tiled=True)) + by_cols(
        d_inner_down, down_a
    )

    def gated(gate_part, up_part):
        return jax.nn.gelu(gate_part) * up_part

    unused, pull_glu = jax.vjp(gated, gate, upper)
    grad_gate, grad_up = pull_glu(grad_hidden)
    grad_gateup = jnp.concatenate([grad_gate, grad_up], axis=1).astype(jnp.bfloat16)
    grad_gateup_a, grad_gateup_b, d_inner_gateup = adapter_back(
        grad_gateup, act_two, inner_gateup, gateup_b, mask
    )
    grad_act_two = by_cols(grad_gateup, full_gateup) + by_cols(d_inner_gateup, gateup_a)
    unused, pull_two = jax.vjp(lambda values: rms_scale(values, gain_mlp), middle)
    grad_middle = cotangent.astype(jnp.float32) + pull_two(grad_act_two)[0]
    grad_branch = grad_middle.astype(jnp.bfloat16)
    grad_output_a, grad_output_b, d_inner_output = adapter_back(
        grad_branch, attention, inner_output, output_b, mask
    )
    grad_attention = (by_cols(grad_branch, full_output) + by_cols(d_inner_output, output_a)).astype(
        jnp.bfloat16
    )
    query_grads = []
    key_grads = []
    for which in range(2):
        key_blocks, keys, allowed, log_total = kept[which]
        rows_query = query[which * width : (which + 1) * width]
        rows_grad = grad_attention[which * width : (which + 1) * width]
        grad_rows, grad_keys = attend_backward(rows_query, keys, allowed, log_total, rows_grad)
        query_grads.append(grad_rows)
        for step, entry in enumerate(key_blocks):
            key_grads.append((entry, grad_keys[step * width : (step + 1) * width]))
    grad_query = jnp.concatenate(query_grads, axis=0).astype(jnp.bfloat16)
    slots = jnp.zeros((2 * reach + 1, local_rows, key_width), jnp.float32)
    for entry, piece in key_grads:
        device_of, row_in = owner_of(entry, count, width)
        slot = device_of - first_device
        current = lax.dynamic_slice(slots, (slot, row_in, jnp.int32(0)), (1, width, key_width))
        slots = lax.dynamic_update_slice(slots, current + piece[None], (slot, row_in, jnp.int32(0)))
    grad_keyval_full = slots[reach]
    for offset in range(1, reach + 1):
        from_lower = shifted(slots[reach + offset].astype(jnp.bfloat16), "ctx", offset).astype(
            jnp.float32
        )
        from_upper = shifted(slots[reach - offset].astype(jnp.bfloat16), "ctx", -offset).astype(
            jnp.float32
        )
        grad_keyval_full = grad_keyval_full + from_lower + from_upper
    grad_keyval = grad_keyval_full.astype(jnp.bfloat16)
    grad_query_a, grad_query_b, d_inner_query = adapter_back(
        grad_query, act_one, inner_query, query_b, mask
    )
    grad_keyval_a, grad_keyval_b, d_inner_keyval = adapter_back(
        grad_keyval, act_one, inner_keyval, keyval_b, mask
    )
    grad_act_one = (
        by_cols(grad_query, full_query)
        + by_cols(grad_keyval, full_keyval)
        + by_cols(d_inner_query, query_a)
        + by_cols(d_inner_keyval, keyval_a)
    )
    unused, pull_one = jax.vjp(lambda values: rms_scale(values, gain_attn), resid)
    grad_tokens = (grad_middle + pull_one(grad_act_one)[0]).astype(jnp.bfloat16)
    sums = lax.psum(
        (
            grad_query_a,
            grad_query_b,
            grad_keyval_a,
            grad_keyval_b,
            grad_output_a,
            grad_output_b,
            grad_gateup_a,
            grad_gateup_b,
            grad_down_a,
            grad_down_b,
        ),
        "ctx",
    )
    return (
        result.astype(jnp.bfloat16),
        grad_tokens,
        sums[0],
        sums[1],
        sums[2],
        sums[3],
        sums[4],
        sums[5],
        sums[6],
        sums[7],
        sums[8],
        sums[9],
    )


def flip(me, bits, b):
    return (me+(1-2*bits[b])*(1<<b),)
def reduce_kernel(rows, in_ref, out_ref, r0, r1, r2, r3, r4, ssem, rsem):
    rb=(r0,r1,r2,r3,r4)
    me=lax.axis_index("ctx")
    bits=[(me//(1<<b))%2 for b in range(5)]
    bar=pltpu.get_barrier_semaphore()
    for b in range(5):
        pl.semaphore_signal(bar,1,device_id=flip(me,bits,b),device_id_type=MESH)
    pl.semaphore_wait(bar,5)
    t=rows//16
    a=round(t*3/7); bb=round(t*3/14)
    classes=[(0,a*16,ORD_A),(a*16,bb*16,ORD_B),((a+bb)*16,rows-(a+bb)*16,ORD_C)]
    def rs(cl,s):
        r0_,n,order=classes[cl]
        red=order[::-1]
        bit=red[s]; done=red[:s]
        rem=[b for b in (4,3,2,1,0) if b not in done]
        src=in_ref if s==0 else rb[s-1]
        idx=tuple((1-bits[b]) if b==bit else slice(None) for b in rem)
        return pltpu.make_async_remote_copy(src.at[idx+(pl.ds(r0_,n),)],rb[s].at[(slice(None),)*(4-s)+(pl.ds(r0_,n),)],ssem.at[cl,s],rsem.at[cl,s],device_id=flip(me,bits,bit),device_id_type=MESH)
    def add(cl,s):
        r0_,n,order=classes[cl]
        red=order[::-1]
        bit=red[s]; done=red[:s]
        rem=[b for b in (4,3,2,1,0) if b not in done]
        src=in_ref if s==0 else rb[s-1]
        rs_=pl.ds(r0_,n)
        nd=4-s
        def body(j,_):
            ds=[(j//(1<<(nd-1-i)))%2 for i in range(nd)]
            it=iter(ds)
            si=tuple(bits[b] if b==bit else next(it) for b in rem)
            v=src[si+(rs_,)].astype(f32)+rb[s][tuple(ds)+(rs_,)].astype(f32)
            rb[s][tuple(ds)+(rs_,)]=v.astype(bf16)
            return 0
        lax.fori_loop(0,1<<nd,body,0)
    def ag(cl,k):
        r0_,n,order=classes[cl]
        bit=order[k]; have=order[:k]
        idx=tuple(slice(None) if b in have else bits[b] for b in (4,3,2,1,0))+(pl.ds(r0_,n),)
        src=out_ref.at[idx] if k else rb[4].at[pl.ds(r0_,n)]
        return pltpu.make_async_remote_copy(src,out_ref.at[idx],ssem.at[cl,5+k],rsem.at[cl,5+k],device_id=flip(me,bits,bit),device_id_type=MESH)
    for cl in range(3): rs(cl,0).start()
    for s in range(5):
        for cl in range(3):
            rs(cl,s).wait_recv()
            add(cl,s)
            if s<4: rs(cl,s+1).start()
            else:
                ag(cl,0).start()
                r0_,n,_=classes[cl]
                out_ref[bits[4],bits[3],bits[2],bits[1],bits[0],pl.ds(r0_,n)]=rb[4][pl.ds(r0_,n)]
    for k in range(1,5):
        for cl in range(3):
            ag(cl,k-1).wait_recv()
            ag(cl,k).start()
    for cl in range(3): ag(cl,4).wait_recv()
    for cl in range(3):
        for s in range(5):
            rs(cl,s).wait_send(); ag(cl,s).wait_send()
def reduce_packed(x, cid=1):
    rows=x.shape[5]
    return pl.pallas_call(functools.partial(reduce_kernel,rows),
        out_shape=jax.ShapeDtypeStruct(x.shape,x.dtype),
        in_specs=[pl.BlockSpec(memory_space=pltpu.VMEM)],out_specs=pl.BlockSpec(memory_space=pltpu.VMEM),
        scratch_shapes=[pltpu.VMEM((2,)*(4-s)+(rows,128),bf16) for s in range(5)]+[pltpu.SemaphoreType.DMA((3,10)),pltpu.SemaphoreType.DMA((3,10))],
        compiler_params=pltpu.CompilerParams(collective_id=cid,has_side_effects=True,vmem_limit_bytes=40<<20))(x)

def gather_units():
    units = [
        [(0, 0, 6, ORD_A), (0, 6, 5, ORD_C), (0, 11, 1, ORD_B), (1, 0, 2, ORD_B)],
        [(2, 0, 5, ORD_A), (2, 5, 4, ORD_C), (2, 9, 3, ORD_B)],
    ]
    sets = ((ORD_A, ORD_C, ORD_B), (ORD_A2, ORD_C2, ORD_B2))
    for i in range(3):
        first, second, third = sets[i % 2]
        units.append([(3, 4 * i, 2, first), (3, 4 * i + 2, 1, second), (3, 4 * i + 3, 1, third)])
    return units


def gather_kernel(parts, events, *refs):
    count = (len(refs) - 3) // 3
    src, dst, held = refs[:count], refs[count : 2 * count], refs[2 * count : 3 * count]
    send_sem, recv_sem, own_sem = refs[3 * count :]
    me = lax.axis_index("ctx")
    bits = [(me // (1 << b)) % 2 for b in range(5)]
    barrier = pltpu.get_barrier_semaphore()
    for b in range(5):
        pl.semaphore_signal(barrier, 1, device_id=flip(me, bits, b), device_id_type=MESH)
    pl.semaphore_wait(barrier, 5)
    own = []
    for w in range(count):
        copy = pltpu.make_async_copy(src[w], held[w], own_sem.at[w])
        copy.start()
        own.append(copy)
    for w in range(count):
        own[w].wait()
        own[w] = copy = pltpu.make_async_copy(
            held[w], dst[w].at[bits[4], bits[3], bits[2], bits[1], bits[0]], own_sem.at[w]
        )
        copy.start()

    def exchange(p, k):
        w, tile, tiles, order = parts[p]
        bit, have = order[k], order[:k]
        where = tuple(pl.ds(0, 2) if b in have else bits[b] for b in (4, 3, 2, 1, 0))
        cols = pl.ds(tile * 128, tiles * 128)
        there = dst[w].at[where + (slice(None), cols)]
        return pltpu.make_async_remote_copy(
            there if k else src[w].at[:, cols],
            there,
            send_sem.at[p, k],
            recv_sem.at[p, k],
            device_id=flip(me, bits, bit),
            device_id_type=MESH,
        )

    waited = set()
    for p, k in events:
        if k:
            if parts[p][0] not in waited:
                waited.add(parts[p][0])
                own[parts[p][0]].wait()
            exchange(p, k - 1).wait_recv()
        exchange(p, k).start()
    for p in range(len(parts)):
        exchange(p, 4).wait_recv()
    for p in range(len(parts)):
        for k in range(5):
            exchange(p, k).wait_send()


def gather_weights(weights):
    units = gather_units()
    parts = [part for unit in units for part in unit]
    unit_of = [i for i, unit in enumerate(units) for part in unit]
    events = sorted(
        ((unit_of[p] + LAGS[k], -k, p, k) for p in range(len(parts)) for k in range(5))
    )
    events = [(p, k) for _, _, p, k in events]
    out = pl.pallas_call(
        functools.partial(gather_kernel, parts, events),
        out_shape=[jax.ShapeDtypeStruct((2,) * 5 + w.shape, w.dtype) for w in weights],
        in_specs=[pl.BlockSpec(memory_space=pl.ANY)] * len(weights),
        out_specs=[pl.BlockSpec(memory_space=pl.ANY)] * len(weights),
        scratch_shapes=[pltpu.VMEM(w.shape, w.dtype) for w in weights]
        + [
            pltpu.SemaphoreType.DMA((len(parts), 5)),
            pltpu.SemaphoreType.DMA((len(parts), 5)),
            pltpu.SemaphoreType.DMA((len(weights),)),
        ],
        compiler_params=pltpu.CompilerParams(collective_id=0, has_side_effects=True),
    )(*weights)
    return [x.reshape(-1, x.shape[-1]) for x in out]


SUB = 128
GROUP = 6
SCALE = HD ** (-0.5)


def heads_down(x):
    return jnp.concatenate([x[:,i*HD:(i+1)*HD] for i in range(x.shape[1]//HD)],axis=0)
def heads_across(x):
    n=x.shape[0]//SUB
    return jnp.concatenate([x[i*SUB:(i+1)*SUB] for i in range(n)],axis=1)
def att_fwd_kernel(span, window, q_ref, kv_ref, qseg_ref, kseg_ref, o_ref, p_ref):
    s=pl.program_id(1)
    start=pl.multiple_of(s*SUB,SUB)
    k=kv_ref[0,pl.ds(start,span),:HD]; v=kv_ref[0,pl.ds(start,span),HD:]
    row=lax.broadcasted_iota(jnp.int32,(SUB,span),0); col=lax.broadcasted_iota(jnp.int32,(SUB,span),1)
    ok=(col<=row+(span-SUB))&(col>row+(span-SUB-window))&(kseg_ref[0,:,pl.ds(start,span)]==qseg_ref[...])
    bias=jnp.where(ok,0.0,MASKED)
    bias=jnp.concatenate([bias]*GROUP,axis=0)
    def body(g,_):
        at=pl.multiple_of(g*GROUP*HD,GROUP*HD)
        q=heads_down(q_ref[:,pl.ds(at,GROUP*HD)])
        sc=lax.dot_general(q,k,NT,preferred_element_type=f32)*SCALE+bias
        e=jnp.exp(sc-jnp.max(sc,axis=1,keepdims=True))
        p=(e*(1.0/jnp.sum(e,axis=1,keepdims=True))).astype(bf16)
        p_ref[0,0,pl.ds(pl.multiple_of(g*GROUP*SUB,GROUP*SUB),GROUP*SUB),:]=p
        o=lax.dot_general(p,v,(((1,),(0,)),((),())),preferred_element_type=f32)
        o_ref[:,pl.ds(at,GROUP*HD)]=heads_across(o).astype(bf16)
        return 0
    lax.fori_loop(0,HEADS//GROUP,body,0)
def att_fwd(q,kv,qseg,kseg,window):
    rows=q.shape[0]; width=rows//2; subs=width//SUB; keys=kv.shape[1]; span=keys-width+SUB
    return pl.pallas_call(functools.partial(att_fwd_kernel,span,window),grid=(2,subs),
      in_specs=[pl.BlockSpec((SUB,q.shape[1]),lambda w,s:(w*subs+s,0)),pl.BlockSpec((1,keys,2*HD),lambda w,s:(w,0,0)),
        pl.BlockSpec((SUB,1),lambda w,s:(w*subs+s,0)),pl.BlockSpec((1,1,keys),lambda w,s:(w,0,0))],
      out_specs=[pl.BlockSpec((SUB,q.shape[1]),lambda w,s:(w*subs+s,0)),pl.BlockSpec((1,1,HEADS*SUB,span),lambda w,s:(w,s,0,0))],
      out_shape=[jax.ShapeDtypeStruct(q.shape,bf16),jax.ShapeDtypeStruct((2,subs,HEADS*SUB,span),bf16)],
      compiler_params=pltpu.CompilerParams(vmem_limit_bytes=56<<20),name="att_fwd")(q,kv,qseg,kseg)
def att_bwd_kernel(span, q_ref, kv_ref, att_ref, do_ref, p_ref, dq_ref, dkv_ref):
    s=pl.program_id(1)
    start=pl.multiple_of(s*SUB,SUB)
    k=kv_ref[0,pl.ds(start,span),:HD]; v=kv_ref[0,pl.ds(start,span),HD:]
    @pl.when(s==0)
    def _(): dkv_ref[...]=jnp.zeros_like(dkv_ref)
    def body(g,_):
        at=pl.multiple_of(g*GROUP*HD,GROUP*HD)
        q=heads_down(q_ref[:,pl.ds(at,GROUP*HD)])
        do=heads_down(do_ref[:,pl.ds(at,GROUP*HD)])
        o=heads_down(att_ref[:,pl.ds(at,GROUP*HD)])
        delta=jnp.sum(do.astype(f32)*o.astype(f32),axis=1,keepdims=True)
        dp=lax.dot_general(do,v,NT,preferred_element_type=f32)
        p=p_ref[0,0,pl.ds(pl.multiple_of(g*GROUP*SUB,GROUP*SUB),GROUP*SUB),:]
        ds=(p.astype(f32)*(dp-delta)).astype(bf16)
        dq=lax.dot_general(ds,k,(((1,),(0,)),((),())),preferred_element_type=f32)*SCALE
        dq_ref[:,pl.ds(at,GROUP*HD)]=heads_across(dq).astype(bf16)
        dk=jnp.dot(q.T,ds,preferred_element_type=f32)*SCALE
        dv=jnp.dot(do.T,p,preferred_element_type=f32)
        dkv_ref[0,:HD,pl.ds(start,span)]+=dk
        dkv_ref[0,HD:,pl.ds(start,span)]+=dv
        return 0
    lax.fori_loop(0,HEADS//GROUP,body,0)
def att_bwd(q,kv,att,do,p):
    rows=q.shape[0]; width=rows//2; subs=width//SUB; keys=kv.shape[1]; span=keys-width+SUB
    rowspec=pl.BlockSpec((SUB,q.shape[1]),lambda w,s:(w*subs+s,0))
    dsh=(2,2*HD,keys)
    return pl.pallas_call(functools.partial(att_bwd_kernel,span),grid=(2,subs),
      in_specs=[rowspec,pl.BlockSpec((1,keys,2*HD),lambda w,s:(w,0,0)),rowspec,rowspec,pl.BlockSpec((1,1,HEADS*SUB,span),lambda w,s:(w,s,0,0))],
      out_specs=[rowspec,pl.BlockSpec((1,)+dsh[1:],lambda w,s:(w,0,0))],
      out_shape=[jax.ShapeDtypeStruct(q.shape,bf16),jax.ShapeDtypeStruct(dsh,f32)],
      compiler_params=pltpu.CompilerParams(vmem_limit_bytes=56<<20),name="att_bwd")(q,kv,att,do,p)


def dot(a,b,dims=NN): return lax.dot_general(a,b,dims,preferred_element_type=f32)
CH=512; UNIT=256
def mlp_kernel(ff, a2_ref, g_ref, mid_ref, mask_ref, gain_ref, igu_ref, did_ref, ga_ref, gb_ref, da_ref, db_ref, wd_hbm, wgu_own,
               out_ref, dmid_ref, gga_ref, ggb_ref, gda_ref, gdb_ref, land,
               own_v, wbuf, dbuf, acc_o, acc_a, gu_s, dh_s, hid_s, dgu_s, wsem, dsem, ownsem, ssem, rsem):
    me=lax.axis_index("ctx")
    bits=[(me//(1<<b))%2 for b in range(5)]
    nu=ff//UNIT; nc=ff//CH; half=ff//128
    bar=pltpu.get_barrier_semaphore()
    for b in range(5):
        pl.semaphore_signal(bar,1,device_id=flip(me,bits,b),device_id_type=MESH)
    pl.semaphore_wait(bar,5)
    stage=pltpu.make_async_copy(wgu_own,own_v,ownsem)
    stage.start(); stage.wait()
    own=pltpu.make_async_copy(own_v,land.at[bits[4],bits[3],bits[2],bits[1],bits[0]],ownsem)
    own.start()
    SETS=(((ORD_A,0,256,0),(ORD_C,ff,128,0),(ORD_B,ff+128,128,0)),((ORD_A2,0,256,0),(ORD_C2,ff,128,0),(ORD_B2,ff+128,128,0)))
    def ex(v,par,cl,k):
        order,base,n,_=SETS[par][cl]
        bit,have=order[k],order[:k]
        where=tuple(pl.ds(0,2) if b in have else bits[b] for b in (4,3,2,1,0))
        at=base+v*UNIT
        cols=pl.ds(pl.multiple_of(at,128) if not isinstance(at,int) else at,n)
        there=land.at[where+(slice(None),cols)]
        return pltpu.make_async_remote_copy(there if k else wgu_own.at[:,cols],there,ssem.at[v,cl,k],rsem.at[v,cl,k],device_id=flip(me,bits,bit),device_id_type=MESH)
    def step(t,par,guard):
        for k in (4,3,2,1,0):
            v=t+8-LAGS[k]; vp=(par+8-LAGS[k])%2
            def go(v=v,vp=vp,k=k):
                for cl in range(3):
                    if k: ex(v,vp,cl,k-1).wait_recv()
                    ex(v,vp,cl,k).start()
            if guard: pl.when(v<nu)(go)
            elif 0<=v<nu: go()
    def fetch(c,slot):
        n=CH
        return [pltpu.make_async_copy(land.at[(slice(None),)*6+(pl.ds(pl.multiple_of(base+c*CH,128),n),)],wbuf.at[(slot,)+(slice(None),)*6+(pl.ds(o,n),)],wsem.at[slot,i]) for i,(base,o) in enumerate(((0,0),(ff,CH)))]+\
               [pltpu.make_async_copy(wd_hbm.at[pl.ds(pl.multiple_of(c*CH,CH),CH)],dbuf.at[slot],dsem.at[slot])]
    def arrived(c):
        for j in range(CH//UNIT):
            for cl in range(3): ex(c*(CH//UNIT)+j,j%2,cl,4).wait_recv()
    acc_o[...]=jnp.zeros_like(acc_o); acc_a[...]=jnp.zeros_like(acc_a)
    for t in range(-8,0):
        if t==-7: own.wait()
        step(t,t%2,False)
    arrived(0)
    for cp in fetch(0,0): cp.start()
    for cp in fetch(0,0): cp.wait()
    def body(c,_):
        slot=c%2
        step(2*c,0,True)
        gbc=[gb_ref[:,pl.ds(pl.multiple_of(base+c*CH,128),CH)] for base in (0,ff)]
        dac=da_ref[pl.ds(pl.multiple_of(c*CH,CH),CH),:]
        def wx(): return jnp.concatenate([wbuf[slot].reshape(-1,2*CH),jnp.concatenate(gbc,1)],0)
        def wdx(): return jnp.concatenate([dbuf[slot],dac],1)
        def ax(): return jnp.concatenate([a2_ref[...],igu_ref[...]],1)
        def gx(): return jnp.concatenate([g_ref[...],did_ref[...]],1)
        gu_s[...]=dot(ax(),wx())
        step(2*c+1,1,True)
        dh_s[...]=dot(gx(),wdx(),NT)
        k0=0.7978845608028654
        def ew(r,_):
            rows=pl.ds(pl.multiple_of(r*16,16),16)
            gate=gu_s[rows,:CH]; up=gu_s[rows,CH:]; dh=dh_s[rows,:]
            sq=gate*gate
            th=jnp.tanh(gate*(k0+(k0*0.044715)*sq))
            ht=0.5+0.5*th
            gl=gate*ht
            dgl=ht+(gate*(0.5-0.5*th*th))*(k0+(3*k0*0.044715)*sq)
            hid_s[rows,:]=(gl*up).astype(bf16)
            dgu_s[rows,:CH]=(dh*up*dgl).astype(bf16)
            dgu_s[rows,CH:]=(dh*gl).astype(bf16)
            return 0
        lax.fori_loop(0,g_ref.shape[0]//16,ew,0)
        acc_o[...]+=dot(hid_s[...],wdx())
        gda_ref[pl.ds(pl.multiple_of(c*CH,CH),CH),:]=dot(hid_s[...],did_ref[...],TN).astype(bf16)
        r=dot(igu_ref[...],dgu_s[...],TN).astype(bf16)
        for i in range(2):
            for j in range(CH//128):
                ggb_ref[pl.ds(c*(CH//128)+(ff//128)*i+j,1)]=r[None,:,(i*(CH//128)+j)*128:(i*(CH//128)+j+1)*128]
        @pl.when(c+1<nc)
        def _():
            arrived(c+1)
            for cp in fetch(c+1,1-slot): cp.start()
        acc_a[...]+=dot(dgu_s[...],wx(),NT)
        @pl.when(c+1<nc)
        def _():
            for cp in fetch(c+1,1-slot): cp.wait()
        return 0
    lax.fori_loop(0,nc,body,0)
    mask=mask_ref[...]
    g=g_ref[...]
    d=g_ref.shape[1]
    inner_d=(acc_o[:,d:]*mask).astype(bf16)
    mid=mid_ref[...]
    out_ref[...]=(mid+(acc_o[:,:d]+dot(inner_d,db_ref[...]))).astype(bf16)
    r=dot(inner_d,g,TN).astype(bf16)
    for j in range(g.shape[1]//128): gdb_ref[j]=r[:,j*128:(j+1)*128]
    dgu=(acc_a[:,d:]*mask).astype(bf16)
    gga_ref[...]=dot(a2_ref[...],dgu,TN).astype(bf16)
    da2=acc_a[:,:d]+dot(dgu,ga_ref[...],NT)
    e=da2*gain_ref[...]
    rr=lax.rsqrt(jnp.mean(mid*mid,axis=1,keepdims=True)+1e-6)
    dmid_ref[...]=g.astype(f32)+rr*e-(rr*rr*rr)*mid*jnp.mean(e*mid,axis=1,keepdims=True)
    def fin(v,_):
        for par in range(2):
            for cl in range(3):
                for k in range(5): ex(2*v+par,par,cl,k).wait_send()
        return 0
    lax.fori_loop(0,nu//2,fin,0)
def mlp(a2,g,mid,mask,gain,igu,did,ga,gb,da,db,wd,wgu):
    rows,d=a2.shape; ff=da.shape[0]; nu=ff//UNIT
    V=pl.BlockSpec(memory_space=pltpu.VMEM); H=pl.BlockSpec(memory_space=pl.ANY)
    S=jax.ShapeDtypeStruct
    return pl.pallas_call(functools.partial(mlp_kernel,ff),
        in_specs=[V]*11+[H,H],
        out_specs=[V]*6+[H],
        out_shape=[S((rows,d),bf16),S((rows,d),f32),S((d,128),bf16),S((2*ff//128,128,128),bf16),S((ff,128),bf16),S((d//128,128,128),bf16),S((2,)*5+wgu.shape,bf16)],
        scratch_shapes=[pltpu.VMEM(wgu.shape,bf16),pltpu.VMEM((2,)+(2,)*5+(wgu.shape[0],2*CH),bf16),pltpu.VMEM((2,CH,d),bf16),pltpu.VMEM((rows,d+128),f32),pltpu.VMEM((rows,d+128),f32),pltpu.VMEM((rows,2*CH),f32),pltpu.VMEM((rows,CH),f32),pltpu.VMEM((rows,CH),bf16),pltpu.VMEM((rows,2*CH),bf16),
            pltpu.SemaphoreType.DMA((2,2)),pltpu.SemaphoreType.DMA((2,)),pltpu.SemaphoreType.DMA,pltpu.SemaphoreType.DMA((nu,3,5)),pltpu.SemaphoreType.DMA((nu,3,5))],
        compiler_params=pltpu.CompilerParams(collective_id=2,has_side_effects=True,vmem_limit_bytes=60<<20),name="mlp")(a2,g,mid,mask,gain,igu,did,ga,gb,da,db,wd,wgu)


def tiles_out(x):
    return x.reshape(x.shape[0], -1, 128).transpose(1, 0, 2).reshape(-1, 128)


def tiles_in(x, rows):
    return x.reshape(-1, rows, 128).transpose(1, 0, 2).reshape(rows, -1)


def pack(grads):
    parts = [g.astype(bf16) for g in grads]
    have = sum(g.shape[0] for g in parts)
    total = -(-have // 512) * 512
    if total > have:
        parts.append(jnp.zeros((total - have, 128), bf16))
    return jnp.concatenate(parts, axis=0).reshape((2,) * 5 + (total // 32, 128))


def local_own(
    tokens,
    cotangent,
    doc_lengths,
    adapter_ids,
    w_query,
    w_keyval,
    w_output,
    w_gateup,
    w_down,
    gain_attn,
    gain_mlp,
    query_a,
    query_b,
    keyval_a,
    keyval_b,
    output_a,
    output_b,
    gateup_a,
    gateup_b,
    down_a,
    down_b,
):
    count = lax.axis_size("ctx")
    device = lax.axis_index("ctx")
    local_rows = tokens.shape[0]
    width = local_rows // 2
    reach = (WINDOW + width - 1) // width
    key_width = w_keyval.shape[1]
    half_rows = jnp.arange(width, dtype=jnp.int32)
    own_blocks = (device, 2 * count - 1 - device)
    positions = jnp.concatenate(
        [own_blocks[0] * width + half_rows, own_blocks[1] * width + half_rows]
    )
    segment, mask = adapter_mask(doc_lengths, adapter_ids, positions)
    resid = tokens.astype(f32)
    act_one = rms_scale(resid, gain_attn).astype(bf16)
    full_query, full_keyval, full_output, full_down = gather_weights(
        (w_query, w_keyval, w_output, w_down)
    )
    query_full, inner_query = adapted(act_one, full_query, query_a, query_b, mask)
    keyval_full, inner_keyval = adapted(act_one, full_keyval, keyval_a, keyval_b, mask)
    query = query_full.astype(bf16)
    keyval = keyval_full.astype(bf16)
    stacked = [keyval]
    for offset in range(1, reach + 1):
        later = shifted(keyval, "ctx", -offset)
        prior = shifted(keyval, "ctx", offset)
        stacked = [prior] + stacked + [later]
    table = jnp.stack(stacked)
    first_device = device - reach
    key_blocks = [[block - reach + step for step in range(reach + 1)] for block in own_blocks]
    keys = jnp.stack(
        [
            jnp.concatenate([key_block(table, first_device, e, count, width) for e in blocks], axis=0)
            for blocks in key_blocks
        ]
    )
    key_pos = jnp.stack(
        [jnp.concatenate([e * width + half_rows for e in blocks]) for blocks in key_blocks]
    )
    key_seg = segment_of(doc_lengths, key_pos.reshape(-1)).reshape(2, 1, -1)
    attention, prob = att_fwd(query, keys, segment[:, None], key_seg, WINDOW)
    branch_one, inner_output = adapted(attention, full_output, output_a, output_b, mask)
    middle = resid + branch_one
    act_two = rms_scale(middle, gain_mlp).astype(bf16)
    inner_gateup = (dot(act_two, gateup_a) * mask).astype(bf16)
    d_inner_down = (dot(cotangent, down_b, NT) * mask).astype(bf16)
    result, grad_middle, g_gateup_a, g_gateup_b, g_down_a, g_down_b, unused = mlp(
        act_two,
        cotangent,
        middle,
        mask,
        gain_mlp[None, :],
        inner_gateup,
        d_inner_down,
        gateup_a,
        gateup_b,
        down_a,
        down_b,
        full_down,
        w_gateup,
    )
    grad_branch = grad_middle.astype(bf16)
    g_output_a, g_output_b, d_inner_output = adapter_back(
        grad_branch, attention, inner_output, output_b, mask
    )
    grad_attention = (by_cols(grad_branch, full_output) + by_cols(d_inner_output, output_a)).astype(
        bf16
    )
    grad_query, grad_keys = att_bwd(query, keys, attention, grad_attention, prob)
    grad_keys = grad_keys.transpose(0, 2, 1)
    slots = jnp.zeros((2 * reach + 1, local_rows, key_width), f32)
    for which in range(2):
        for step, entry in enumerate(key_blocks[which]):
            piece = grad_keys[which, step * width : (step + 1) * width]
            device_of, row_in = owner_of(entry, count, width)
            at = (device_of - first_device, row_in, jnp.int32(0))
            current = lax.dynamic_slice(slots, at, (1, width, key_width))
            slots = lax.dynamic_update_slice(slots, current + piece[None], at)
    grad_keyval_full = slots[reach]
    for offset in range(1, reach + 1):
        from_lower = shifted(slots[reach + offset].astype(bf16), "ctx", offset).astype(f32)
        from_upper = shifted(slots[reach - offset].astype(bf16), "ctx", -offset).astype(f32)
        grad_keyval_full = grad_keyval_full + from_lower + from_upper
    grad_keyval = grad_keyval_full.astype(bf16)
    g_query_a, g_query_b, d_inner_query = adapter_back(
        grad_query, act_one, inner_query, query_b, mask
    )
    g_keyval_a, g_keyval_b, d_inner_keyval = adapter_back(
        grad_keyval, act_one, inner_keyval, keyval_b, mask
    )
    grad_act_one = (
        by_cols(grad_query, full_query)
        + by_cols(grad_keyval, full_keyval)
        + by_cols(d_inner_query, query_a)
        + by_cols(d_inner_keyval, keyval_a)
    )
    unused, pull_one = jax.vjp(lambda values: rms_scale(values, gain_attn), resid)
    grad_tokens = (grad_middle + pull_one(grad_act_one)[0]).astype(bf16)
    parts = [
        g_query_a,
        tiles_out(g_query_b),
        g_keyval_a,
        tiles_out(g_keyval_b),
        g_output_a,
        tiles_out(g_output_b),
        g_gateup_a,
        g_gateup_b.reshape(-1, 128),
        g_down_a,
        g_down_b.reshape(-1, 128),
    ]
    summed = reduce_packed(pack(parts)).reshape(-1, 128)
    sums = []
    start = 0
    for at, part in enumerate(parts):
        rows = part.shape[0]
        piece = summed[start : start + rows].astype(f32)
        sums.append(tiles_in(piece, 128) if at % 2 else piece)
        start += rows
    return (result, grad_tokens, *sums)


def solution(mesh):
    in_specs = (
        P("ctx", None),
        P("ctx", None),
        P(),
        P(),
        P("ctx", None),
        P("ctx", None),
        P("ctx", None),
        P("ctx", None),
        P("ctx", None),
        P(),
        P(),
        P(),
        P(),
        P(),
        P(),
        P(),
        P(),
        P(),
        P(),
        P(),
        P(),
    )
    out_specs = (P("ctx", None), P("ctx", None), P(), P(), P(), P(), P(), P(), P(), P(), P(), P())
    local = local_own if mesh.shape["ctx"] == 32 else local_native
    return jax.shard_map(local, mesh=mesh, in_specs=in_specs, out_specs=out_specs, check_vma=False)
```

```python
import functools

import jax
import jax.numpy as jnp
from jax import lax
from jax.experimental import pallas as pl
from jax.experimental.pallas import tpu as pltpu
from jax.sharding import PartitionSpec as P

HEADS = 12
HD = 128
FF = 4608
WINDOW = 1024
RANK = 16
ADAPTERS = 8


NORM_EPS = 1e-06
MASKED = -1e30


MESH = pl.DeviceIdType.MESH
bf16 = jnp.bfloat16
f32 = jnp.float32
NN = (((1,), (0,)), ((), ()))
NT = (((1,), (1,)), ((), ()))
TN = (((0,), (0,)), ((), ()))
VMEM = pl.BlockSpec(memory_space=pltpu.VMEM)
HBM = pl.BlockSpec(memory_space=pl.ANY)
ORD_A = (4, 3, 1, 2, 0)
ORD_A2 = (4, 3, 2, 1, 0)
ORD_B = (4, 1, 2, 3, 0)
ORD_B2 = (4, 2, 1, 3, 0)
ORD_C = (4, 2, 3, 1, 0)
ORD_C2 = (4, 1, 3, 2, 0)


def shifted(x, axis, by):
    size = lax.axis_size(axis)
    pairs = [(i, i + by) for i in range(size) if 0 <= i + by < size]
    return lax.ppermute(x, axis, pairs)


def segment_of(doc_lengths, positions):
    starts = jnp.cumsum(doc_lengths) - doc_lengths
    return jnp.sum((starts[None, :] <= positions[:, None]).astype(jnp.int32), axis=1) - 1


def adapter_mask(doc_lengths, adapter_ids, positions):
    segment = segment_of(doc_lengths, positions)
    owner = segment[:, None] == jnp.arange(doc_lengths.shape[0], dtype=jnp.int32)[None, :]
    chosen = jnp.sum(jnp.where(owner, adapter_ids[None, :], 0), axis=1)
    columns = jnp.arange(ADAPTERS * RANK, dtype=jnp.int32) // RANK
    return (segment, (columns[None, :] == chosen[:, None]).astype(jnp.float32))


def rms_scale(values, gain):
    return values * lax.rsqrt(jnp.mean(values * values, axis=-1, keepdims=True) + NORM_EPS) * gain


def by_rows(left, right):
    return lax.dot_general(
        left, right, (((0,), (0,)), ((), ())), preferred_element_type=jnp.float32
    )


def by_cols(left, right):
    return lax.dot_general(
        left, right, (((1,), (1,)), ((), ())), preferred_element_type=jnp.float32
    )


def adapted(inputs, weight, down_part, up_part, mask):
    inner = (jnp.dot(inputs, down_part, preferred_element_type=jnp.float32) * mask).astype(
        jnp.bfloat16
    )
    return (
        jnp.dot(inputs, weight, preferred_element_type=jnp.float32)
        + jnp.dot(inner, up_part, preferred_element_type=jnp.float32),
        inner,
    )


def adapter_back(grad_out, inputs, inner, up_part, mask):
    grad_up = by_rows(inner, grad_out)
    grad_inner = (by_cols(grad_out, up_part) * mask).astype(jnp.bfloat16)
    return (by_rows(inputs, grad_inner), grad_up, grad_inner)


def owner_of(block, count, width):
    device_of = jnp.where(block < count, block, 2 * count - 1 - block)
    return (device_of, jnp.where(block < count, 0, width))


def key_block(table, first_device, block, count, width):
    device_of, row_in = owner_of(block, count, width)
    piece = lax.dynamic_slice(
        table, (device_of - first_device, row_in, jnp.int32(0)), (1, width, table.shape[2])
    )
    return piece[0]


def block_scores(query, keys, allowed):
    rows = query.shape[0]
    heads = query.reshape(rows, HEADS, HD)
    raw = jnp.einsum(
        "rhd,kd->rhk", heads, keys[:, :HD], preferred_element_type=jnp.float32
    ) * HD ** (-0.5)
    return jnp.where(allowed[:, None, :], raw, MASKED)


def attend_forward(query, keys, allowed):
    scores = block_scores(query, keys, allowed)
    top = jnp.max(scores, axis=-1, keepdims=True)
    total = jnp.sum(jnp.exp(scores - top), axis=-1, keepdims=True)
    log_total = top + jnp.log(total)
    weights = jnp.exp(scores - log_total).astype(jnp.bfloat16)
    mixed = jnp.einsum("rhk,kd->rhd", weights, keys[:, HD:], preferred_element_type=jnp.float32)
    return (mixed.reshape(query.shape[0], -1), log_total)


def attend_backward(query, keys, allowed, log_total, grad_out):
    rows = query.shape[0]
    prob = jnp.exp(block_scores(query, keys, allowed) - log_total)
    grad_heads = grad_out.reshape(rows, HEADS, HD)
    grad_prob = jnp.einsum(
        "rhd,kd->rhk", grad_heads, keys[:, HD:], preferred_element_type=jnp.float32
    )
    delta = jnp.sum(prob * grad_prob, axis=-1, keepdims=True)
    grad_scores = (prob * (grad_prob - delta)).astype(jnp.bfloat16)
    scale = HD ** (-0.5)
    grad_query = (
        jnp.einsum("rhk,kd->rhd", grad_scores, keys[:, :HD], preferred_element_type=jnp.float32)
        * scale
    )
    grad_key = (
        jnp.einsum(
            "rhk,rhd->kd",
            grad_scores,
            query.reshape(rows, HEADS, HD),
            preferred_element_type=jnp.float32,
        )
        * scale
    )
    grad_value = jnp.einsum(
        "rhk,rhd->kd", prob.astype(jnp.bfloat16), grad_heads, preferred_element_type=jnp.float32
    )
    return (grad_query.reshape(rows, -1), jnp.concatenate([grad_key, grad_value], axis=1))


def local_native(
    tokens,
    cotangent,
    doc_lengths,
    adapter_ids,
    w_query,
    w_keyval,
    w_output,
    w_gateup,
    w_down,
    gain_attn,
    gain_mlp,
    query_a,
    query_b,
    keyval_a,
    keyval_b,
    output_a,
    output_b,
    gateup_a,
    gateup_b,
    down_a,
    down_b,
):
    count = lax.axis_size("ctx")
    device = lax.axis_index("ctx")
    local_rows = tokens.shape[0]
    width = local_rows // 2
    reach = (WINDOW + width - 1) // width
    key_width = w_keyval.shape[1]
    half_rows = jnp.arange(width, dtype=jnp.int32)
    own_blocks = (device, 2 * count - 1 - device)
    positions = jnp.concatenate(
        [own_blocks[0] * width + half_rows, own_blocks[1] * width + half_rows]
    )
    segment, mask = adapter_mask(doc_lengths, adapter_ids, positions)
    resid = tokens.astype(jnp.float32)
    act_one = rms_scale(resid, gain_attn).astype(jnp.bfloat16)
    full_query, full_keyval, full_output, full_gateup = (
        lax.all_gather(w_query, "ctx", axis=0, tiled=True),
        lax.all_gather(w_keyval, "ctx", axis=0, tiled=True),
        lax.all_gather(w_output, "ctx", axis=0, tiled=True),
        lax.all_gather(w_gateup, "ctx", axis=0, tiled=True),
    )
    query_full, inner_query = adapted(act_one, full_query, query_a, query_b, mask)
    keyval_full, inner_keyval = adapted(act_one, full_keyval, keyval_a, keyval_b, mask)
    query = query_full.astype(jnp.bfloat16)
    keyval = keyval_full.astype(jnp.bfloat16)
    stacked = [keyval]
    for offset in range(1, reach + 1):
        later = shifted(keyval, "ctx", -offset)
        prior = shifted(keyval, "ctx", offset)
        stacked = [prior] + stacked + [later]
    table = jnp.stack(stacked)
    first_device = device - reach
    kept = []
    mixed_parts = []
    for which in range(2):
        block = own_blocks[which]
        key_blocks = [block - reach + step for step in range(reach + 1)]
        keys = jnp.concatenate(
            [key_block(table, first_device, entry, count, width) for entry in key_blocks], axis=0
        )
        key_pos = jnp.concatenate([entry * width + half_rows for entry in key_blocks])
        key_seg = segment_of(doc_lengths, key_pos)
        query_pos = positions[which * width : (which + 1) * width]
        query_seg = segment[which * width : (which + 1) * width]
        allowed = (
            (key_pos[None, :] <= query_pos[:, None])
            & (query_pos[:, None] - key_pos[None, :] < WINDOW)
            & (key_seg[None, :] == query_seg[:, None])
        )
        mixed, log_total = attend_forward(query[which * width : (which + 1) * width], keys, allowed)
        kept.append((key_blocks, keys, allowed, log_total))
        mixed_parts.append(mixed)
    attention = jnp.concatenate(mixed_parts, axis=0).astype(jnp.bfloat16)
    branch_one, inner_output = adapted(attention, full_output, output_a, output_b, mask)
    middle = resid + branch_one
    act_two = rms_scale(middle, gain_mlp).astype(jnp.bfloat16)
    gate_up, inner_gateup = adapted(act_two, full_gateup, gateup_a, gateup_b, mask)
    gate = gate_up[:, :FF]
    upper = gate_up[:, FF:]
    hidden = (jax.nn.gelu(gate) * upper).astype(jnp.bfloat16)
    down_main = jnp.dot(
        hidden,
        lax.all_gather(w_down, "ctx", axis=0, tiled=True),
        preferred_element_type=jnp.float32,
    )
    inner_down = (jnp.dot(hidden, down_a, preferred_element_type=jnp.float32) * mask).astype(
        jnp.bfloat16
    )
    result = middle + (down_main + jnp.dot(inner_down, down_b, preferred_element_type=jnp.float32))
    grad_down_a, grad_down_b, d_inner_down = adapter_back(
        cotangent, hidden, inner_down, down_b, mask
    )
    grad_hidden = by_cols(cotangent, lax.all_gather(w_down, "ctx", axis=0, tiled=True)) + by_cols(
        d_inner_down, down_a
    )

    def gated(gate_part, up_part):
        return jax.nn.gelu(gate_part) * up_part

    unused, pull_glu = jax.vjp(gated, gate, upper)
    grad_gate, grad_up = pull_glu(grad_hidden)
    grad_gateup = jnp.concatenate([grad_gate, grad_up], axis=1).astype(jnp.bfloat16)
    grad_gateup_a, grad_gateup_b, d_inner_gateup = adapter_back(
        grad_gateup, act_two, inner_gateup, gateup_b, mask
    )
    grad_act_two = by_cols(grad_gateup, full_gateup) + by_cols(d_inner_gateup, gateup_a)
    unused, pull_two = jax.vjp(lambda values: rms_scale(values, gain_mlp), middle)
    grad_middle = cotangent.astype(jnp.float32) + pull_two(grad_act_two)[0]
    grad_branch = grad_middle.astype(jnp.bfloat16)
    grad_output_a, grad_output_b, d_inner_output = adapter_back(
        grad_branch, attention, inner_output, output_b, mask
    )
    grad_attention = (by_cols(grad_branch, full_output) + by_cols(d_inner_output, output_a)).astype(
        jnp.bfloat16
    )
    query_grads = []
    key_grads = []
    for which in range(2):
        key_blocks, keys, allowed, log_total = kept[which]
        rows_query = query[which * width : (which + 1) * width]
        rows_grad = grad_attention[which * width : (which + 1) * width]
        grad_rows, grad_keys = attend_backward(rows_query, keys, allowed, log_total, rows_grad)
        query_grads.append(grad_rows)
        for step, entry in enumerate(key_blocks):
            key_grads.append((entry, grad_keys[step * width : (step + 1) * width]))
    grad_query = jnp.concatenate(query_grads, axis=0).astype(jnp.bfloat16)
    slots = jnp.zeros((2 * reach + 1, local_rows, key_width), jnp.float32)
    for entry, piece in key_grads:
        device_of, row_in = owner_of(entry, count, width)
        slot = device_of - first_device
        current = lax.dynamic_slice(slots, (slot, row_in, jnp.int32(0)), (1, width, key_width))
        slots = lax.dynamic_update_slice(slots, current + piece[None], (slot, row_in, jnp.int32(0)))
    grad_keyval_full = slots[reach]
    for offset in range(1, reach + 1):
        from_lower = shifted(slots[reach + offset].astype(jnp.bfloat16), "ctx", offset).astype(
            jnp.float32
        )
        from_upper = shifted(slots[reach - offset].astype(jnp.bfloat16), "ctx", -offset).astype(
            jnp.float32
        )
        grad_keyval_full = grad_keyval_full + from_lower + from_upper
    grad_keyval = grad_keyval_full.astype(jnp.bfloat16)
    grad_query_a, grad_query_b, d_inner_query = adapter_back(
        grad_query, act_one, inner_query, query_b, mask
    )
    grad_keyval_a, grad_keyval_b, d_inner_keyval = adapter_back(
        grad_keyval, act_one, inner_keyval, keyval_b, mask
    )
    grad_act_one = (
        by_cols(grad_query, full_query)
        + by_cols(grad_keyval, full_keyval)
        + by_cols(d_inner_query, query_a)
        + by_cols(d_inner_keyval, keyval_a)
    )
    unused, pull_one = jax.vjp(lambda values: rms_scale(values, gain_attn), resid)
    grad_tokens = (grad_middle + pull_one(grad_act_one)[0]).astype(jnp.bfloat16)
    sums = lax.psum(
        (
            grad_query_a,
            grad_query_b,
            grad_keyval_a,
            grad_keyval_b,
            grad_output_a,
            grad_output_b,
            grad_gateup_a,
            grad_gateup_b,
            grad_down_a,
            grad_down_b,
        ),
        "ctx",
    )
    return (
        result.astype(jnp.bfloat16),
        grad_tokens,
        sums[0],
        sums[1],
        sums[2],
        sums[3],
        sums[4],
        sums[5],
        sums[6],
        sums[7],
        sums[8],
        sums[9],
    )


def flip(me, bits, b):
    return (me+(1-2*bits[b])*(1<<b),)
def reduce_kernel(rows, in_ref, out_ref, r0, r1, r2, r3, r4, ssem, rsem):
    rb=(r0,r1,r2,r3,r4)
    me=lax.axis_index("ctx")
    bits=[(me//(1<<b))%2 for b in range(5)]
    bar=pltpu.get_barrier_semaphore()
    for b in range(5):
        pl.semaphore_signal(bar,1,device_id=flip(me,bits,b),device_id_type=MESH)
    pl.semaphore_wait(bar,5)
    t=rows//16
    a=round(t*3/7); bb=round(t*3/14)
    classes=[(0,a*16,ORD_A),(a*16,bb*16,ORD_B),((a+bb)*16,rows-(a+bb)*16,ORD_C)]
    def rs(cl,s):
        r0_,n,order=classes[cl]
        red=order[::-1]
        bit=red[s]; done=red[:s]
        rem=[b for b in (4,3,2,1,0) if b not in done]
        src=in_ref if s==0 else rb[s-1]
        idx=tuple((1-bits[b]) if b==bit else slice(None) for b in rem)
        return pltpu.make_async_remote_copy(src.at[idx+(pl.ds(r0_,n),)],rb[s].at[(slice(None),)*(4-s)+(pl.ds(r0_,n),)],ssem.at[cl,s],rsem.at[cl,s],device_id=flip(me,bits,bit),device_id_type=MESH)
    def add(cl,s):
        r0_,n,order=classes[cl]
        red=order[::-1]
        bit=red[s]; done=red[:s]
        rem=[b for b in (4,3,2,1,0) if b not in done]
        src=in_ref if s==0 else rb[s-1]
        rs_=pl.ds(r0_,n)
        nd=4-s
        def body(j,_):
            ds=[(j//(1<<(nd-1-i)))%2 for i in range(nd)]
            it=iter(ds)
            si=tuple(bits[b] if b==bit else next(it) for b in rem)
            v=src[si+(rs_,)].astype(f32)+rb[s][tuple(ds)+(rs_,)].astype(f32)
            rb[s][tuple(ds)+(rs_,)]=v.astype(bf16)
            return 0
        lax.fori_loop(0,1<<nd,body,0)
    def ag(cl,k):
        r0_,n,order=classes[cl]
        bit=order[k]; have=order[:k]
        idx=tuple(slice(None) if b in have else bits[b] for b in (4,3,2,1,0))+(pl.ds(r0_,n),)
        src=out_ref.at[idx] if k else rb[4].at[pl.ds(r0_,n)]
        return pltpu.make_async_remote_copy(src,out_ref.at[idx],ssem.at[cl,5+k],rsem.at[cl,5+k],device_id=flip(me,bits,bit),device_id_type=MESH)
    for cl in range(3): rs(cl,0).start()
    for s in range(5):
        for cl in range(3):
            rs(cl,s).wait_recv()
            add(cl,s)
            if s<4: rs(cl,s+1).start()
            else:
                ag(cl,0).start()
                r0_,n,_=classes[cl]
                out_ref[bits[4],bits[3],bits[2],bits[1],bits[0],pl.ds(r0_,n)]=rb[4][pl.ds(r0_,n)]
    for k in range(1,5):
        for cl in range(3):
            ag(cl,k-1).wait_recv()
            ag(cl,k).start()
    for cl in range(3): ag(cl,4).wait_recv()
    for cl in range(3):
        for s in range(5):
            rs(cl,s).wait_send(); ag(cl,s).wait_send()
def reduce_packed(x, cid=1):
    rows=x.shape[5]
    return pl.pallas_call(functools.partial(reduce_kernel,rows),
        out_shape=jax.ShapeDtypeStruct(x.shape,x.dtype),
        in_specs=[pl.BlockSpec(memory_space=pltpu.VMEM)],out_specs=pl.BlockSpec(memory_space=pltpu.VMEM),
        scratch_shapes=[pltpu.VMEM((2,)*(4-s)+(rows,128),bf16) for s in range(5)]+[pltpu.SemaphoreType.DMA((3,10)),pltpu.SemaphoreType.DMA((3,10))],
        compiler_params=pltpu.CompilerParams(collective_id=cid,has_side_effects=True,vmem_limit_bytes=40<<20))(x)


BGROUP = 6
CHUNK = 512
UNIT = 256
SUB = 128
GROUP = 4
SCALE = HD ** (-0.5)
LAGS = (0, 1, 2, 4, 6)
SOFT_UNROLL = 8
AHEAD = 24


def dot(a, b, dims=NN):
    return lax.dot_general(a, b, dims, preferred_element_type=f32)


def tile_at(i, size):
    return pl.ds(i * size if isinstance(i, int) else pl.multiple_of(i * size, size), size)


def even_odd(par, low, high):
    if par % 2:
        return ((low, 2, ORD_A2), (high, 1, ORD_C2), (high + 1, 1, ORD_B2))
    return ((low, 2, ORD_A), (high, 1, ORD_C), (high + 1, 1, ORD_B))


def bits_of(me):
    return [(me // (1 << b)) % 2 for b in range(5)]


def meet_all(count, me):
    barrier = pltpu.get_barrier_semaphore()

    def greet(k, unused):
        pl.semaphore_signal(
            barrier, 1, device_id=(lax.rem(me + k, count),), device_id_type=MESH
        )
        return unused

    lax.fori_loop(1, count, greet, 0)
    pl.semaphore_wait(barrier, count - 1)


def heads_down(x):
    return jnp.concatenate([x[:, i * HD : (i + 1) * HD] for i in range(x.shape[1] // HD)], axis=0)


def heads_across(x):
    return jnp.concatenate([x[i * SUB : (i + 1) * SUB] for i in range(x.shape[0] // SUB)], axis=1)


def norm_rows(read, gain_ref, write, rows):
    def block(r, unused):
        at = tile_at(r, 16)
        x = read(at)
        scale = lax.rsqrt(jnp.mean(x * x, axis=1, keepdims=True) + NORM_EPS)
        write(at, (x * scale * gain_ref[...]).astype(bf16))
        return unused

    lax.fori_loop(0, rows // 16, block, 0, unroll=8)


def forward_kernel(
    count,
    x_ref,
    g_ref,
    mask_ref,
    qseg_ref,
    kseg_ref,
    gain1_ref,
    gain2_ref,
    qa_ref,
    qb_ref,
    ka_ref,
    kb_ref,
    oa_ref,
    ob_ref,
    ga_ref,
    gb_ref,
    da_ref,
    db_ref,
    wq_own,
    wk_own,
    wo_own,
    wd_own,
    wg_own,
    out_ref,
    dmid_ref,
    a1_ref,
    q_ref,
    keys_ref,
    att_ref,
    iq_ref,
    ik_ref,
    io_ref,
    gga_ref,
    ggb_ref,
    gda_ref,
    gdb_ref,
    prob_hbm,
    wq_all,
    wk_all,
    wo_all,
    wd_all,
    wg_all,
    held_q,
    held_k,
    held_o,
    held_d,
    held_g,
    wbuf,
    dbuf,
    pbuf,
    kv_own,
    a2_s,
    igu_s,
    did_s,
    acc_o,
    acc_a,
    gu_s,
    dh_s,
    hid_s,
    dgu_s,
    wsem,
    dsem,
    psem,
    own_sem,
    xsend,
    xrecv,
    hsend,
    hrecv,
):
    rows, d = x_ref.shape
    width = rows // 2
    reach = WINDOW // width
    keys = keys_ref.shape[1]
    span = keys - width + SUB
    ff = da_ref.shape[0]
    nu, nc = ff // UNIT, ff // CHUNK
    me = lax.axis_index("ctx")
    bits = bits_of(me)
    meet_all(count, me)
    here = (bits[4], bits[3], bits[2], bits[1], bits[0])
    own = (wq_own, wk_own, wo_own, wd_own, wg_own)
    held = (held_q, held_k, held_o, held_d, held_g)
    full = (wq_all, wk_all, wo_all, wd_all, wg_all)

    def where(bit_set):
        return tuple(pl.ds(0, 2) if b in bit_set else bits[b] for b in (4, 3, 2, 1, 0))

    def remote(src, dst, send, recv, bit):
        return pltpu.make_async_remote_copy(
            src, dst, send, recv, device_id=flip(me, bits, bit), device_id_type=MESH
        )

    units = []
    for u in range(3):
        units.append((0, 0, even_odd(u, 4 * u, 4 * u + 2)))
    units.append((1, 0, ((0, 1, ORD_A), (1, 1, ORD_C2))))
    for u in range(3):
        units.append((2, 0, even_odd(u, 4 * u, 4 * u + 2)))
    thick = wd_own.shape[0] // 3
    for u in range(9):
        units.append((3, u // 3 * thick, even_odd(u + 1, u % 3 * 4, u % 3 * 4 + 2)))
    first = len(units)

    def exchange(u, cl, k):
        w, row, split = units[u]
        tile, tiles, order = split[cl]
        lines = pl.ds(row, wq_own.shape[0])
        cols = pl.ds(tile * 128, tiles * 128)
        there = full[w].at[where(order[:k]) + (lines, cols)]
        return remote(
            there if k else own[w].at[lines, cols],
            there,
            xsend.at[u, cl, k],
            xrecv.at[u, cl, k],
            order[k],
        )

    def gate(v, par, cl, k):
        tile, tiles, order = even_odd(par, 0, ff // 128)[cl]
        at = tile * 128 + v * UNIT
        cols = pl.ds(at if isinstance(at, int) else pl.multiple_of(at, 128), tiles * 128)
        there = wg_all.at[where(order[:k]) + (slice(None), cols)]
        return remote(
            there if k else wg_own.at[:, cols],
            there,
            xsend.at[first + v, cl, k],
            xrecv.at[first + v, cl, k],
            order[k],
        )

    staged = [pltpu.make_async_copy(own[w], held[w], own_sem.at[w]) for w in range(5)]
    placed = [pltpu.make_async_copy(held[w], full[w].at[here], own_sem.at[w]) for w in range(5)]
    for copy in staged:
        copy.start()
    state = {"step": 0, "placed": set()}

    def place(w):
        if w not in state["placed"]:
            state["placed"].add(w)
            placed[w].wait()

    def steps(n):
        while state["step"] < n:
            t = state["step"]
            state["step"] += 1
            for k in (4, 3, 2, 1, 0):
                u = t - LAGS[k]
                if not 0 <= u < first + nu:
                    continue
                w = units[u][0] if u < first else 4
                if k:
                    place(w)
                for cl in range(2 if w == 1 else 3):
                    at = (
                        functools.partial(exchange, u, cl)
                        if u < first
                        else functools.partial(gate, u - first, (u - first) % 2, cl)
                    )
                    if k:
                        at(k - 1).wait_recv()
                    at(k).start()

    def loop_steps(c, point):
        for i in (2 * point, 2 * point + 1):
            t, k = i // 5, 4 - i % 5
            v = 2 * c + t + AHEAD - first - LAGS[k]
            par = (t + AHEAD - first - LAGS[k]) % 2

            @pl.when(v < nu)
            def _(v=v, par=par, k=k):
                for cl in range(3):
                    if k:
                        gate(v, par, cl, k - 1).wait_recv()
                    gate(v, par, cl, k).start()

    def arrived(weight_at):
        for u, unit in enumerate(units):
            if unit[0] == weight_at:
                for cl in range(len(unit[2])):
                    exchange(u, cl, 4).wait_recv()

    def load(w, lo, n, slot, at, sem):
        return pltpu.make_async_copy(
            full[w].at[(slice(None),) * 6 + (pl.ds(lo, n),)],
            wbuf.at[(slot,) + (slice(None),) * 6 + (pl.ds(at, n),)],
            wsem.at[slot, sem],
        )

    def weight(slot, lo, n):
        return wbuf[slot, :, :, :, :, :, :, lo : lo + n].reshape(-1, n)

    for w in range(5):
        staged[w].wait()
        placed[w].start()
    steps(4)
    def read_x(at):
        return x_ref[at, :].astype(f32)

    def write_a1(at, y):
        a1_ref[at, :] = y

    norm_rows(read_x, gain1_ref, write_a1, rows)
    iq_ref[...] = (dot(a1_ref[...], qa_ref[...]) * mask_ref[...]).astype(bf16)
    ik_ref[...] = (dot(a1_ref[...], ka_ref[...]) * mask_ref[...]).astype(bf16)
    did_s[...] = (dot(g_ref[...], db_ref[...], NT) * mask_ref[...]).astype(bf16)
    steps(10)
    arrived(0)
    arrived(1)
    loads = [load(0, 0, 1024, 0, 0, 0), load(0, 1024, d - 1024, 1, 0, 0)]
    loads.append(load(1, 0, 2 * HD, 1, d - 1024, 1))
    for copy in loads:
        copy.start()
    for copy in loads:
        copy.wait()

    def beside(a, b):
        return jnp.concatenate([a, b], axis=1)

    def under(a, b):
        return jnp.concatenate([a, b], axis=0)

    kv_own[...] = dot(
        beside(a1_ref[...], ik_ref[...]), under(weight(1, d - 1024, 2 * HD), kb_ref[...])
    ).astype(bf16)
    keys_ref[0, pl.ds(reach * width, width)] = kv_own[pl.ds(0, width)]
    keys_ref[1, pl.ds(reach * width, width)] = kv_own[pl.ds(width, width)]

    def low(j):
        block = me + j
        upper = block // count
        target = block + upper * (2 * count - 1 - 2 * block)
        copy = pltpu.make_async_remote_copy(
            kv_own.at[pl.ds(0, width)],
            keys_ref.at[upper, pl.ds((reach - j) * width, width)],
            hsend.at[0, j],
            hrecv.at[upper, j],
            device_id=(target,),
            device_id_type=MESH,
        )
        return copy, target

    def high(j):
        return pltpu.make_async_remote_copy(
            kv_own.at[pl.ds(width, width)],
            keys_ref.at[1, pl.ds((reach - j) * width, width)],
            hsend.at[1, j],
            hrecv.at[1, j],
            device_id=(me - j,),
            device_id_type=MESH,
        )

    def incoming(which, j):
        return pltpu.make_async_remote_copy(
            kv_own.at[pl.ds(0, width)],
            keys_ref.at[which, pl.ds((reach - j) * width, width)],
            hsend.at[0, j],
            hrecv.at[which, j],
            device_id=flip(me, bits, 0),
            device_id_type=MESH,
        )

    for j in range(1, reach + 1):
        copy, target = low(j)
        pl.when(target != me)(copy.start)
        pl.when(me >= j)(high(j).start)

        @pl.when(target == me)
        def _(j=j):
            keys_ref[1, pl.ds((reach - j) * width, width)] = kv_own[pl.ds(0, width)]

        @pl.when(me < j)
        def _(j=j):
            keys_ref[0, pl.ds((reach - j) * width, width)] = jnp.zeros((width, 2 * HD), bf16)

    steps(11)
    q_ref[:, :1024] = dot(
        beside(a1_ref[...], iq_ref[...]), under(weight(0, 0, 1024), qb_ref[:, :1024])
    ).astype(bf16)
    q_ref[:, 1024:] = dot(
        beside(a1_ref[...], iq_ref[...]), under(weight(1, 0, d - 1024), qb_ref[:, 1024:])
    ).astype(bf16)
    for j in range(1, reach + 1):
        pl.when(me >= j)(incoming(0, j).wait_recv)
        pl.when(2 * me != 2 * count - 1 - j)(incoming(1, j).wait_recv)
    steps(12)

    groups = HEADS // GROUP
    subs = width // SUB
    turn = 0
    for which in range(2):
        for s in range(subs):
            base = s * SUB
            lines = slice(which * width + base, which * width + base + SUB)
            row = lax.broadcasted_iota(jnp.int32, (SUB, span), 0)
            col = lax.broadcasted_iota(jnp.int32, (SUB, span), 1)
            ok = (
                (col <= row + (span - SUB))
                & (col > row + (span - SUB - WINDOW))
                & (kseg_ref[which, :, base : base + span] == qseg_ref[lines, :])
            )
            acc_a[:SUB, :span] = jnp.where(ok, 0.0, MASKED)

            for g in range(groups):
                heads = slice(g * GROUP * HD, (g + 1) * GROUP * HD)
                k = keys_ref[which, base : base + span, :HD]
                v = keys_ref[which, base : base + span, HD:]
                acc_o[: GROUP * SUB, :span] = dot(heads_down(q_ref[lines, heads]), k, NT)
                slot = turn % 2
                if turn >= 2:
                    pltpu.make_async_copy(
                        pbuf.at[slot], prob_hbm.at[0, 0, pl.ds(0, GROUP * SUB)], psem.at[slot]
                    ).wait()

                def soft(r, unused, slot=slot):
                    at = tile_at(r, 16)
                    bias = acc_a[tile_at(r % (SUB // 16), 16), :span]
                    sc = acc_o[at, :span] * SCALE + bias
                    e = jnp.exp(sc - jnp.max(sc, axis=1, keepdims=True))
                    inv = 1.0 / jnp.sum(e, axis=1, keepdims=True)
                    pbuf[slot, at, :] = (e * inv).astype(bf16)
                    return unused

                lax.fori_loop(0, GROUP * SUB // 16, soft, 0, unroll=SOFT_UNROLL)
                pltpu.make_async_copy(
                    pbuf.at[slot],
                    prob_hbm.at[which, s, pl.ds(g * GROUP * SUB, GROUP * SUB)],
                    psem.at[slot],
                ).start()
                att_ref[lines, heads] = heads_across(dot(pbuf[slot], v)).astype(bf16)
                turn += 1
            steps(13 + which * subs + s)
    for slot in range(2):
        pltpu.make_async_copy(
            pbuf.at[slot], prob_hbm.at[0, 0, pl.ds(0, GROUP * SUB)], psem.at[slot]
        ).wait()
    arrived(2)
    loads = [load(2, 0, 1024, 0, 0, 0), load(2, 1024, d - 1024, 1, 0, 0)]
    for copy in loads:
        copy.start()
    io_ref[...] = (dot(att_ref[...], oa_ref[...]) * mask_ref[...]).astype(bf16)
    for copy in loads:
        copy.wait()
    dmid_ref[:, :1024] = x_ref[:, :1024].astype(f32) + dot(
        beside(att_ref[...], io_ref[...]), under(weight(0, 0, 1024), ob_ref[:, :1024])
    )
    dmid_ref[:, 1024:] = x_ref[:, 1024:].astype(f32) + dot(
        beside(att_ref[...], io_ref[...]), under(weight(1, 0, d - 1024), ob_ref[:, 1024:])
    )
    steps(17)

    def read_mid(at):
        return dmid_ref[at, :]

    def write_a2(at, y):
        a2_s[at, :] = y

    norm_rows(read_mid, gain2_ref, write_a2, rows)
    igu_s[...] = (dot(a2_s[...], ga_ref[...]) * mask_ref[...]).astype(bf16)
    acc_o[...] = jnp.zeros_like(acc_o)
    acc_a[...] = jnp.zeros_like(acc_a)
    steps(AHEAD)
    arrived(3)

    def arrived_gate(c):
        for j in range(CHUNK // UNIT):
            for cl in range(3):
                gate(c * (CHUNK // UNIT) + j, j % 2, cl, 4).wait_recv()

    def down_rows(c):
        return wd_rows.at[tile_at(c, CHUNK)]

    wd_rows = wd_all.reshape(ff, d)

    def fetch(c, slot):
        cps = [
            pltpu.make_async_copy(
                wg_all.at[(slice(None),) * 6 + (tile_at_base(base, c),)],
                wbuf.at[(slot,) + (slice(None),) * 6 + (pl.ds(o, CHUNK),)],
                wsem.at[slot, i],
            )
            for i, (base, o) in enumerate(((0, 0), (ff, CHUNK)))
        ]
        cps.append(pltpu.make_async_copy(down_rows(c), dbuf.at[slot], dsem.at[slot]))
        return cps

    def tile_at_base(base, c):
        at = base + c * CHUNK
        return pl.ds(at if isinstance(at, int) else pl.multiple_of(at, 128), CHUNK)

    arrived_gate(0)
    for copy in fetch(0, 0):
        copy.start()
    for copy in fetch(0, 0):
        copy.wait()

    def chunk(c, unused):
        slot = c % 2
        loop_steps(c, 0)
        gbc = beside(gb_ref[:, tile_at_base(0, c)], gb_ref[:, tile_at_base(ff, c)])
        dac = da_ref[tile_at(c, CHUNK), :]

        def wx():
            return under(weight(slot, 0, 2 * CHUNK), gbc)

        def wdx():
            return beside(dbuf[slot], dac)

        gu_s[...] = dot(beside(a2_s[...], igu_s[...]), wx())
        loop_steps(c, 1)
        dh_s[...] = dot(beside(g_ref[...], did_s[...]), wdx(), NT)
        k0 = 0.7978845608028654

        def glu(r, unused):
            at = tile_at(r, 16)
            gate_v, up, dh = gu_s[at, :CHUNK], gu_s[at, CHUNK:], dh_s[at, :]
            sq = gate_v * gate_v
            th = jnp.tanh(gate_v * (k0 + (k0 * 0.044715) * sq))
            ht = 0.5 + 0.5 * th
            gl = gate_v * ht
            dgl = ht + (gate_v * (0.5 - 0.5 * th * th)) * (k0 + (3 * k0 * 0.044715) * sq)
            hid_s[at, :] = (gl * up).astype(bf16)
            dgu_s[at, :CHUNK] = (dh * up * dgl).astype(bf16)
            dgu_s[at, CHUNK:] = (dh * gl).astype(bf16)
            return unused

        loop_steps(c, 2)
        lax.fori_loop(0, rows // 16, glu, 0)
        loop_steps(c, 3)
        acc_o[...] += dot(hid_s[...], wdx())
        loop_steps(c, 4)
        gda_ref[tile_at(c, CHUNK), :] = dot(hid_s[...], did_s[...], TN).astype(bf16)
        r = dot(igu_s[...], dgu_s[...], TN).astype(bf16)
        for i in range(2):
            for j in range(CHUNK // 128):
                lo = i * CHUNK + j * 128
                ggb_ref[pl.ds(c * (CHUNK // 128) + (ff // 128) * i + j, 1)] = r[
                    None, :, lo : lo + 128
                ]

        @pl.when(c + 1 < nc)
        def _():
            arrived_gate(c + 1)
            for copy in fetch(c + 1, 1 - slot):
                copy.start()

        acc_a[...] += dot(dgu_s[...], wx(), NT)

        @pl.when(c + 1 < nc)
        def _():
            for copy in fetch(c + 1, 1 - slot):
                copy.wait()

        return unused

    lax.fori_loop(0, nc, chunk, 0)
    inner_d = (acc_o[:, d:] * mask_ref[...]).astype(bf16)
    acc_o[:, :d] += dot(inner_d, db_ref[...])
    r = dot(inner_d, g_ref[...], TN).astype(bf16)
    for j in range(d // 128):
        gdb_ref[j] = r[:, j * 128 : (j + 1) * 128]
    dgu = (acc_a[:, d:] * mask_ref[...]).astype(bf16)
    gga_ref[...] = dot(a2_s[...], dgu, TN).astype(bf16)
    acc_a[:, :d] += dot(dgu, ga_ref[...], NT)

    def finish(r, unused):
        at = tile_at(r, 16)
        mid = dmid_ref[at, :]
        out_ref[at, :] = (mid + acc_o[at, :d]).astype(bf16)
        e = acc_a[at, :d] * gain2_ref[...]
        rr = lax.rsqrt(jnp.mean(mid * mid, axis=1, keepdims=True) + NORM_EPS)
        pull = (rr * rr * rr) * jnp.mean(e * mid, axis=1, keepdims=True)
        dmid_ref[at, :] = g_ref[at, :].astype(f32) + rr * e - pull * mid
        return unused

    lax.fori_loop(0, rows // 16, finish, 0, unroll=8)
    for j in range(1, reach + 1):
        copy, target = low(j)
        pl.when(target != me)(copy.wait_send)
        pl.when(me >= j)(high(j).wait_send)
    for u, unit in enumerate(units):
        for cl in range(len(unit[2])):
            for k in range(5):
                exchange(u, cl, k).wait_send()

    def sent(v, unused):
        for par in range(2):
            for cl in range(3):
                for k in range(5):
                    gate(2 * v + par, par, cl, k).wait_send()
        return unused

    lax.fori_loop(0, nu // 2, sent, 0)


def forward(count, small, weights):
    x, g = small[0], small[1]
    rows, d = x.shape
    ff = weights[3].shape[0] * count
    width = rows // 2
    keys = WINDOW + width
    span = keys - width + SUB
    nu = ff // UNIT
    S = jax.ShapeDtypeStruct
    full = [S((2,) * 5 + w.shape, bf16) for w in weights]
    outs = [
        S((rows, d), bf16),
        S((rows, d), f32),
        S((rows, d), bf16),
        S((rows, d), bf16),
        S((2, keys, 2 * HD), bf16),
        S((rows, d), bf16),
        S((rows, 128), bf16),
        S((rows, 128), bf16),
        S((rows, 128), bf16),
        S((d, 128), bf16),
        S((2 * ff // 128, 128, 128), bf16),
        S((ff, 128), bf16),
        S((d // 128, 128, 128), bf16),
    ]
    DMA = pltpu.SemaphoreType.DMA
    return pl.pallas_call(
        functools.partial(forward_kernel, count),
        in_specs=[VMEM] * len(small) + [HBM] * 5,
        out_specs=[VMEM] * len(outs) + [HBM] * 6,
        out_shape=outs + [S((2, width // SUB, HEADS * SUB, span), bf16)] + full,
        scratch_shapes=[pltpu.VMEM(w.shape, bf16) for w in weights]
        + [
            pltpu.VMEM((2,) * 6 + (weights[0].shape[0], 2 * CHUNK), bf16),
            pltpu.VMEM((2, CHUNK, d), bf16),
            pltpu.VMEM((2, GROUP * SUB, span), bf16),
            pltpu.VMEM((rows, 2 * HD), bf16),
            pltpu.VMEM((rows, d), bf16),
            pltpu.VMEM((rows, 128), bf16),
            pltpu.VMEM((rows, 128), bf16),
            pltpu.VMEM((rows, d + 128), f32),
            pltpu.VMEM((rows, d + 128), f32),
            pltpu.VMEM((rows, 2 * CHUNK), f32),
            pltpu.VMEM((rows, CHUNK), f32),
            pltpu.VMEM((rows, CHUNK), bf16),
            pltpu.VMEM((rows, 2 * CHUNK), bf16),
            DMA((2, 2)),
            DMA((2,)),
            DMA((2,)),
            DMA((5,)),
            DMA((16 + nu, 3, 5)),
            DMA((16 + nu, 3, 5)),
            DMA((2, 5)),
            DMA((2, 5)),
        ],
        compiler_params=pltpu.CompilerParams(
            collective_id=0, has_side_effects=True, vmem_limit_bytes=63 << 20
        ),
        name="forward",
    )(*small, *weights)


def att_bwd_kernel(span, q_ref, kv_ref, att_ref, do_ref, p_ref, dq_ref, dkv_ref):
    s=pl.program_id(1)
    start=pl.multiple_of(s*SUB,SUB)
    k=kv_ref[0,pl.ds(start,span),:HD]; v=kv_ref[0,pl.ds(start,span),HD:]
    @pl.when(s==0)
    def _(): dkv_ref[...]=jnp.zeros_like(dkv_ref)
    def body(g,_):
        at=pl.multiple_of(g*BGROUP*HD,BGROUP*HD)
        q=heads_down(q_ref[:,pl.ds(at,BGROUP*HD)])
        do=heads_down(do_ref[:,pl.ds(at,BGROUP*HD)])
        o=heads_down(att_ref[:,pl.ds(at,BGROUP*HD)])
        delta=jnp.sum(do.astype(f32)*o.astype(f32),axis=1,keepdims=True)
        dp=lax.dot_general(do,v,NT,preferred_element_type=f32)
        p=p_ref[0,0,pl.ds(pl.multiple_of(g*BGROUP*SUB,BGROUP*SUB),BGROUP*SUB),:]
        ds=(p.astype(f32)*(dp-delta)).astype(bf16)
        dq=lax.dot_general(ds,k,(((1,),(0,)),((),())),preferred_element_type=f32)*SCALE
        dq_ref[:,pl.ds(at,BGROUP*HD)]=heads_across(dq).astype(bf16)
        dk=jnp.dot(q.T,ds,preferred_element_type=f32)*SCALE
        dv=jnp.dot(do.T,p,preferred_element_type=f32)
        dkv_ref[0,:HD,pl.ds(start,span)]+=dk
        dkv_ref[0,HD:,pl.ds(start,span)]+=dv
        return 0
    lax.fori_loop(0,HEADS//BGROUP,body,0)
def att_bwd(q,kv,att,do,p):
    rows=q.shape[0]; width=rows//2; subs=width//SUB; keys=kv.shape[1]; span=keys-width+SUB
    rowspec=pl.BlockSpec((SUB,q.shape[1]),lambda w,s:(w*subs+s,0))
    dsh=(2,2*HD,keys)
    return pl.pallas_call(functools.partial(att_bwd_kernel,span),grid=(2,subs),
      in_specs=[rowspec,pl.BlockSpec((1,keys,2*HD),lambda w,s:(w,0,0)),rowspec,rowspec,pl.BlockSpec((1,1,HEADS*SUB,span),lambda w,s:(w,s,0,0))],
      out_specs=[rowspec,pl.BlockSpec((1,)+dsh[1:],lambda w,s:(w,0,0))],
      out_shape=[jax.ShapeDtypeStruct(q.shape,bf16),jax.ShapeDtypeStruct(dsh,f32)],
      compiler_params=pltpu.CompilerParams(vmem_limit_bytes=56<<20),name="att_bwd")(q,kv,att,do,p)


def tiles_out(x):
    return x.reshape(x.shape[0], -1, 128).transpose(1, 0, 2).reshape(-1, 128)


def tiles_in(x, rows):
    return x.reshape(-1, rows, 128).transpose(1, 0, 2).reshape(rows, -1)


def pack(grads):
    parts = [g.astype(bf16) for g in grads]
    have = sum(g.shape[0] for g in parts)
    total = -(-have // 512) * 512
    if total > have:
        parts.append(jnp.zeros((total - have, 128), bf16))
    return jnp.concatenate(parts, axis=0).reshape((2,) * 5 + (total // 32, 128))


def local_own(
    tokens,
    cotangent,
    doc_lengths,
    adapter_ids,
    w_query,
    w_keyval,
    w_output,
    w_gateup,
    w_down,
    gain_attn,
    gain_mlp,
    query_a,
    query_b,
    keyval_a,
    keyval_b,
    output_a,
    output_b,
    gateup_a,
    gateup_b,
    down_a,
    down_b,
):
    count = lax.axis_size("ctx")
    device = lax.axis_index("ctx")
    local_rows = tokens.shape[0]
    width = local_rows // 2
    reach = (WINDOW + width - 1) // width
    key_width = w_keyval.shape[1]
    half_rows = jnp.arange(width, dtype=jnp.int32)
    own_blocks = (device, 2 * count - 1 - device)
    positions = jnp.concatenate(
        [own_blocks[0] * width + half_rows, own_blocks[1] * width + half_rows]
    )
    segment, mask = adapter_mask(doc_lengths, adapter_ids, positions)
    resid = tokens.astype(f32)
    key_blocks = [[block - reach + step for step in range(reach + 1)] for block in own_blocks]
    key_pos = jnp.stack(
        [jnp.concatenate([e * width + half_rows for e in blocks]) for blocks in key_blocks]
    )
    key_seg = segment_of(doc_lengths, key_pos.reshape(-1)).reshape(2, 1, -1)
    (
        result,
        grad_middle,
        act_one,
        query,
        keys,
        attention,
        inner_query,
        inner_keyval,
        inner_output,
        g_gateup_a,
        g_gateup_b,
        g_down_a,
        g_down_b,
        prob,
        full_query,
        full_keyval,
        full_output,
        unused_down,
        unused_gateup,
    ) = forward(
        count,
        (
            tokens,
            cotangent,
            mask,
            segment[:, None],
            key_seg,
            gain_attn[None, :],
            gain_mlp[None, :],
            query_a,
            query_b,
            keyval_a,
            keyval_b,
            output_a,
            output_b,
            gateup_a,
            gateup_b,
            down_a,
            down_b,
        ),
        (w_query, w_keyval, w_output, w_down, w_gateup),
    )
    full_query, full_keyval, full_output = (
        w.reshape(-1, w.shape[-1]) for w in (full_query, full_keyval, full_output)
    )
    grad_branch = grad_middle.astype(bf16)
    g_output_a, g_output_b, d_inner_output = adapter_back(
        grad_branch, attention, inner_output, output_b, mask
    )
    grad_attention = (by_cols(grad_branch, full_output) + by_cols(d_inner_output, output_a)).astype(
        bf16
    )
    grad_query, grad_keys = att_bwd(query, keys, attention, grad_attention, prob)
    grad_keys = grad_keys.transpose(0, 2, 1)
    first_device = device - reach
    slots = jnp.zeros((2 * reach + 1, local_rows, key_width), f32)
    for which in range(2):
        for step, entry in enumerate(key_blocks[which]):
            piece = grad_keys[which, step * width : (step + 1) * width]
            device_of, row_in = owner_of(entry, count, width)
            at = (device_of - first_device, row_in, jnp.int32(0))
            current = lax.dynamic_slice(slots, at, (1, width, key_width))
            slots = lax.dynamic_update_slice(slots, current + piece[None], at)
    grad_keyval_full = slots[reach]
    for offset in range(1, reach + 1):
        from_lower = shifted(slots[reach + offset].astype(bf16), "ctx", offset).astype(f32)
        from_upper = shifted(slots[reach - offset].astype(bf16), "ctx", -offset).astype(f32)
        grad_keyval_full = grad_keyval_full + from_lower + from_upper
    grad_keyval = grad_keyval_full.astype(bf16)
    g_query_a, g_query_b, d_inner_query = adapter_back(
        grad_query, act_one, inner_query, query_b, mask
    )
    g_keyval_a, g_keyval_b, d_inner_keyval = adapter_back(
        grad_keyval, act_one, inner_keyval, keyval_b, mask
    )
    grad_act_one = (
        by_cols(grad_query, full_query)
        + by_cols(grad_keyval, full_keyval)
        + by_cols(d_inner_query, query_a)
        + by_cols(d_inner_keyval, keyval_a)
    )
    unused, pull_one = jax.vjp(lambda values: rms_scale(values, gain_attn), resid)
    grad_tokens = (grad_middle + pull_one(grad_act_one)[0]).astype(bf16)
    parts = [
        g_query_a,
        tiles_out(g_query_b),
        g_keyval_a,
        tiles_out(g_keyval_b),
        g_output_a,
        tiles_out(g_output_b),
        g_gateup_a,
        g_gateup_b.reshape(-1, 128),
        g_down_a,
        g_down_b.reshape(-1, 128),
    ]
    summed = reduce_packed(pack(parts)).reshape(-1, 128)
    sums = []
    start = 0
    for at, part in enumerate(parts):
        rows = part.shape[0]
        piece = summed[start : start + rows].astype(f32)
        sums.append(tiles_in(piece, 128) if at % 2 else piece)
        start += rows
    return (result, grad_tokens, *sums)


def solution(mesh):
    in_specs = (
        P("ctx", None),
        P("ctx", None),
        P(),
        P(),
        P("ctx", None),
        P("ctx", None),
        P("ctx", None),
        P("ctx", None),
        P("ctx", None),
        P(),
        P(),
        P(),
        P(),
        P(),
        P(),
        P(),
        P(),
        P(),
        P(),
        P(),
        P(),
    )
    out_specs = (P("ctx", None), P("ctx", None), P(), P(), P(), P(), P(), P(), P(), P(), P(), P())
    local = local_own if mesh.shape["ctx"] == 32 else local_native
    return jax.shard_map(local, mesh=mesh, in_specs=in_specs, out_specs=out_specs, check_vma=False)
```

```python
import functools

import jax
import jax.numpy as jnp
from jax import lax
from jax.experimental import pallas as pl
from jax.experimental.pallas import tpu as pltpu
from jax.sharding import PartitionSpec as P

HEADS = 12
HD = 128
FF = 4608
WINDOW = 1024
RANK = 16
ADAPTERS = 8


NORM_EPS = 1e-06
MASKED = -1e30


MESH = pl.DeviceIdType.MESH
bf16 = jnp.bfloat16
f32 = jnp.float32
NN = (((1,), (0,)), ((), ()))
NT = (((1,), (1,)), ((), ()))
TN = (((0,), (0,)), ((), ()))
VMEM = pl.BlockSpec(memory_space=pltpu.VMEM)
HBM = pl.BlockSpec(memory_space=pl.ANY)
ORD_A = (4, 3, 1, 2, 0)
ORD_A2 = (4, 3, 2, 1, 0)
ORD_B = (4, 1, 2, 3, 0)
ORD_B2 = (4, 2, 1, 3, 0)
ORD_C = (4, 2, 3, 1, 0)
ORD_C2 = (4, 1, 3, 2, 0)


def shifted(x, axis, by):
    size = lax.axis_size(axis)
    pairs = [(i, i + by) for i in range(size) if 0 <= i + by < size]
    return lax.ppermute(x, axis, pairs)


def segment_of(doc_lengths, positions):
    starts = jnp.cumsum(doc_lengths) - doc_lengths
    return jnp.sum((starts[None, :] <= positions[:, None]).astype(jnp.int32), axis=1) - 1


def adapter_mask(doc_lengths, adapter_ids, positions):
    segment = segment_of(doc_lengths, positions)
    owner = segment[:, None] == jnp.arange(doc_lengths.shape[0], dtype=jnp.int32)[None, :]
    chosen = jnp.sum(jnp.where(owner, adapter_ids[None, :], 0), axis=1)
    columns = jnp.arange(ADAPTERS * RANK, dtype=jnp.int32) // RANK
    return (segment, (columns[None, :] == chosen[:, None]).astype(jnp.float32))


def rms_scale(values, gain):
    return values * lax.rsqrt(jnp.mean(values * values, axis=-1, keepdims=True) + NORM_EPS) * gain


def by_rows(left, right):
    return lax.dot_general(
        left, right, (((0,), (0,)), ((), ())), preferred_element_type=jnp.float32
    )


def by_cols(left, right):
    return lax.dot_general(
        left, right, (((1,), (1,)), ((), ())), preferred_element_type=jnp.float32
    )


def adapted(inputs, weight, down_part, up_part, mask):
    inner = (jnp.dot(inputs, down_part, preferred_element_type=jnp.float32) * mask).astype(
        jnp.bfloat16
    )
    return (
        jnp.dot(inputs, weight, preferred_element_type=jnp.float32)
        + jnp.dot(inner, up_part, preferred_element_type=jnp.float32),
        inner,
    )


def adapter_back(grad_out, inputs, inner, up_part, mask):
    grad_up = by_rows(inner, grad_out)
    grad_inner = (by_cols(grad_out, up_part) * mask).astype(jnp.bfloat16)
    return (by_rows(inputs, grad_inner), grad_up, grad_inner)


def owner_of(block, count, width):
    device_of = jnp.where(block < count, block, 2 * count - 1 - block)
    return (device_of, jnp.where(block < count, 0, width))


def key_block(table, first_device, block, count, width):
    device_of, row_in = owner_of(block, count, width)
    piece = lax.dynamic_slice(
        table, (device_of - first_device, row_in, jnp.int32(0)), (1, width, table.shape[2])
    )
    return piece[0]


def block_scores(query, keys, allowed):
    rows = query.shape[0]
    heads = query.reshape(rows, HEADS, HD)
    raw = jnp.einsum(
        "rhd,kd->rhk", heads, keys[:, :HD], preferred_element_type=jnp.float32
    ) * HD ** (-0.5)
    return jnp.where(allowed[:, None, :], raw, MASKED)


def attend_forward(query, keys, allowed):
    scores = block_scores(query, keys, allowed)
    top = jnp.max(scores, axis=-1, keepdims=True)
    total = jnp.sum(jnp.exp(scores - top), axis=-1, keepdims=True)
    log_total = top + jnp.log(total)
    weights = jnp.exp(scores - log_total).astype(jnp.bfloat16)
    mixed = jnp.einsum("rhk,kd->rhd", weights, keys[:, HD:], preferred_element_type=jnp.float32)
    return (mixed.reshape(query.shape[0], -1), log_total)


def attend_backward(query, keys, allowed, log_total, grad_out):
    rows = query.shape[0]
    prob = jnp.exp(block_scores(query, keys, allowed) - log_total)
    grad_heads = grad_out.reshape(rows, HEADS, HD)
    grad_prob = jnp.einsum(
        "rhd,kd->rhk", grad_heads, keys[:, HD:], preferred_element_type=jnp.float32
    )
    delta = jnp.sum(prob * grad_prob, axis=-1, keepdims=True)
    grad_scores = (prob * (grad_prob - delta)).astype(jnp.bfloat16)
    scale = HD ** (-0.5)
    grad_query = (
        jnp.einsum("rhk,kd->rhd", grad_scores, keys[:, :HD], preferred_element_type=jnp.float32)
        * scale
    )
    grad_key = (
        jnp.einsum(
            "rhk,rhd->kd",
            grad_scores,
            query.reshape(rows, HEADS, HD),
            preferred_element_type=jnp.float32,
        )
        * scale
    )
    grad_value = jnp.einsum(
        "rhk,rhd->kd", prob.astype(jnp.bfloat16), grad_heads, preferred_element_type=jnp.float32
    )
    return (grad_query.reshape(rows, -1), jnp.concatenate([grad_key, grad_value], axis=1))


def local_native(
    tokens,
    cotangent,
    doc_lengths,
    adapter_ids,
    w_query,
    w_keyval,
    w_output,
    w_gateup,
    w_down,
    gain_attn,
    gain_mlp,
    query_a,
    query_b,
    keyval_a,
    keyval_b,
    output_a,
    output_b,
    gateup_a,
    gateup_b,
    down_a,
    down_b,
):
    count = lax.axis_size("ctx")
    device = lax.axis_index("ctx")
    local_rows = tokens.shape[0]
    width = local_rows // 2
    reach = (WINDOW + width - 1) // width
    key_width = w_keyval.shape[1]
    half_rows = jnp.arange(width, dtype=jnp.int32)
    own_blocks = (device, 2 * count - 1 - device)
    positions = jnp.concatenate(
        [own_blocks[0] * width + half_rows, own_blocks[1] * width + half_rows]
    )
    segment, mask = adapter_mask(doc_lengths, adapter_ids, positions)
    resid = tokens.astype(jnp.float32)
    act_one = rms_scale(resid, gain_attn).astype(jnp.bfloat16)
    full_query, full_keyval, full_output, full_gateup = (
        lax.all_gather(w_query, "ctx", axis=0, tiled=True),
        lax.all_gather(w_keyval, "ctx", axis=0, tiled=True),
        lax.all_gather(w_output, "ctx", axis=0, tiled=True),
        lax.all_gather(w_gateup, "ctx", axis=0, tiled=True),
    )
    query_full, inner_query = adapted(act_one, full_query, query_a, query_b, mask)
    keyval_full, inner_keyval = adapted(act_one, full_keyval, keyval_a, keyval_b, mask)
    query = query_full.astype(jnp.bfloat16)
    keyval = keyval_full.astype(jnp.bfloat16)
    stacked = [keyval]
    for offset in range(1, reach + 1):
        later = shifted(keyval, "ctx", -offset)
        prior = shifted(keyval, "ctx", offset)
        stacked = [prior] + stacked + [later]
    table = jnp.stack(stacked)
    first_device = device - reach
    kept = []
    mixed_parts = []
    for which in range(2):
        block = own_blocks[which]
        key_blocks = [block - reach + step for step in range(reach + 1)]
        keys = jnp.concatenate(
            [key_block(table, first_device, entry, count, width) for entry in key_blocks], axis=0
        )
        key_pos = jnp.concatenate([entry * width + half_rows for entry in key_blocks])
        key_seg = segment_of(doc_lengths, key_pos)
        query_pos = positions[which * width : (which + 1) * width]
        query_seg = segment[which * width : (which + 1) * width]
        allowed = (
            (key_pos[None, :] <= query_pos[:, None])
            & (query_pos[:, None] - key_pos[None, :] < WINDOW)
            & (key_seg[None, :] == query_seg[:, None])
        )
        mixed, log_total = attend_forward(query[which * width : (which + 1) * width], keys, allowed)
        kept.append((key_blocks, keys, allowed, log_total))
        mixed_parts.append(mixed)
    attention = jnp.concatenate(mixed_parts, axis=0).astype(jnp.bfloat16)
    branch_one, inner_output = adapted(attention, full_output, output_a, output_b, mask)
    middle = resid + branch_one
    act_two = rms_scale(middle, gain_mlp).astype(jnp.bfloat16)
    gate_up, inner_gateup = adapted(act_two, full_gateup, gateup_a, gateup_b, mask)
    gate = gate_up[:, :FF]
    upper = gate_up[:, FF:]
    hidden = (jax.nn.gelu(gate) * upper).astype(jnp.bfloat16)
    down_main = jnp.dot(
        hidden,
        lax.all_gather(w_down, "ctx", axis=0, tiled=True),
        preferred_element_type=jnp.float32,
    )
    inner_down = (jnp.dot(hidden, down_a, preferred_element_type=jnp.float32) * mask).astype(
        jnp.bfloat16
    )
    result = middle + (down_main + jnp.dot(inner_down, down_b, preferred_element_type=jnp.float32))
    grad_down_a, grad_down_b, d_inner_down = adapter_back(
        cotangent, hidden, inner_down, down_b, mask
    )
    grad_hidden = by_cols(cotangent, lax.all_gather(w_down, "ctx", axis=0, tiled=True)) + by_cols(
        d_inner_down, down_a
    )

    def gated(gate_part, up_part):
        return jax.nn.gelu(gate_part) * up_part

    unused, pull_glu = jax.vjp(gated, gate, upper)
    grad_gate, grad_up = pull_glu(grad_hidden)
    grad_gateup = jnp.concatenate([grad_gate, grad_up], axis=1).astype(jnp.bfloat16)
    grad_gateup_a, grad_gateup_b, d_inner_gateup = adapter_back(
        grad_gateup, act_two, inner_gateup, gateup_b, mask
    )
    grad_act_two = by_cols(grad_gateup, full_gateup) + by_cols(d_inner_gateup, gateup_a)
    unused, pull_two = jax.vjp(lambda values: rms_scale(values, gain_mlp), middle)
    grad_middle = cotangent.astype(jnp.float32) + pull_two(grad_act_two)[0]
    grad_branch = grad_middle.astype(jnp.bfloat16)
    grad_output_a, grad_output_b, d_inner_output = adapter_back(
        grad_branch, attention, inner_output, output_b, mask
    )
    grad_attention = (by_cols(grad_branch, full_output) + by_cols(d_inner_output, output_a)).astype(
        jnp.bfloat16
    )
    query_grads = []
    key_grads = []
    for which in range(2):
        key_blocks, keys, allowed, log_total = kept[which]
        rows_query = query[which * width : (which + 1) * width]
        rows_grad = grad_attention[which * width : (which + 1) * width]
        grad_rows, grad_keys = attend_backward(rows_query, keys, allowed, log_total, rows_grad)
        query_grads.append(grad_rows)
        for step, entry in enumerate(key_blocks):
            key_grads.append((entry, grad_keys[step * width : (step + 1) * width]))
    grad_query = jnp.concatenate(query_grads, axis=0).astype(jnp.bfloat16)
    slots = jnp.zeros((2 * reach + 1, local_rows, key_width), jnp.float32)
    for entry, piece in key_grads:
        device_of, row_in = owner_of(entry, count, width)
        slot = device_of - first_device
        current = lax.dynamic_slice(slots, (slot, row_in, jnp.int32(0)), (1, width, key_width))
        slots = lax.dynamic_update_slice(slots, current + piece[None], (slot, row_in, jnp.int32(0)))
    grad_keyval_full = slots[reach]
    for offset in range(1, reach + 1):
        from_lower = shifted(slots[reach + offset].astype(jnp.bfloat16), "ctx", offset).astype(
            jnp.float32
        )
        from_upper = shifted(slots[reach - offset].astype(jnp.bfloat16), "ctx", -offset).astype(
            jnp.float32
        )
        grad_keyval_full = grad_keyval_full + from_lower + from_upper
    grad_keyval = grad_keyval_full.astype(jnp.bfloat16)
    grad_query_a, grad_query_b, d_inner_query = adapter_back(
        grad_query, act_one, inner_query, query_b, mask
    )
    grad_keyval_a, grad_keyval_b, d_inner_keyval = adapter_back(
        grad_keyval, act_one, inner_keyval, keyval_b, mask
    )
    grad_act_one = (
        by_cols(grad_query, full_query)
        + by_cols(grad_keyval, full_keyval)
        + by_cols(d_inner_query, query_a)
        + by_cols(d_inner_keyval, keyval_a)
    )
    unused, pull_one = jax.vjp(lambda values: rms_scale(values, gain_attn), resid)
    grad_tokens = (grad_middle + pull_one(grad_act_one)[0]).astype(jnp.bfloat16)
    sums = lax.psum(
        (
            grad_query_a,
            grad_query_b,
            grad_keyval_a,
            grad_keyval_b,
            grad_output_a,
            grad_output_b,
            grad_gateup_a,
            grad_gateup_b,
            grad_down_a,
            grad_down_b,
        ),
        "ctx",
    )
    return (
        result.astype(jnp.bfloat16),
        grad_tokens,
        sums[0],
        sums[1],
        sums[2],
        sums[3],
        sums[4],
        sums[5],
        sums[6],
        sums[7],
        sums[8],
        sums[9],
    )


def flip(me, bits, b):
    return (me+(1-2*bits[b])*(1<<b),)
CHUNK = 512
UNIT = 256
SUB = 128
GROUP = 4
SCALE = HD ** (-0.5)
LAGS = (0, 1, 2, 4, 6)
SOFT_UNROLL = 8
AHEAD = 24


def dot(a, b, dims=NN):
    return lax.dot_general(a, b, dims, preferred_element_type=f32)


def tile_at(i, size):
    return pl.ds(i * size if isinstance(i, int) else pl.multiple_of(i * size, size), size)


def even_odd(par, low, high):
    if par % 2:
        return ((low, 2, ORD_A2), (high, 1, ORD_C2), (high + 1, 1, ORD_B2))
    return ((low, 2, ORD_A), (high, 1, ORD_C), (high + 1, 1, ORD_B))


def bits_of(me):
    return [(me // (1 << b)) % 2 for b in range(5)]


def meet_all(count, me):
    barrier = pltpu.get_barrier_semaphore()

    def greet(k, unused):
        pl.semaphore_signal(
            barrier, 1, device_id=(lax.rem(me + k, count),), device_id_type=MESH
        )
        return unused

    lax.fori_loop(1, count, greet, 0)
    pl.semaphore_wait(barrier, count - 1)


def heads_down(x):
    return jnp.concatenate([x[:, i * HD : (i + 1) * HD] for i in range(x.shape[1] // HD)], axis=0)


def heads_across(x):
    return jnp.concatenate([x[i * SUB : (i + 1) * SUB] for i in range(x.shape[0] // SUB)], axis=1)


def norm_rows(read, gain_ref, write, rows):
    def block(r, unused):
        at = tile_at(r, 16)
        x = read(at)
        scale = lax.rsqrt(jnp.mean(x * x, axis=1, keepdims=True) + NORM_EPS)
        write(at, (x * scale * gain_ref[...]).astype(bf16))
        return unused

    lax.fori_loop(0, rows // 16, block, 0, unroll=8)


def forward_kernel(
    count,
    x_ref,
    g_ref,
    mask_ref,
    qseg_ref,
    kseg_ref,
    gain1_ref,
    gain2_ref,
    qa_ref,
    qb_ref,
    ka_ref,
    kb_ref,
    oa_ref,
    ob_ref,
    ga_ref,
    gb_ref,
    da_ref,
    db_ref,
    wq_own,
    wk_own,
    wo_own,
    wd_own,
    wg_own,
    out_ref,
    dmid_ref,
    a1_ref,
    q_ref,
    keys_ref,
    att_ref,
    iq_ref,
    ik_ref,
    io_ref,
    gga_ref,
    ggb_ref,
    gda_ref,
    gdb_ref,
    prob_hbm,
    wq_all,
    wk_all,
    wo_all,
    wd_all,
    wg_all,
    held_q,
    held_k,
    held_o,
    held_d,
    held_g,
    wbuf,
    dbuf,
    pbuf,
    kv_own,
    a2_s,
    igu_s,
    did_s,
    acc_o,
    acc_a,
    gu_s,
    dh_s,
    hid_s,
    dgu_s,
    wsem,
    dsem,
    psem,
    own_sem,
    xsend,
    xrecv,
    hsend,
    hrecv,
):
    rows, d = x_ref.shape
    width = rows // 2
    reach = WINDOW // width
    keys = keys_ref.shape[1]
    span = keys - width + SUB
    ff = da_ref.shape[0]
    nu, nc = ff // UNIT, ff // CHUNK
    me = lax.axis_index("ctx")
    bits = bits_of(me)
    meet_all(count, me)
    here = (bits[4], bits[3], bits[2], bits[1], bits[0])
    own = (wq_own, wk_own, wo_own, wd_own, wg_own)
    held = (held_q, held_k, held_o, held_d, held_g)
    full = (wq_all, wk_all, wo_all, wd_all, wg_all)

    def where(bit_set):
        return tuple(pl.ds(0, 2) if b in bit_set else bits[b] for b in (4, 3, 2, 1, 0))

    def remote(src, dst, send, recv, bit):
        return pltpu.make_async_remote_copy(
            src, dst, send, recv, device_id=flip(me, bits, bit), device_id_type=MESH
        )

    units = []
    for u in range(3):
        units.append((0, 0, even_odd(u, 4 * u, 4 * u + 2)))
    units.append((1, 0, ((0, 1, ORD_A), (1, 1, ORD_C2))))
    for u in range(3):
        units.append((2, 0, even_odd(u, 4 * u, 4 * u + 2)))
    thick = wd_own.shape[0] // 3
    for u in range(9):
        units.append((3, u // 3 * thick, even_odd(u + 1, u % 3 * 4, u % 3 * 4 + 2)))
    first = len(units)

    def exchange(u, cl, k):
        w, row, split = units[u]
        tile, tiles, order = split[cl]
        lines = pl.ds(row, wq_own.shape[0])
        cols = pl.ds(tile * 128, tiles * 128)
        there = full[w].at[where(order[:k]) + (lines, cols)]
        return remote(
            there if k else own[w].at[lines, cols],
            there,
            xsend.at[u, cl, k],
            xrecv.at[u, cl, k],
            order[k],
        )

    def gate(v, par, cl, k):
        tile, tiles, order = even_odd(par, 0, ff // 128)[cl]
        at = tile * 128 + v * UNIT
        cols = pl.ds(at if isinstance(at, int) else pl.multiple_of(at, 128), tiles * 128)
        there = wg_all.at[where(order[:k]) + (slice(None), cols)]
        return remote(
            there if k else wg_own.at[:, cols],
            there,
            xsend.at[first + v, cl, k],
            xrecv.at[first + v, cl, k],
            order[k],
        )

    staged = [pltpu.make_async_copy(own[w], held[w], own_sem.at[w]) for w in range(5)]
    placed = [pltpu.make_async_copy(held[w], full[w].at[here], own_sem.at[w]) for w in range(5)]
    for copy in staged:
        copy.start()
    state = {"step": 0, "placed": set()}

    def place(w):
        if w not in state["placed"]:
            state["placed"].add(w)
            placed[w].wait()

    def steps(n):
        while state["step"] < n:
            t = state["step"]
            state["step"] += 1
            for k in (4, 3, 2, 1, 0):
                u = t - LAGS[k]
                if not 0 <= u < first + nu:
                    continue
                w = units[u][0] if u < first else 4
                if k:
                    place(w)
                for cl in range(2 if w == 1 else 3):
                    at = (
                        functools.partial(exchange, u, cl)
                        if u < first
                        else functools.partial(gate, u - first, (u - first) % 2, cl)
                    )
                    if k:
                        at(k - 1).wait_recv()
                    at(k).start()

    def loop_steps(c, point):
        for i in (2 * point, 2 * point + 1):
            t, k = i // 5, 4 - i % 5
            v = 2 * c + t + AHEAD - first - LAGS[k]
            par = (t + AHEAD - first - LAGS[k]) % 2

            @pl.when(v < nu)
            def _(v=v, par=par, k=k):
                for cl in range(3):
                    if k:
                        gate(v, par, cl, k - 1).wait_recv()
                    gate(v, par, cl, k).start()

    def arrived(weight_at):
        for u, unit in enumerate(units):
            if unit[0] == weight_at:
                for cl in range(len(unit[2])):
                    exchange(u, cl, 4).wait_recv()

    def load(w, lo, n, slot, at, sem):
        return pltpu.make_async_copy(
            full[w].at[(slice(None),) * 6 + (pl.ds(lo, n),)],
            wbuf.at[(slot,) + (slice(None),) * 6 + (pl.ds(at, n),)],
            wsem.at[slot, sem],
        )

    def weight(slot, lo, n):
        return wbuf[slot, :, :, :, :, :, :, lo : lo + n].reshape(-1, n)

    for w in range(5):
        staged[w].wait()
        placed[w].start()
    steps(4)
    def read_x(at):
        return x_ref[at, :].astype(f32)

    def write_a1(at, y):
        a1_ref[at, :] = y

    norm_rows(read_x, gain1_ref, write_a1, rows)
    iq_ref[...] = (dot(a1_ref[...], qa_ref[...]) * mask_ref[...]).astype(bf16)
    ik_ref[...] = (dot(a1_ref[...], ka_ref[...]) * mask_ref[...]).astype(bf16)
    did_s[...] = (dot(g_ref[...], db_ref[...], NT) * mask_ref[...]).astype(bf16)
    steps(10)
    arrived(0)
    arrived(1)
    loads = [load(0, 0, 1024, 0, 0, 0), load(0, 1024, d - 1024, 1, 0, 0)]
    loads.append(load(1, 0, 2 * HD, 1, d - 1024, 1))
    for copy in loads:
        copy.start()
    for copy in loads:
        copy.wait()

    def beside(a, b):
        return jnp.concatenate([a, b], axis=1)

    def under(a, b):
        return jnp.concatenate([a, b], axis=0)

    kv_own[...] = dot(
        beside(a1_ref[...], ik_ref[...]), under(weight(1, d - 1024, 2 * HD), kb_ref[...])
    ).astype(bf16)
    keys_ref[0, pl.ds(reach * width, width)] = kv_own[pl.ds(0, width)]
    keys_ref[1, pl.ds(reach * width, width)] = kv_own[pl.ds(width, width)]

    def low(j):
        block = me + j
        upper = block // count
        target = block + upper * (2 * count - 1 - 2 * block)
        copy = pltpu.make_async_remote_copy(
            kv_own.at[pl.ds(0, width)],
            keys_ref.at[upper, pl.ds((reach - j) * width, width)],
            hsend.at[0, j],
            hrecv.at[upper, j],
            device_id=(target,),
            device_id_type=MESH,
        )
        return copy, target

    def high(j):
        return pltpu.make_async_remote_copy(
            kv_own.at[pl.ds(width, width)],
            keys_ref.at[1, pl.ds((reach - j) * width, width)],
            hsend.at[1, j],
            hrecv.at[1, j],
            device_id=(me - j,),
            device_id_type=MESH,
        )

    def incoming(which, j):
        return pltpu.make_async_remote_copy(
            kv_own.at[pl.ds(0, width)],
            keys_ref.at[which, pl.ds((reach - j) * width, width)],
            hsend.at[0, j],
            hrecv.at[which, j],
            device_id=flip(me, bits, 0),
            device_id_type=MESH,
        )

    for j in range(1, reach + 1):
        copy, target = low(j)
        pl.when(target != me)(copy.start)
        pl.when(me >= j)(high(j).start)

        @pl.when(target == me)
        def _(j=j):
            keys_ref[1, pl.ds((reach - j) * width, width)] = kv_own[pl.ds(0, width)]

        @pl.when(me < j)
        def _(j=j):
            keys_ref[0, pl.ds((reach - j) * width, width)] = jnp.zeros((width, 2 * HD), bf16)

    steps(11)
    q_ref[:, :1024] = dot(
        beside(a1_ref[...], iq_ref[...]), under(weight(0, 0, 1024), qb_ref[:, :1024])
    ).astype(bf16)
    q_ref[:, 1024:] = dot(
        beside(a1_ref[...], iq_ref[...]), under(weight(1, 0, d - 1024), qb_ref[:, 1024:])
    ).astype(bf16)
    for j in range(1, reach + 1):
        pl.when(me >= j)(incoming(0, j).wait_recv)
        pl.when(2 * me != 2 * count - 1 - j)(incoming(1, j).wait_recv)
    steps(12)

    groups = HEADS // GROUP
    subs = width // SUB
    turn = 0
    for which in range(2):
        for s in range(subs):
            base = s * SUB
            lines = slice(which * width + base, which * width + base + SUB)
            row = lax.broadcasted_iota(jnp.int32, (SUB, span), 0)
            col = lax.broadcasted_iota(jnp.int32, (SUB, span), 1)
            ok = (
                (col <= row + (span - SUB))
                & (col > row + (span - SUB - WINDOW))
                & (kseg_ref[which, :, base : base + span] == qseg_ref[lines, :])
            )
            acc_a[:SUB, :span] = jnp.where(ok, 0.0, MASKED)

            for g in range(groups):
                heads = slice(g * GROUP * HD, (g + 1) * GROUP * HD)
                k = keys_ref[which, base : base + span, :HD]
                v = keys_ref[which, base : base + span, HD:]
                acc_o[: GROUP * SUB, :span] = dot(heads_down(q_ref[lines, heads]), k, NT)
                slot = turn % 2
                if turn >= 2:
                    pltpu.make_async_copy(
                        pbuf.at[slot], prob_hbm.at[0, 0, pl.ds(0, GROUP * SUB)], psem.at[slot]
                    ).wait()

                def soft(r, unused, slot=slot):
                    at = tile_at(r, 16)
                    bias = acc_a[tile_at(r % (SUB // 16), 16), :span]
                    sc = acc_o[at, :span] * SCALE + bias
                    e = jnp.exp(sc - jnp.max(sc, axis=1, keepdims=True))
                    inv = 1.0 / jnp.sum(e, axis=1, keepdims=True)
                    pbuf[slot, at, :] = (e * inv).astype(bf16)
                    return unused

                lax.fori_loop(0, GROUP * SUB // 16, soft, 0, unroll=SOFT_UNROLL)
                pltpu.make_async_copy(
                    pbuf.at[slot],
                    prob_hbm.at[which, s, pl.ds(g * GROUP * SUB, GROUP * SUB)],
                    psem.at[slot],
                ).start()
                att_ref[lines, heads] = heads_across(dot(pbuf[slot], v)).astype(bf16)
                turn += 1
            steps(13 + which * subs + s)
    for slot in range(2):
        pltpu.make_async_copy(
            pbuf.at[slot], prob_hbm.at[0, 0, pl.ds(0, GROUP * SUB)], psem.at[slot]
        ).wait()
    arrived(2)
    loads = [load(2, 0, 1024, 0, 0, 0), load(2, 1024, d - 1024, 1, 0, 0)]
    for copy in loads:
        copy.start()
    io_ref[...] = (dot(att_ref[...], oa_ref[...]) * mask_ref[...]).astype(bf16)
    for copy in loads:
        copy.wait()
    dmid_ref[:, :1024] = x_ref[:, :1024].astype(f32) + dot(
        beside(att_ref[...], io_ref[...]), under(weight(0, 0, 1024), ob_ref[:, :1024])
    )
    dmid_ref[:, 1024:] = x_ref[:, 1024:].astype(f32) + dot(
        beside(att_ref[...], io_ref[...]), under(weight(1, 0, d - 1024), ob_ref[:, 1024:])
    )
    steps(17)

    def read_mid(at):
        return dmid_ref[at, :]

    def write_a2(at, y):
        a2_s[at, :] = y

    norm_rows(read_mid, gain2_ref, write_a2, rows)
    igu_s[...] = (dot(a2_s[...], ga_ref[...]) * mask_ref[...]).astype(bf16)
    acc_o[...] = jnp.zeros_like(acc_o)
    acc_a[...] = jnp.zeros_like(acc_a)
    steps(AHEAD)
    arrived(3)

    def arrived_gate(c):
        for j in range(CHUNK // UNIT):
            for cl in range(3):
                gate(c * (CHUNK // UNIT) + j, j % 2, cl, 4).wait_recv()

    def down_rows(c):
        return wd_rows.at[tile_at(c, CHUNK)]

    wd_rows = wd_all.reshape(ff, d)

    def fetch(c, slot):
        cps = [
            pltpu.make_async_copy(
                wg_all.at[(slice(None),) * 6 + (tile_at_base(base, c),)],
                wbuf.at[(slot,) + (slice(None),) * 6 + (pl.ds(o, CHUNK),)],
                wsem.at[slot, i],
            )
            for i, (base, o) in enumerate(((0, 0), (ff, CHUNK)))
        ]
        cps.append(pltpu.make_async_copy(down_rows(c), dbuf.at[slot], dsem.at[slot]))
        return cps

    def tile_at_base(base, c):
        at = base + c * CHUNK
        return pl.ds(at if isinstance(at, int) else pl.multiple_of(at, 128), CHUNK)

    arrived_gate(0)
    for copy in fetch(0, 0):
        copy.start()
    for copy in fetch(0, 0):
        copy.wait()

    def chunk(c, unused):
        slot = c % 2
        loop_steps(c, 0)
        gbc = beside(gb_ref[:, tile_at_base(0, c)], gb_ref[:, tile_at_base(ff, c)])
        dac = da_ref[tile_at(c, CHUNK), :]

        def wx():
            return under(weight(slot, 0, 2 * CHUNK), gbc)

        def wdx():
            return beside(dbuf[slot], dac)

        gu_s[...] = dot(beside(a2_s[...], igu_s[...]), wx())
        loop_steps(c, 1)
        dh_s[...] = dot(beside(g_ref[...], did_s[...]), wdx(), NT)
        k0 = 0.7978845608028654

        def glu(r, unused):
            at = tile_at(r, 16)
            gate_v, up, dh = gu_s[at, :CHUNK], gu_s[at, CHUNK:], dh_s[at, :]
            sq = gate_v * gate_v
            th = jnp.tanh(gate_v * (k0 + (k0 * 0.044715) * sq))
            ht = 0.5 + 0.5 * th
            gl = gate_v * ht
            dgl = ht + (gate_v * (0.5 - 0.5 * th * th)) * (k0 + (3 * k0 * 0.044715) * sq)
            hid_s[at, :] = (gl * up).astype(bf16)
            dgu_s[at, :CHUNK] = (dh * up * dgl).astype(bf16)
            dgu_s[at, CHUNK:] = (dh * gl).astype(bf16)
            return unused

        loop_steps(c, 2)
        lax.fori_loop(0, rows // 16, glu, 0)
        loop_steps(c, 3)
        acc_o[...] += dot(hid_s[...], wdx())
        loop_steps(c, 4)
        gda_ref[tile_at(c, CHUNK), :] = dot(hid_s[...], did_s[...], TN).astype(bf16)
        r = dot(igu_s[...], dgu_s[...], TN).astype(bf16)
        for i in range(2):
            for j in range(CHUNK // 128):
                lo = i * CHUNK + j * 128
                ggb_ref[pl.ds(c * (CHUNK // 128) + (ff // 128) * i + j, 1)] = r[
                    None, :, lo : lo + 128
                ]

        @pl.when(c + 1 < nc)
        def _():
            arrived_gate(c + 1)
            for copy in fetch(c + 1, 1 - slot):
                copy.start()

        acc_a[...] += dot(dgu_s[...], wx(), NT)

        @pl.when(c + 1 < nc)
        def _():
            for copy in fetch(c + 1, 1 - slot):
                copy.wait()

        return unused

    lax.fori_loop(0, nc, chunk, 0)
    inner_d = (acc_o[:, d:] * mask_ref[...]).astype(bf16)
    acc_o[:, :d] += dot(inner_d, db_ref[...])
    r = dot(inner_d, g_ref[...], TN).astype(bf16)
    for j in range(d // 128):
        gdb_ref[j] = r[:, j * 128 : (j + 1) * 128]
    dgu = (acc_a[:, d:] * mask_ref[...]).astype(bf16)
    gga_ref[...] = dot(a2_s[...], dgu, TN).astype(bf16)
    acc_a[:, :d] += dot(dgu, ga_ref[...], NT)

    def finish(r, unused):
        at = tile_at(r, 16)
        mid = dmid_ref[at, :]
        out_ref[at, :] = (mid + acc_o[at, :d]).astype(bf16)
        e = acc_a[at, :d] * gain2_ref[...]
        rr = lax.rsqrt(jnp.mean(mid * mid, axis=1, keepdims=True) + NORM_EPS)
        pull = (rr * rr * rr) * jnp.mean(e * mid, axis=1, keepdims=True)
        dmid_ref[at, :] = g_ref[at, :].astype(f32) + rr * e - pull * mid
        return unused

    lax.fori_loop(0, rows // 16, finish, 0, unroll=8)
    for j in range(1, reach + 1):
        copy, target = low(j)
        pl.when(target != me)(copy.wait_send)
        pl.when(me >= j)(high(j).wait_send)
    for u, unit in enumerate(units):
        for cl in range(len(unit[2])):
            for k in range(5):
                exchange(u, cl, k).wait_send()

    def sent(v, unused):
        for par in range(2):
            for cl in range(3):
                for k in range(5):
                    gate(2 * v + par, par, cl, k).wait_send()
        return unused

    lax.fori_loop(0, nu // 2, sent, 0)


def forward(count, small, weights):
    x, g = small[0], small[1]
    rows, d = x.shape
    ff = weights[3].shape[0] * count
    width = rows // 2
    keys = WINDOW + width
    span = keys - width + SUB
    nu = ff // UNIT
    S = jax.ShapeDtypeStruct
    full = [S((2,) * 5 + w.shape, bf16) for w in weights]
    outs = [
        S((rows, d), bf16),
        S((rows, d), f32),
        S((rows, d), bf16),
        S((rows, d), bf16),
        S((2, keys, 2 * HD), bf16),
        S((rows, d), bf16),
        S((rows, 128), bf16),
        S((rows, 128), bf16),
        S((rows, 128), bf16),
        S((d, 128), bf16),
        S((2 * ff // 128, 128, 128), bf16),
        S((ff, 128), bf16),
        S((d // 128, 128, 128), bf16),
    ]
    DMA = pltpu.SemaphoreType.DMA
    return pl.pallas_call(
        functools.partial(forward_kernel, count),
        in_specs=[VMEM] * len(small) + [HBM] * 5,
        out_specs=[VMEM] * len(outs) + [HBM] * 6,
        out_shape=outs + [S((2, width // SUB, HEADS * SUB, span), bf16)] + full,
        scratch_shapes=[pltpu.VMEM(w.shape, bf16) for w in weights]
        + [
            pltpu.VMEM((2,) * 6 + (weights[0].shape[0], 2 * CHUNK), bf16),
            pltpu.VMEM((2, CHUNK, d), bf16),
            pltpu.VMEM((2, GROUP * SUB, span), bf16),
            pltpu.VMEM((rows, 2 * HD), bf16),
            pltpu.VMEM((rows, d), bf16),
            pltpu.VMEM((rows, 128), bf16),
            pltpu.VMEM((rows, 128), bf16),
            pltpu.VMEM((rows, d + 128), f32),
            pltpu.VMEM((rows, d + 128), f32),
            pltpu.VMEM((rows, 2 * CHUNK), f32),
            pltpu.VMEM((rows, CHUNK), f32),
            pltpu.VMEM((rows, CHUNK), bf16),
            pltpu.VMEM((rows, 2 * CHUNK), bf16),
            DMA((2, 2)),
            DMA((2,)),
            DMA((2,)),
            DMA((5,)),
            DMA((16 + nu, 3, 5)),
            DMA((16 + nu, 3, 5)),
            DMA((2, 5)),
            DMA((2, 5)),
        ],
        compiler_params=pltpu.CompilerParams(
            collective_id=0, has_side_effects=True, vmem_limit_bytes=63 << 20
        ),
        name="forward",
    )(*small, *weights)


class Sum:
    def __init__(self, me, buf, parts, send, recv):
        self.me, self.bits = me, bits_of(me)
        self.buf, self.parts, self.send, self.recv = buf, parts, send, recv
        tiles = buf.shape[5] // 16
        a, b = round(tiles * 3 / 7), round(tiles * 3 / 14)
        self.split = (
            (0, a * 16, ORD_A),
            (a * 16, b * 16, ORD_B),
            ((a + b) * 16, (tiles - a - b) * 16, ORD_C),
        )
        self.queue = [(s, cl) for s in range(1, 11) for cl in range(3)]

    def copy(self, cl, s):
        row, n, order = self.split[cl]
        lines = pl.ds(row, n)
        bits = self.bits
        if s < 5:
            red = order[::-1]
            bit = red[s]
            rem = [b for b in (4, 3, 2, 1, 0) if b not in red[:s]]
            src = self.buf if s == 0 else self.parts[s - 1]
            idx = tuple((1 - bits[b]) if b == bit else pl.ds(0, 2) for b in rem)
            src = src.at[idx + (lines,)]
            dst = self.parts[s].at[(pl.ds(0, 2),) * (4 - s) + (lines,)]
        else:
            bit, have = order[s - 5], order[: s - 5]
            idx = tuple(pl.ds(0, 2) if b in have else bits[b] for b in (4, 3, 2, 1, 0))
            src = dst = self.buf.at[idx + (lines,)]
        return pltpu.make_async_remote_copy(
            src,
            dst,
            self.send.at[cl, s],
            self.recv.at[cl, s],
            device_id=flip(self.me, bits, bit),
            device_id_type=MESH,
        )

    def add(self, cl, s):
        row, n, order = self.split[cl]
        red = order[::-1]
        rem = [b for b in (4, 3, 2, 1, 0) if b not in red[:s]]
        src, dst = (self.buf if s == 0 else self.parts[s - 1]), self.parts[s]
        lines = pl.ds(row, n)
        free = 4 - s

        def one(j, unused):
            at = [(j // (1 << (free - 1 - i))) % 2 for i in range(free)]
            rest = iter(at)
            idx = tuple(self.bits[b] if b == red[s] else next(rest) for b in rem)
            total = src[idx + (lines,)].astype(f32) + dst[tuple(at) + (lines,)].astype(f32)
            dst[tuple(at) + (lines,)] = total.astype(bf16)
            return unused

        lax.fori_loop(0, 1 << free, one, 0)

    def begin(self):
        for cl in range(3):
            self.copy(cl, 0).start()

    def advance(self, n=1):
        for unused in range(n):
            if not self.queue:
                return
            s, cl = self.queue.pop(0)
            before = self.copy(cl, s - 1)
            before.wait_recv()
            before.wait_send()
            if s <= 5:
                self.add(cl, s - 1)
            if s == 5:
                row, n_, unused_order = self.split[cl]
                b = self.bits
                self.buf[b[4], b[3], b[2], b[1], b[0], pl.ds(row, n_)] = self.parts[4][
                    pl.ds(row, n_)
                ]
            if s < 10:
                self.copy(cl, s).start()


def backward_kernel(
    count,
    dmid_ref,
    x_ref,
    mask_ref,
    gain_ref,
    a1_ref,
    q_ref,
    keys_ref,
    att_ref,
    iq_ref,
    ik_ref,
    io_ref,
    qa_ref,
    qb_ref,
    ka_ref,
    kb_ref,
    oa_ref,
    ob_ref,
    gga_hbm,
    ggb_hbm,
    gda_hbm,
    gdb_hbm,
    prob_hbm,
    wq_all,
    wk_all,
    wo_all,
    dx_ref,
    oqa_ref,
    oqb_ref,
    oka_ref,
    okb_ref,
    ooa_ref,
    oob_ref,
    oga_ref,
    ogb_ref,
    oda_ref,
    odb_ref,
    one,
    two,
    pa0,
    pa1,
    pa2,
    pa3,
    pa4,
    pb0,
    pb1,
    pb2,
    pb3,
    pb4,
    wbuf,
    pbuf,
    grad_s,
    small_s,
    dkv_s,
    acc,
    hout,
    hin,
    wsem,
    psem,
    gsem,
    send1,
    recv1,
    send2,
    recv2,
    hsend,
    hrecv,
):
    rows, d = x_ref.shape
    width = rows // 2
    reach = WINDOW // width
    keys = keys_ref.shape[1]
    span = keys - width + SUB
    me = lax.axis_index("ctx")
    bits = bits_of(me)
    meet_all(count, me)
    flat_one = one.reshape(-1, 128)
    flat_two = two.reshape(-1, 128)
    hid_rows = gda_hbm.shape[0]
    gates = ggb_hbm.shape[0] * 128
    at_ggb = d
    at_gda = at_ggb + gates
    at_gdb = at_gda + hid_rows
    at_goa = at_gdb + d
    at_gob = at_goa + d
    at_qb, at_ka, at_kb = d, 2 * d, 3 * d

    def whole(ref):
        return ref.at[(slice(None),) * 7]

    loads = [
        pltpu.make_async_copy(wo_all, wbuf.at[(slice(None),) * 6 + (pl.ds(0, d),)], wsem.at[0])
    ]
    grads = [
        pltpu.make_async_copy(src.reshape(-1, 128), flat_one.at[pl.ds(at, n)], gsem.at[i])
        for i, (src, at, n) in enumerate(
            (
                (gga_hbm, 0, d),
                (ggb_hbm, at_ggb, gates),
                (gda_hbm, at_gda, hid_rows),
                (gdb_hbm, at_gdb, d),
            )
        )
    ]
    groups = HEADS // GROUP
    subs = width // SUB
    turns = [(w, s, g) for w in range(2) for s in range(subs) for g in range(groups)]

    def prob(n):
        w, s, g = turns[n]
        return pltpu.make_async_copy(
            prob_hbm.at[w, s, pl.ds(g * GROUP * SUB, GROUP * SUB)], pbuf.at[n % 2], psem.at[n % 2]
        )

    for copy in loads + grads + [prob(0), prob(1)]:
        copy.start()

    def beside(*xs):
        return jnp.concatenate(xs, axis=1)

    def weight(lo, n):
        return wbuf[:, :, :, :, :, :, lo : lo + n].reshape(-1, n)

    def store_tiles(flat, at, x):
        for j in range(x.shape[1] // 128):
            flat[pl.ds(at + j * 128, 128)] = x[:, j * 128 : (j + 1) * 128].astype(bf16)

    grad_s[...] = dmid_ref[...].astype(bf16)
    small_s[:, :128] = (dot(grad_s[...], ob_ref[...], NT) * mask_ref[...]).astype(bf16)
    flat_one[pl.ds(at_goa, d)] = dot(att_ref[...], small_s[:, :128], TN).astype(bf16)
    store_tiles(flat_one, at_gob, dot(io_ref[...], grad_s[...], TN))
    for copy in grads:
        copy.wait()
    first = Sum(me, one, (pa0, pa1, pa2, pa3, pa4), send1, recv1)
    second = Sum(me, two, (pb0, pb1, pb2, pb3, pb4), send2, recv2)
    first.begin()
    for copy in loads:
        copy.wait()
    acc[:, :d] = dot(
        beside(grad_s[...], small_s[:, :128]), beside(weight(0, d), oa_ref[...]), NT
    )
    grad_s[...] = acc[:, :d].astype(bf16)
    loads = [
        pltpu.make_async_copy(wq_all, wbuf.at[(slice(None),) * 6 + (pl.ds(0, d),)], wsem.at[0]),
        pltpu.make_async_copy(
            wk_all, wbuf.at[(slice(None),) * 6 + (pl.ds(d, 2 * HD),)], wsem.at[1]
        ),
    ]
    for copy in loads:
        copy.start()
    dkv_s[...] = jnp.zeros_like(dkv_s)
    first.advance(1)

    for n, (which, s, g) in enumerate(turns):
        base = s * SUB
        lines = slice(which * width + base, which * width + base + SUB)
        heads = slice(g * GROUP * HD, (g + 1) * GROUP * HD)
        k = keys_ref[which, base : base + span, :HD]
        v = keys_ref[which, base : base + span, HD:]
        q = heads_down(q_ref[lines, heads])
        do = heads_down(grad_s[lines, heads])
        o = heads_down(att_ref[lines, heads])
        delta = jnp.sum(do.astype(f32) * o.astype(f32), axis=1, keepdims=True)
        prob(n).wait()
        p = pbuf[n % 2]
        ds = (p.astype(f32) * (dot(do, v, NT) - delta)).astype(bf16)
        dkv_s[which, HD:, base : base + span] += dot(do.T, p)
        dkv_s[which, :HD, base : base + span] += dot(q.T, ds) * SCALE
        grad_s[lines, heads] = heads_across(dot(ds, k) * SCALE).astype(bf16)
        if n + 2 < len(turns):
            prob(n + 2).start()
        first.advance(1)

    def piece(which, j):
        lo = (reach - j) * width
        return dkv_s[which, :, lo : lo + width].T

    for j in range(1, reach + 1):
        for which in range(2):
            hout[which, j - 1] = piece(which, j).astype(bf16)

    def low(j):
        return pltpu.make_async_remote_copy(
            hout.at[0, j - 1],
            hin.at[0, j - 1],
            hsend.at[0, j],
            hrecv.at[0, j],
            device_id=(me - j,),
            device_id_type=MESH,
        )

    def high(j):
        block = 2 * count - 1 - me - j
        upper = block // count
        target = block + upper * (2 * count - 1 - 2 * block)
        copy = pltpu.make_async_remote_copy(
            hout.at[1, j - 1],
            hin.at[upper, j - 1],
            hsend.at[1, j],
            hrecv.at[upper, j],
            device_id=(target,),
            device_id_type=MESH,
        )
        return copy, target

    def incoming(half, j):
        return pltpu.make_async_remote_copy(
            hout.at[0, j - 1],
            hin.at[half, j - 1],
            hsend.at[0, j],
            hrecv.at[half, j],
            device_id=flip(me, bits, 0),
            device_id_type=MESH,
        )

    for j in range(1, reach + 1):
        pl.when(me >= j)(low(j).start)
        copy, target = high(j)
        pl.when(target != me)(copy.start)
    first.advance(1)
    small_s[:, :128] = (dot(grad_s[...], qb_ref[...], NT) * mask_ref[...]).astype(bf16)
    flat_two[pl.ds(0, d)] = dot(a1_ref[...], small_s[:, :128], TN).astype(bf16)
    store_tiles(flat_two, at_qb, dot(iq_ref[...], grad_s[...], TN))
    used = 3 * d + 2 * HD
    spare = flat_two.shape[0] - used
    flat_two[pl.ds(used, spare)] = jnp.zeros((spare, 128), bf16)
    first.advance(2)
    for half in range(2):
        own = dkv_s[half, :, reach * width :].T
        acc[half * width : (half + 1) * width, : 2 * HD] = own
    for j in range(1, reach + 1):
        lower_self = 2 * me == 2 * count - 1 - j

        @pl.when(jnp.logical_not(lower_self))
        def _(j=j):
            incoming(0, j).wait_recv()
            acc[:width, : 2 * HD] += hin[0, j - 1].astype(f32)

        @pl.when(lower_self)
        def _(j=j):
            acc[:width, : 2 * HD] += hout[1, j - 1].astype(f32)

        @pl.when(me >= j)
        def _(j=j):
            incoming(1, j).wait_recv()
            acc[width:, : 2 * HD] += hin[1, j - 1].astype(f32)

    small_s[:, 128 : 128 + 2 * HD] = acc[:, : 2 * HD].astype(bf16)
    dkv = small_s[:, 128 : 128 + 2 * HD]
    small_s[:, 128 + 2 * HD :] = (dot(dkv, kb_ref[...], NT) * mask_ref[...]).astype(bf16)
    flat_two[pl.ds(at_ka, d)] = dot(a1_ref[...], small_s[:, 128 + 2 * HD :], TN).astype(bf16)
    store_tiles(flat_two, at_kb, dot(ik_ref[...], small_s[:, 128 : 128 + 2 * HD], TN))
    second.begin()
    first.advance(3)
    for copy in loads:
        copy.wait()
    acc[:, :d] = dot(
        beside(grad_s[...], small_s[...]),
        beside(weight(0, d), qa_ref[...], weight(d, 2 * HD), ka_ref[...]),
        NT,
    )
    first.advance(3)
    second.advance(3)

    def finish(r, unused):
        at = tile_at(r, 16)
        x = x_ref[at, :].astype(f32)
        e = acc[at, :d] * gain_ref[...]
        rr = lax.rsqrt(jnp.mean(x * x, axis=1, keepdims=True) + NORM_EPS)
        pull = (rr * rr * rr) * jnp.mean(e * x, axis=1, keepdims=True)
        dx_ref[at, :] = (dmid_ref[at, :] + rr * e - pull * x).astype(bf16)
        return unused

    lax.fori_loop(0, rows // 16, finish, 0, unroll=8)
    while first.queue or second.queue:
        second.advance(3)
        first.advance(3)

    def take(out, flat, at, tiles):
        if tiles:
            for j in range(out.shape[1] // 128):
                out[:, j * 128 : (j + 1) * 128] = flat[pl.ds(at + j * 128, 128)].astype(f32)
        else:
            out[...] = flat[pl.ds(at, out.shape[0])].astype(f32)

    take(oga_ref, flat_one, 0, False)
    take(ogb_ref, flat_one, at_ggb, True)
    take(oda_ref, flat_one, at_gda, False)
    take(odb_ref, flat_one, at_gdb, True)
    take(ooa_ref, flat_one, at_goa, False)
    take(oob_ref, flat_one, at_gob, True)
    take(oqa_ref, flat_two, 0, False)
    take(oqb_ref, flat_two, at_qb, True)
    take(oka_ref, flat_two, at_ka, False)
    take(okb_ref, flat_two, at_kb, True)
    for j in range(1, reach + 1):
        pl.when(me >= j)(low(j).wait_send)
        copy, target = high(j)
        pl.when(target != me)(copy.wait_send)


def backward(count, small, large):
    rows, d = small[0].shape
    gates, hid = large[1].shape[0] * 128, large[2].shape[0]
    keys = small[6].shape[1]
    span = keys - rows // 2 + SUB
    one = (2 * d + gates + hid + 2 * d) // 32
    two = -(-(3 * d + 2 * HD) // 512) * 16
    S = jax.ShapeDtypeStruct
    V = pltpu.VMEM
    DMA = pltpu.SemaphoreType.DMA
    five = (2,) * 5
    outs = [S((rows, d), bf16)]
    for a, b in ((d, d), (d, 2 * HD), (d, d), (d, gates), (hid, d)):
        outs += [S((a, 128), f32), S((128, b), f32)]
    return pl.pallas_call(
        functools.partial(backward_kernel, count),
        in_specs=[VMEM] * len(small) + [HBM] * len(large),
        out_specs=[VMEM] * len(outs),
        out_shape=outs,
        scratch_shapes=[V(five + (one, 128), bf16), V(five + (two, 128), bf16)]
        + [V((2,) * (4 - s) + (one, 128), bf16) for s in range(5)]
        + [V((2,) * (4 - s) + (two, 128), bf16) for s in range(5)]
        + [
            V(five + (d // 32, d + 2 * HD), bf16),
            V((2, GROUP * SUB, span), bf16),
            V((rows, d), bf16),
            V((rows, 256 + 2 * HD), bf16),
            V((2, 2 * HD, keys), f32),
            V((rows, d), f32),
            V((2, 4, rows // 2, 2 * HD), bf16),
            V((2, 4, rows // 2, 2 * HD), bf16),
            DMA((2,)),
            DMA((2,)),
            DMA((4,)),
            DMA((3, 10)),
            DMA((3, 10)),
            DMA((3, 10)),
            DMA((3, 10)),
            DMA((2, 5)),
            DMA((2, 5)),
        ],
        compiler_params=pltpu.CompilerParams(
            collective_id=1, has_side_effects=True, vmem_limit_bytes=63 << 20
        ),
        name="backward",
    )(*small, *large)


def local_own(
    tokens,
    cotangent,
    doc_lengths,
    adapter_ids,
    w_query,
    w_keyval,
    w_output,
    w_gateup,
    w_down,
    gain_attn,
    gain_mlp,
    query_a,
    query_b,
    keyval_a,
    keyval_b,
    output_a,
    output_b,
    gateup_a,
    gateup_b,
    down_a,
    down_b,
):
    count = lax.axis_size("ctx")
    device = lax.axis_index("ctx")
    local_rows = tokens.shape[0]
    width = local_rows // 2
    reach = (WINDOW + width - 1) // width
    half_rows = jnp.arange(width, dtype=jnp.int32)
    own_blocks = (device, 2 * count - 1 - device)
    positions = jnp.concatenate(
        [own_blocks[0] * width + half_rows, own_blocks[1] * width + half_rows]
    )
    segment, mask = adapter_mask(doc_lengths, adapter_ids, positions)
    key_blocks = [[block - reach + step for step in range(reach + 1)] for block in own_blocks]
    key_pos = jnp.stack(
        [jnp.concatenate([e * width + half_rows for e in blocks]) for blocks in key_blocks]
    )
    key_seg = segment_of(doc_lengths, key_pos.reshape(-1)).reshape(2, 1, -1)
    (
        result,
        grad_middle,
        act_one,
        query,
        keys,
        attention,
        inner_query,
        inner_keyval,
        inner_output,
        g_gateup_a,
        g_gateup_b,
        g_down_a,
        g_down_b,
        prob,
        full_query,
        full_keyval,
        full_output,
        unused_down,
        unused_gateup,
    ) = forward(
        count,
        (
            tokens,
            cotangent,
            mask,
            segment[:, None],
            key_seg,
            gain_attn[None, :],
            gain_mlp[None, :],
            query_a,
            query_b,
            keyval_a,
            keyval_b,
            output_a,
            output_b,
            gateup_a,
            gateup_b,
            down_a,
            down_b,
        ),
        (w_query, w_keyval, w_output, w_down, w_gateup),
    )
    grad_tokens, *sums = backward(
        count,
        (
            grad_middle,
            tokens,
            mask,
            gain_attn[None, :],
            act_one,
            query,
            keys,
            attention,
            inner_query,
            inner_keyval,
            inner_output,
            query_a,
            query_b,
            keyval_a,
            keyval_b,
            output_a,
            output_b,
        ),
        (
            g_gateup_a,
            g_gateup_b,
            g_down_a,
            g_down_b,
            prob,
            full_query,
            full_keyval,
            full_output,
        ),
    )
    return (result, grad_tokens, *sums)


def solution(mesh):
    in_specs = (
        P("ctx", None),
        P("ctx", None),
        P(),
        P(),
        P("ctx", None),
        P("ctx", None),
        P("ctx", None),
        P("ctx", None),
        P("ctx", None),
        P(),
        P(),
        P(),
        P(),
        P(),
        P(),
        P(),
        P(),
        P(),
        P(),
        P(),
        P(),
    )
    out_specs = (P("ctx", None), P("ctx", None), P(), P(), P(), P(), P(), P(), P(), P(), P(), P())
    local = local_own if mesh.shape["ctx"] == 32 else local_native
    return jax.shard_map(local, mesh=mesh, in_specs=in_specs, out_specs=out_specs, check_vma=False)
```

```python
import functools

import jax
import jax.numpy as jnp
from jax import lax
from jax.experimental import pallas as pl
from jax.experimental.pallas import tpu as pltpu
from jax.sharding import PartitionSpec as P

HEADS = 12
HD = 128
FF = 4608
WINDOW = 1024
RANK = 16
ADAPTERS = 8


NORM_EPS = 1e-06
MASKED = -1e30


MESH = pl.DeviceIdType.MESH
bf16 = jnp.bfloat16
f32 = jnp.float32
NN = (((1,), (0,)), ((), ()))
NT = (((1,), (1,)), ((), ()))
TN = (((0,), (0,)), ((), ()))
VMEM = pl.BlockSpec(memory_space=pltpu.VMEM)
HBM = pl.BlockSpec(memory_space=pl.ANY)
ORD_A = (4, 3, 1, 2, 0)
ORD_A2 = (4, 3, 2, 1, 0)
ORD_B = (4, 1, 2, 3, 0)
ORD_B2 = (4, 2, 1, 3, 0)
ORD_C = (4, 2, 3, 1, 0)
ORD_C2 = (4, 1, 3, 2, 0)


def shifted(x, axis, by):
    size = lax.axis_size(axis)
    pairs = [(i, i + by) for i in range(size) if 0 <= i + by < size]
    return lax.ppermute(x, axis, pairs)


def segment_of(doc_lengths, positions):
    starts = jnp.cumsum(doc_lengths) - doc_lengths
    return jnp.sum((starts[None, :] <= positions[:, None]).astype(jnp.int32), axis=1) - 1


def adapter_mask(doc_lengths, adapter_ids, positions):
    segment = segment_of(doc_lengths, positions)
    owner = segment[:, None] == jnp.arange(doc_lengths.shape[0], dtype=jnp.int32)[None, :]
    chosen = jnp.sum(jnp.where(owner, adapter_ids[None, :], 0), axis=1)
    columns = jnp.arange(ADAPTERS * RANK, dtype=jnp.int32) // RANK
    return (segment, (columns[None, :] == chosen[:, None]).astype(jnp.float32))


def rms_scale(values, gain):
    return values * lax.rsqrt(jnp.mean(values * values, axis=-1, keepdims=True) + NORM_EPS) * gain


def by_rows(left, right):
    return lax.dot_general(
        left, right, (((0,), (0,)), ((), ())), preferred_element_type=jnp.float32
    )


def by_cols(left, right):
    return lax.dot_general(
        left, right, (((1,), (1,)), ((), ())), preferred_element_type=jnp.float32
    )


def adapted(inputs, weight, down_part, up_part, mask):
    inner = (jnp.dot(inputs, down_part, preferred_element_type=jnp.float32) * mask).astype(
        jnp.bfloat16
    )
    return (
        jnp.dot(inputs, weight, preferred_element_type=jnp.float32)
        + jnp.dot(inner, up_part, preferred_element_type=jnp.float32),
        inner,
    )


def adapter_back(grad_out, inputs, inner, up_part, mask):
    grad_up = by_rows(inner, grad_out)
    grad_inner = (by_cols(grad_out, up_part) * mask).astype(jnp.bfloat16)
    return (by_rows(inputs, grad_inner), grad_up, grad_inner)


def owner_of(block, count, width):
    device_of = jnp.where(block < count, block, 2 * count - 1 - block)
    return (device_of, jnp.where(block < count, 0, width))


def key_block(table, first_device, block, count, width):
    device_of, row_in = owner_of(block, count, width)
    piece = lax.dynamic_slice(
        table, (device_of - first_device, row_in, jnp.int32(0)), (1, width, table.shape[2])
    )
    return piece[0]


def block_scores(query, keys, allowed):
    rows = query.shape[0]
    heads = query.reshape(rows, HEADS, HD)
    raw = jnp.einsum(
        "rhd,kd->rhk", heads, keys[:, :HD], preferred_element_type=jnp.float32
    ) * HD ** (-0.5)
    return jnp.where(allowed[:, None, :], raw, MASKED)


def attend_forward(query, keys, allowed):
    scores = block_scores(query, keys, allowed)
    top = jnp.max(scores, axis=-1, keepdims=True)
    total = jnp.sum(jnp.exp(scores - top), axis=-1, keepdims=True)
    log_total = top + jnp.log(total)
    weights = jnp.exp(scores - log_total).astype(jnp.bfloat16)
    mixed = jnp.einsum("rhk,kd->rhd", weights, keys[:, HD:], preferred_element_type=jnp.float32)
    return (mixed.reshape(query.shape[0], -1), log_total)


def attend_backward(query, keys, allowed, log_total, grad_out):
    rows = query.shape[0]
    prob = jnp.exp(block_scores(query, keys, allowed) - log_total)
    grad_heads = grad_out.reshape(rows, HEADS, HD)
    grad_prob = jnp.einsum(
        "rhd,kd->rhk", grad_heads, keys[:, HD:], preferred_element_type=jnp.float32
    )
    delta = jnp.sum(prob * grad_prob, axis=-1, keepdims=True)
    grad_scores = (prob * (grad_prob - delta)).astype(jnp.bfloat16)
    scale = HD ** (-0.5)
    grad_query = (
        jnp.einsum("rhk,kd->rhd", grad_scores, keys[:, :HD], preferred_element_type=jnp.float32)
        * scale
    )
    grad_key = (
        jnp.einsum(
            "rhk,rhd->kd",
            grad_scores,
            query.reshape(rows, HEADS, HD),
            preferred_element_type=jnp.float32,
        )
        * scale
    )
    grad_value = jnp.einsum(
        "rhk,rhd->kd", prob.astype(jnp.bfloat16), grad_heads, preferred_element_type=jnp.float32
    )
    return (grad_query.reshape(rows, -1), jnp.concatenate([grad_key, grad_value], axis=1))


def local_native(
    tokens,
    cotangent,
    doc_lengths,
    adapter_ids,
    w_query,
    w_keyval,
    w_output,
    w_gateup,
    w_down,
    gain_attn,
    gain_mlp,
    query_a,
    query_b,
    keyval_a,
    keyval_b,
    output_a,
    output_b,
    gateup_a,
    gateup_b,
    down_a,
    down_b,
):
    count = lax.axis_size("ctx")
    device = lax.axis_index("ctx")
    local_rows = tokens.shape[0]
    width = local_rows // 2
    reach = (WINDOW + width - 1) // width
    key_width = w_keyval.shape[1]
    half_rows = jnp.arange(width, dtype=jnp.int32)
    own_blocks = (device, 2 * count - 1 - device)
    positions = jnp.concatenate(
        [own_blocks[0] * width + half_rows, own_blocks[1] * width + half_rows]
    )
    segment, mask = adapter_mask(doc_lengths, adapter_ids, positions)
    resid = tokens.astype(jnp.float32)
    act_one = rms_scale(resid, gain_attn).astype(jnp.bfloat16)
    full_query, full_keyval, full_output, full_gateup = (
        lax.all_gather(w_query, "ctx", axis=0, tiled=True),
        lax.all_gather(w_keyval, "ctx", axis=0, tiled=True),
        lax.all_gather(w_output, "ctx", axis=0, tiled=True),
        lax.all_gather(w_gateup, "ctx", axis=0, tiled=True),
    )
    query_full, inner_query = adapted(act_one, full_query, query_a, query_b, mask)
    keyval_full, inner_keyval = adapted(act_one, full_keyval, keyval_a, keyval_b, mask)
    query = query_full.astype(jnp.bfloat16)
    keyval = keyval_full.astype(jnp.bfloat16)
    stacked = [keyval]
    for offset in range(1, reach + 1):
        later = shifted(keyval, "ctx", -offset)
        prior = shifted(keyval, "ctx", offset)
        stacked = [prior] + stacked + [later]
    table = jnp.stack(stacked)
    first_device = device - reach
    kept = []
    mixed_parts = []
    for which in range(2):
        block = own_blocks[which]
        key_blocks = [block - reach + step for step in range(reach + 1)]
        keys = jnp.concatenate(
            [key_block(table, first_device, entry, count, width) for entry in key_blocks], axis=0
        )
        key_pos = jnp.concatenate([entry * width + half_rows for entry in key_blocks])
        key_seg = segment_of(doc_lengths, key_pos)
        query_pos = positions[which * width : (which + 1) * width]
        query_seg = segment[which * width : (which + 1) * width]
        allowed = (
            (key_pos[None, :] <= query_pos[:, None])
            & (query_pos[:, None] - key_pos[None, :] < WINDOW)
            & (key_seg[None, :] == query_seg[:, None])
        )
        mixed, log_total = attend_forward(query[which * width : (which + 1) * width], keys, allowed)
        kept.append((key_blocks, keys, allowed, log_total))
        mixed_parts.append(mixed)
    attention = jnp.concatenate(mixed_parts, axis=0).astype(jnp.bfloat16)
    branch_one, inner_output = adapted(attention, full_output, output_a, output_b, mask)
    middle = resid + branch_one
    act_two = rms_scale(middle, gain_mlp).astype(jnp.bfloat16)
    gate_up, inner_gateup = adapted(act_two, full_gateup, gateup_a, gateup_b, mask)
    gate = gate_up[:, :FF]
    upper = gate_up[:, FF:]
    hidden = (jax.nn.gelu(gate) * upper).astype(jnp.bfloat16)
    down_main = jnp.dot(
        hidden,
        lax.all_gather(w_down, "ctx", axis=0, tiled=True),
        preferred_element_type=jnp.float32,
    )
    inner_down = (jnp.dot(hidden, down_a, preferred_element_type=jnp.float32) * mask).astype(
        jnp.bfloat16
    )
    result = middle + (down_main + jnp.dot(inner_down, down_b, preferred_element_type=jnp.float32))
    grad_down_a, grad_down_b, d_inner_down = adapter_back(
        cotangent, hidden, inner_down, down_b, mask
    )
    grad_hidden = by_cols(cotangent, lax.all_gather(w_down, "ctx", axis=0, tiled=True)) + by_cols(
        d_inner_down, down_a
    )

    def gated(gate_part, up_part):
        return jax.nn.gelu(gate_part) * up_part

    unused, pull_glu = jax.vjp(gated, gate, upper)
    grad_gate, grad_up = pull_glu(grad_hidden)
    grad_gateup = jnp.concatenate([grad_gate, grad_up], axis=1).astype(jnp.bfloat16)
    grad_gateup_a, grad_gateup_b, d_inner_gateup = adapter_back(
        grad_gateup, act_two, inner_gateup, gateup_b, mask
    )
    grad_act_two = by_cols(grad_gateup, full_gateup) + by_cols(d_inner_gateup, gateup_a)
    unused, pull_two = jax.vjp(lambda values: rms_scale(values, gain_mlp), middle)
    grad_middle = cotangent.astype(jnp.float32) + pull_two(grad_act_two)[0]
    grad_branch = grad_middle.astype(jnp.bfloat16)
    grad_output_a, grad_output_b, d_inner_output = adapter_back(
        grad_branch, attention, inner_output, output_b, mask
    )
    grad_attention = (by_cols(grad_branch, full_output) + by_cols(d_inner_output, output_a)).astype(
        jnp.bfloat16
    )
    query_grads = []
    key_grads = []
    for which in range(2):
        key_blocks, keys, allowed, log_total = kept[which]
        rows_query = query[which * width : (which + 1) * width]
        rows_grad = grad_attention[which * width : (which + 1) * width]
        grad_rows, grad_keys = attend_backward(rows_query, keys, allowed, log_total, rows_grad)
        query_grads.append(grad_rows)
        for step, entry in enumerate(key_blocks):
            key_grads.append((entry, grad_keys[step * width : (step + 1) * width]))
    grad_query = jnp.concatenate(query_grads, axis=0).astype(jnp.bfloat16)
    slots = jnp.zeros((2 * reach + 1, local_rows, key_width), jnp.float32)
    for entry, piece in key_grads:
        device_of, row_in = owner_of(entry, count, width)
        slot = device_of - first_device
        current = lax.dynamic_slice(slots, (slot, row_in, jnp.int32(0)), (1, width, key_width))
        slots = lax.dynamic_update_slice(slots, current + piece[None], (slot, row_in, jnp.int32(0)))
    grad_keyval_full = slots[reach]
    for offset in range(1, reach + 1):
        from_lower = shifted(slots[reach + offset].astype(jnp.bfloat16), "ctx", offset).astype(
            jnp.float32
        )
        from_upper = shifted(slots[reach - offset].astype(jnp.bfloat16), "ctx", -offset).astype(
            jnp.float32
        )
        grad_keyval_full = grad_keyval_full + from_lower + from_upper
    grad_keyval = grad_keyval_full.astype(jnp.bfloat16)
    grad_query_a, grad_query_b, d_inner_query = adapter_back(
        grad_query, act_one, inner_query, query_b, mask
    )
    grad_keyval_a, grad_keyval_b, d_inner_keyval = adapter_back(
        grad_keyval, act_one, inner_keyval, keyval_b, mask
    )
    grad_act_one = (
        by_cols(grad_query, full_query)
        + by_cols(grad_keyval, full_keyval)
        + by_cols(d_inner_query, query_a)
        + by_cols(d_inner_keyval, keyval_a)
    )
    unused, pull_one = jax.vjp(lambda values: rms_scale(values, gain_attn), resid)
    grad_tokens = (grad_middle + pull_one(grad_act_one)[0]).astype(jnp.bfloat16)
    sums = lax.psum(
        (
            grad_query_a,
            grad_query_b,
            grad_keyval_a,
            grad_keyval_b,
            grad_output_a,
            grad_output_b,
            grad_gateup_a,
            grad_gateup_b,
            grad_down_a,
            grad_down_b,
        ),
        "ctx",
    )
    return (
        result.astype(jnp.bfloat16),
        grad_tokens,
        sums[0],
        sums[1],
        sums[2],
        sums[3],
        sums[4],
        sums[5],
        sums[6],
        sums[7],
        sums[8],
        sums[9],
    )


def flip(me, bits, b):
    return (me+(1-2*bits[b])*(1<<b),)
CHUNK = 512
UNIT = 256
SUB = 128
GROUP = 4
SCALE = HD ** (-0.5)
LAGS = (0, 2, 4, 6, 8)
SOFT_UNROLL = 8
AHEAD = 18 + LAGS[4]
KEYS_AT = 4 + LAGS[4]
ATT_STEPS = 8


def dot(a, b, dims=NN):
    return lax.dot_general(a, b, dims, preferred_element_type=f32)


def tile_at(i, size):
    return pl.ds(i * size if isinstance(i, int) else pl.multiple_of(i * size, size), size)


def even_odd(par, low, high):
    if par % 2:
        return ((low, 2, ORD_A2), (high, 1, ORD_C2), (high + 1, 1, ORD_B2))
    return ((low, 2, ORD_A), (high, 1, ORD_C), (high + 1, 1, ORD_B))


def bits_of(me):
    return [(me // (1 << b)) % 2 for b in range(5)]


def meet_all(count, me):
    barrier = pltpu.get_barrier_semaphore()

    def greet(k, unused):
        pl.semaphore_signal(
            barrier, 1, device_id=(lax.rem(me + k, count),), device_id_type=MESH
        )
        return unused

    lax.fori_loop(1, count, greet, 0)
    pl.semaphore_wait(barrier, count - 1)


def heads_down(x):
    return jnp.concatenate([x[:, i * HD : (i + 1) * HD] for i in range(x.shape[1] // HD)], axis=0)


def heads_across(x):
    return jnp.concatenate([x[i * SUB : (i + 1) * SUB] for i in range(x.shape[0] // SUB)], axis=1)


def norm_rows(read, gain_ref, write, rows):
    def block(r, unused):
        at = tile_at(r, 16)
        x = read(at)
        scale = lax.rsqrt(jnp.mean(x * x, axis=1, keepdims=True) + NORM_EPS)
        write(at, (x * scale * gain_ref[...]).astype(bf16))
        return unused

    lax.fori_loop(0, rows // 16, block, 0, unroll=8)


def forward_kernel(
    count,
    x_ref,
    g_ref,
    mask_ref,
    qseg_ref,
    kseg_ref,
    gain1_ref,
    gain2_ref,
    qa_ref,
    qb_ref,
    ka_ref,
    kb_ref,
    oa_ref,
    ob_ref,
    ga_ref,
    gb_ref,
    da_ref,
    db_ref,
    wq_own,
    wk_own,
    wo_own,
    wd_own,
    wg_own,
    out_ref,
    dmid_ref,
    a1_ref,
    q_ref,
    keys_ref,
    att_ref,
    iq_ref,
    ik_ref,
    io_ref,
    gga_ref,
    ggb_ref,
    gda_ref,
    gdb_ref,
    prob_hbm,
    wq_all,
    wk_all,
    wo_all,
    wd_all,
    wg_all,
    held_q,
    held_k,
    held_o,
    held_d,
    held_g,
    wbuf,
    dbuf,
    pbuf,
    kv_own,
    a2_s,
    igu_s,
    did_s,
    acc_o,
    acc_a,
    gu_s,
    dh_s,
    hid_s,
    dgu_s,
    wsem,
    dsem,
    psem,
    own_sem,
    xsend,
    xrecv,
    hsend,
    hrecv,
):
    rows, d = x_ref.shape
    width = rows // 2
    reach = WINDOW // width
    keys = keys_ref.shape[1]
    span = keys - width + SUB
    ff = da_ref.shape[0]
    nu, nc = ff // UNIT, ff // CHUNK
    me = lax.axis_index("ctx")
    bits = bits_of(me)
    meet_all(count, me)
    here = (bits[4], bits[3], bits[2], bits[1], bits[0])
    own = (wq_own, wk_own, wo_own, wd_own, wg_own)
    held = (held_q, held_k, held_o, held_d, held_g)
    full = (wq_all, wk_all, wo_all, wd_all, wg_all)

    def where(bit_set):
        return tuple(pl.ds(0, 2) if b in bit_set else bits[b] for b in (4, 3, 2, 1, 0))

    def remote(src, dst, send, recv, bit):
        return pltpu.make_async_remote_copy(
            src, dst, send, recv, device_id=flip(me, bits, bit), device_id_type=MESH
        )

    units = []
    for u in range(3):
        units.append((0, 0, even_odd(u, 4 * u, 4 * u + 2)))
    units.append((1, 0, ((0, 1, ORD_A), (1, 1, ORD_C2))))
    for u in range(3):
        units.append((2, 0, even_odd(u, 4 * u, 4 * u + 2)))
    thick = wd_own.shape[0] // 3
    for u in range(9):
        units.append((3, u // 3 * thick, even_odd(u + 1, u % 3 * 4, u % 3 * 4 + 2)))
    first = len(units)

    def exchange(u, cl, k):
        w, row, split = units[u]
        tile, tiles, order = split[cl]
        lines = pl.ds(row, wq_own.shape[0])
        cols = pl.ds(tile * 128, tiles * 128)
        there = full[w].at[where(order[:k]) + (lines, cols)]
        return remote(
            there if k else own[w].at[lines, cols],
            there,
            xsend.at[u, cl, k],
            xrecv.at[u, cl, k],
            order[k],
        )

    def gate(v, par, cl, k):
        tile, tiles, order = even_odd(par, 0, ff // 128)[cl]
        at = tile * 128 + v * UNIT
        cols = pl.ds(at if isinstance(at, int) else pl.multiple_of(at, 128), tiles * 128)
        there = wg_all.at[where(order[:k]) + (slice(None), cols)]
        return remote(
            there if k else wg_own.at[:, cols],
            there,
            xsend.at[first + v, cl, k],
            xrecv.at[first + v, cl, k],
            order[k],
        )

    staged = [pltpu.make_async_copy(own[w], held[w], own_sem.at[w]) for w in range(5)]
    placed = [pltpu.make_async_copy(held[w], full[w].at[here], own_sem.at[w]) for w in range(5)]
    for copy in staged:
        copy.start()
    done_place = set()

    def place(w):
        if w not in done_place:
            done_place.add(w)
            placed[w].wait()

    order = []
    for t in range(AHEAD):
        for k in (4, 3, 2, 1, 0):
            u = t - LAGS[k]
            if 0 <= u < first + nu:
                order.append((t + (4 - k) / 5, u, k))

    def steps(n):
        while order and order[0][0] < n:
            unused, u, k = order.pop(0)
            w = units[u][0] if u < first else 4
            if k:
                place(w)
            for cl in range(2 if w == 1 else 3):
                at = (
                    functools.partial(exchange, u, cl)
                    if u < first
                    else functools.partial(gate, u - first, (u - first) % 2, cl)
                )
                if k:
                    at(k - 1).wait_recv()
                at(k).start()

    def loop_steps(c, point):
        for i in (2 * point, 2 * point + 1):
            t, k = i // 5, 4 - i % 5
            v = 2 * c + t + AHEAD - first - LAGS[k]
            par = (t + AHEAD - first - LAGS[k]) % 2

            @pl.when(v < nu)
            def _(v=v, par=par, k=k):
                for cl in range(3):
                    if k:
                        gate(v, par, cl, k - 1).wait_recv()
                    gate(v, par, cl, k).start()

    def arrived(weight_at):
        for u, unit in enumerate(units):
            if unit[0] == weight_at:
                for cl in range(len(unit[2])):
                    exchange(u, cl, 4).wait_recv()

    def load(w, lo, n, slot, at, sem):
        return pltpu.make_async_copy(
            full[w].at[(slice(None),) * 6 + (pl.ds(lo, n),)],
            wbuf.at[(slot,) + (slice(None),) * 6 + (pl.ds(at, n),)],
            wsem.at[slot, sem],
        )

    def weight(slot, lo, n):
        return wbuf[slot, :, :, :, :, :, :, lo : lo + n].reshape(-1, n)

    for w in range(5):
        staged[w].wait()
        placed[w].start()
    steps(4)
    def read_x(at):
        return x_ref[at, :].astype(f32)

    def write_a1(at, y):
        a1_ref[at, :] = y

    norm_rows(read_x, gain1_ref, write_a1, rows)
    iq_ref[...] = (dot(a1_ref[...], qa_ref[...]) * mask_ref[...]).astype(bf16)
    ik_ref[...] = (dot(a1_ref[...], ka_ref[...]) * mask_ref[...]).astype(bf16)
    did_s[...] = (dot(g_ref[...], db_ref[...], NT) * mask_ref[...]).astype(bf16)
    steps(KEYS_AT)
    arrived(0)
    arrived(1)
    loads = [load(0, 0, 1024, 0, 0, 0), load(0, 1024, d - 1024, 1, 0, 0)]
    loads.append(load(1, 0, 2 * HD, 1, d - 1024, 1))
    for copy in loads:
        copy.start()
    for copy in loads:
        copy.wait()

    def beside(a, b):
        return jnp.concatenate([a, b], axis=1)

    def under(a, b):
        return jnp.concatenate([a, b], axis=0)

    kv_own[...] = dot(
        beside(a1_ref[...], ik_ref[...]), under(weight(1, d - 1024, 2 * HD), kb_ref[...])
    ).astype(bf16)
    keys_ref[0, pl.ds(reach * width, width)] = kv_own[pl.ds(0, width)]
    keys_ref[1, pl.ds(reach * width, width)] = kv_own[pl.ds(width, width)]

    def low(j):
        block = me + j
        upper = block // count
        target = block + upper * (2 * count - 1 - 2 * block)
        copy = pltpu.make_async_remote_copy(
            kv_own.at[pl.ds(0, width)],
            keys_ref.at[upper, pl.ds((reach - j) * width, width)],
            hsend.at[0, j],
            hrecv.at[upper, j],
            device_id=(target,),
            device_id_type=MESH,
        )
        return copy, target

    def high(j):
        return pltpu.make_async_remote_copy(
            kv_own.at[pl.ds(width, width)],
            keys_ref.at[1, pl.ds((reach - j) * width, width)],
            hsend.at[1, j],
            hrecv.at[1, j],
            device_id=(me - j,),
            device_id_type=MESH,
        )

    def incoming(which, j):
        return pltpu.make_async_remote_copy(
            kv_own.at[pl.ds(0, width)],
            keys_ref.at[which, pl.ds((reach - j) * width, width)],
            hsend.at[0, j],
            hrecv.at[which, j],
            device_id=flip(me, bits, 0),
            device_id_type=MESH,
        )

    for j in range(1, reach + 1):
        copy, target = low(j)
        pl.when(target != me)(copy.start)
        pl.when(me >= j)(high(j).start)

        @pl.when(target == me)
        def _(j=j):
            keys_ref[1, pl.ds((reach - j) * width, width)] = kv_own[pl.ds(0, width)]

        @pl.when(me < j)
        def _(j=j):
            keys_ref[0, pl.ds((reach - j) * width, width)] = jnp.zeros((width, 2 * HD), bf16)

    steps(KEYS_AT + 1)
    q_ref[:, :1024] = dot(
        beside(a1_ref[...], iq_ref[...]), under(weight(0, 0, 1024), qb_ref[:, :1024])
    ).astype(bf16)
    q_ref[:, 1024:] = dot(
        beside(a1_ref[...], iq_ref[...]), under(weight(1, 0, d - 1024), qb_ref[:, 1024:])
    ).astype(bf16)
    for j in range(1, reach + 1):
        pl.when(me >= j)(incoming(0, j).wait_recv)
        pl.when(2 * me != 2 * count - 1 - j)(incoming(1, j).wait_recv)
    steps(KEYS_AT + 2)

    groups = HEADS // GROUP
    subs = width // SUB
    turn = 0
    for which in range(2):
        for s in range(subs):
            base = s * SUB
            lines = slice(which * width + base, which * width + base + SUB)
            row = lax.broadcasted_iota(jnp.int32, (SUB, span), 0)
            col = lax.broadcasted_iota(jnp.int32, (SUB, span), 1)
            ok = (
                (col <= row + (span - SUB))
                & (col > row + (span - SUB - WINDOW))
                & (kseg_ref[which, :, base : base + span] == qseg_ref[lines, :])
            )
            acc_a[:SUB, :span] = jnp.where(ok, 0.0, MASKED)

            for g in range(groups):
                heads = slice(g * GROUP * HD, (g + 1) * GROUP * HD)
                k = keys_ref[which, base : base + span, :HD]
                v = keys_ref[which, base : base + span, HD:]
                acc_o[: GROUP * SUB, :span] = dot(heads_down(q_ref[lines, heads]), k, NT)
                slot = turn % 2
                if turn >= 2:
                    pltpu.make_async_copy(
                        pbuf.at[slot], prob_hbm.at[0, 0, pl.ds(0, GROUP * SUB)], psem.at[slot]
                    ).wait()

                def soft(r, unused, slot=slot):
                    at = tile_at(r, 16)
                    bias = acc_a[tile_at(r % (SUB // 16), 16), :span]
                    sc = acc_o[at, :span] * SCALE + bias
                    e = jnp.exp(sc - jnp.max(sc, axis=1, keepdims=True))
                    inv = 1.0 / jnp.sum(e, axis=1, keepdims=True)
                    pbuf[slot, at, :] = (e * inv).astype(bf16)
                    return unused

                lax.fori_loop(0, GROUP * SUB // 16, soft, 0, unroll=SOFT_UNROLL)
                pltpu.make_async_copy(
                    pbuf.at[slot],
                    prob_hbm.at[which, s, pl.ds(g * GROUP * SUB, GROUP * SUB)],
                    psem.at[slot],
                ).start()
                att_ref[lines, heads] = heads_across(dot(pbuf[slot], v)).astype(bf16)
                turn += 1
                steps(KEYS_AT + 2 + ATT_STEPS * turn / (2 * subs * groups))
    for slot in range(2):
        pltpu.make_async_copy(
            pbuf.at[slot], prob_hbm.at[0, 0, pl.ds(0, GROUP * SUB)], psem.at[slot]
        ).wait()
    arrived(2)
    loads = [load(2, 0, 1024, 0, 0, 0), load(2, 1024, d - 1024, 1, 0, 0)]
    for copy in loads:
        copy.start()
    io_ref[...] = (dot(att_ref[...], oa_ref[...]) * mask_ref[...]).astype(bf16)
    for copy in loads:
        copy.wait()
    dmid_ref[:, :1024] = x_ref[:, :1024].astype(f32) + dot(
        beside(att_ref[...], io_ref[...]), under(weight(0, 0, 1024), ob_ref[:, :1024])
    )
    dmid_ref[:, 1024:] = x_ref[:, 1024:].astype(f32) + dot(
        beside(att_ref[...], io_ref[...]), under(weight(1, 0, d - 1024), ob_ref[:, 1024:])
    )
    steps(KEYS_AT + 2 + ATT_STEPS + 1)

    def read_mid(at):
        return dmid_ref[at, :]

    def write_a2(at, y):
        a2_s[at, :] = y

    norm_rows(read_mid, gain2_ref, write_a2, rows)
    igu_s[...] = (dot(a2_s[...], ga_ref[...]) * mask_ref[...]).astype(bf16)
    acc_o[...] = jnp.zeros_like(acc_o)
    acc_a[...] = jnp.zeros_like(acc_a)
    steps(AHEAD)
    arrived(3)

    def arrived_gate(c):
        for j in range(CHUNK // UNIT):
            for cl in range(3):
                gate(c * (CHUNK // UNIT) + j, j % 2, cl, 4).wait_recv()

    def down_rows(c):
        return wd_rows.at[tile_at(c, CHUNK)]

    wd_rows = wd_all.reshape(ff, d)

    def fetch(c, slot):
        cps = [
            pltpu.make_async_copy(
                wg_all.at[(slice(None),) * 6 + (tile_at_base(base, c),)],
                wbuf.at[(slot,) + (slice(None),) * 6 + (pl.ds(o, CHUNK),)],
                wsem.at[slot, i],
            )
            for i, (base, o) in enumerate(((0, 0), (ff, CHUNK)))
        ]
        cps.append(pltpu.make_async_copy(down_rows(c), dbuf.at[slot], dsem.at[slot]))
        return cps

    def tile_at_base(base, c):
        at = base + c * CHUNK
        return pl.ds(at if isinstance(at, int) else pl.multiple_of(at, 128), CHUNK)

    arrived_gate(0)
    for copy in fetch(0, 0):
        copy.start()
    for copy in fetch(0, 0):
        copy.wait()

    def chunk(c, unused):
        slot = c % 2
        loop_steps(c, 0)
        gbc = beside(gb_ref[:, tile_at_base(0, c)], gb_ref[:, tile_at_base(ff, c)])
        dac = da_ref[tile_at(c, CHUNK), :]

        def wx():
            return under(weight(slot, 0, 2 * CHUNK), gbc)

        def wdx():
            return beside(dbuf[slot], dac)

        gu_s[...] = dot(beside(a2_s[...], igu_s[...]), wx())
        loop_steps(c, 1)
        dh_s[...] = dot(beside(g_ref[...], did_s[...]), wdx(), NT)
        k0 = 0.7978845608028654

        def glu(r, unused):
            at = tile_at(r, 16)
            gate_v, up, dh = gu_s[at, :CHUNK], gu_s[at, CHUNK:], dh_s[at, :]
            sq = gate_v * gate_v
            th = jnp.tanh(gate_v * (k0 + (k0 * 0.044715) * sq))
            ht = 0.5 + 0.5 * th
            gl = gate_v * ht
            dgl = ht + (gate_v * (0.5 - 0.5 * th * th)) * (k0 + (3 * k0 * 0.044715) * sq)
            hid_s[at, :] = (gl * up).astype(bf16)
            dgu_s[at, :CHUNK] = (dh * up * dgl).astype(bf16)
            dgu_s[at, CHUNK:] = (dh * gl).astype(bf16)
            return unused

        loop_steps(c, 2)
        lax.fori_loop(0, rows // 16, glu, 0)
        loop_steps(c, 3)
        acc_o[...] += dot(hid_s[...], wdx())
        loop_steps(c, 4)
        gda_ref[tile_at(c, CHUNK), :] = dot(hid_s[...], did_s[...], TN).astype(bf16)
        r = dot(igu_s[...], dgu_s[...], TN).astype(bf16)
        for i in range(2):
            for j in range(CHUNK // 128):
                lo = i * CHUNK + j * 128
                ggb_ref[pl.ds(c * (CHUNK // 128) + (ff // 128) * i + j, 1)] = r[
                    None, :, lo : lo + 128
                ]

        @pl.when(c + 1 < nc)
        def _():
            arrived_gate(c + 1)
            for copy in fetch(c + 1, 1 - slot):
                copy.start()

        acc_a[...] += dot(dgu_s[...], wx(), NT)

        @pl.when(c + 1 < nc)
        def _():
            for copy in fetch(c + 1, 1 - slot):
                copy.wait()

        return unused

    lax.fori_loop(0, nc, chunk, 0)
    inner_d = (acc_o[:, d:] * mask_ref[...]).astype(bf16)
    acc_o[:, :d] += dot(inner_d, db_ref[...])
    r = dot(inner_d, g_ref[...], TN).astype(bf16)
    for j in range(d // 128):
        gdb_ref[j] = r[:, j * 128 : (j + 1) * 128]
    dgu = (acc_a[:, d:] * mask_ref[...]).astype(bf16)
    gga_ref[...] = dot(a2_s[...], dgu, TN).astype(bf16)
    acc_a[:, :d] += dot(dgu, ga_ref[...], NT)

    def finish(r, unused):
        at = tile_at(r, 16)
        mid = dmid_ref[at, :]
        out_ref[at, :] = (mid + acc_o[at, :d]).astype(bf16)
        e = acc_a[at, :d] * gain2_ref[...]
        rr = lax.rsqrt(jnp.mean(mid * mid, axis=1, keepdims=True) + NORM_EPS)
        pull = (rr * rr * rr) * jnp.mean(e * mid, axis=1, keepdims=True)
        dmid_ref[at, :] = g_ref[at, :].astype(f32) + rr * e - pull * mid
        return unused

    lax.fori_loop(0, rows // 16, finish, 0, unroll=8)
    for j in range(1, reach + 1):
        copy, target = low(j)
        pl.when(target != me)(copy.wait_send)
        pl.when(me >= j)(high(j).wait_send)
    for u, unit in enumerate(units):
        for cl in range(len(unit[2])):
            for k in range(5):
                exchange(u, cl, k).wait_send()

    def sent(v, unused):
        for par in range(2):
            for cl in range(3):
                for k in range(5):
                    gate(2 * v + par, par, cl, k).wait_send()
        return unused

    lax.fori_loop(0, nu // 2, sent, 0)


def forward(count, small, weights):
    x, g = small[0], small[1]
    rows, d = x.shape
    ff = weights[3].shape[0] * count
    width = rows // 2
    keys = WINDOW + width
    span = keys - width + SUB
    nu = ff // UNIT
    S = jax.ShapeDtypeStruct
    full = [S((2,) * 5 + w.shape, bf16) for w in weights]
    outs = [
        S((rows, d), bf16),
        S((rows, d), f32),
        S((rows, d), bf16),
        S((rows, d), bf16),
        S((2, keys, 2 * HD), bf16),
        S((rows, d), bf16),
        S((rows, 128), bf16),
        S((rows, 128), bf16),
        S((rows, 128), bf16),
        S((d, 128), bf16),
        S((2 * ff // 128, 128, 128), bf16),
        S((ff, 128), bf16),
        S((d // 128, 128, 128), bf16),
    ]
    DMA = pltpu.SemaphoreType.DMA
    return pl.pallas_call(
        functools.partial(forward_kernel, count),
        in_specs=[VMEM] * len(small) + [HBM] * 5,
        out_specs=[VMEM] * len(outs) + [HBM] * 6,
        out_shape=outs + [S((2, width // SUB, HEADS * SUB, span), bf16)] + full,
        scratch_shapes=[pltpu.VMEM(w.shape, bf16) for w in weights]
        + [
            pltpu.VMEM((2,) * 6 + (weights[0].shape[0], 2 * CHUNK), bf16),
            pltpu.VMEM((2, CHUNK, d), bf16),
            pltpu.VMEM((2, GROUP * SUB, span), bf16),
            pltpu.VMEM((rows, 2 * HD), bf16),
            pltpu.VMEM((rows, d), bf16),
            pltpu.VMEM((rows, 128), bf16),
            pltpu.VMEM((rows, 128), bf16),
            pltpu.VMEM((rows, d + 128), f32),
            pltpu.VMEM((rows, d + 128), f32),
            pltpu.VMEM((rows, 2 * CHUNK), f32),
            pltpu.VMEM((rows, CHUNK), f32),
            pltpu.VMEM((rows, CHUNK), bf16),
            pltpu.VMEM((rows, 2 * CHUNK), bf16),
            DMA((2, 2)),
            DMA((2,)),
            DMA((2,)),
            DMA((5,)),
            DMA((16 + nu, 3, 5)),
            DMA((16 + nu, 3, 5)),
            DMA((2, 5)),
            DMA((2, 5)),
        ],
        compiler_params=pltpu.CompilerParams(
            collective_id=0, has_side_effects=True, vmem_limit_bytes=63 << 20
        ),
        name="forward",
    )(*small, *weights)


ADVANCE = (6, 11)


class Sum:
    def __init__(self, me, buf, parts, send, recv):
        self.me, self.bits = me, bits_of(me)
        self.buf, self.parts, self.send, self.recv = buf, parts, send, recv
        tiles = buf.shape[5] // 16
        third, sixth = round(tiles / 3), round(tiles / 6)
        sizes = (third, third, sixth, tiles - 2 * third - sixth)
        self.split, row = [], 0
        for n, order in zip(sizes, (ORD_A, ORD_A2, ORD_B, ORD_B2)):
            self.split.append((row, n * 16, order))
            row += n * 16
        self.queue = [(s, cl) for s in range(1, 11) for cl in range(4)]

    def copy(self, cl, s):
        row, n, order = self.split[cl]
        lines = pl.ds(row, n)
        bits = self.bits
        if s < 5:
            red = order[::-1]
            bit = red[s]
            rem = [b for b in (4, 3, 2, 1, 0) if b not in red[:s]]
            src = self.buf if s == 0 else self.parts[s - 1]
            idx = tuple((1 - bits[b]) if b == bit else pl.ds(0, 2) for b in rem)
            src = src.at[idx + (lines,)]
            dst = self.parts[s].at[(pl.ds(0, 2),) * (4 - s) + (lines,)]
        else:
            bit, have = order[s - 5], order[: s - 5]
            idx = tuple(pl.ds(0, 2) if b in have else bits[b] for b in (4, 3, 2, 1, 0))
            src = dst = self.buf.at[idx + (lines,)]
        return pltpu.make_async_remote_copy(
            src,
            dst,
            self.send.at[cl, s],
            self.recv.at[cl, s],
            device_id=flip(self.me, bits, bit),
            device_id_type=MESH,
        )

    def add(self, cl, s):
        row, n, order = self.split[cl]
        red = order[::-1]
        rem = [b for b in (4, 3, 2, 1, 0) if b not in red[:s]]
        src, dst = (self.buf if s == 0 else self.parts[s - 1]), self.parts[s]
        lines = pl.ds(row, n)
        free = 4 - s

        def one(j, unused):
            at = [(j // (1 << (free - 1 - i))) % 2 for i in range(free)]
            rest = iter(at)
            idx = tuple(self.bits[b] if b == red[s] else next(rest) for b in rem)
            total = src[idx + (lines,)].astype(f32) + dst[tuple(at) + (lines,)].astype(f32)
            dst[tuple(at) + (lines,)] = total.astype(bf16)
            return unused

        lax.fori_loop(0, 1 << free, one, 0)

    def begin(self):
        for cl in range(4):
            self.copy(cl, 0).start()

    def advance(self, n=4):
        for unused in range(n):
            if not self.queue:
                return
            s, cl = self.queue.pop(0)
            before = self.copy(cl, s - 1)
            before.wait_recv()
            before.wait_send()
            if s <= 5:
                self.add(cl, s - 1)
            if s == 5:
                row, n_, unused_order = self.split[cl]
                b = self.bits
                self.buf[b[4], b[3], b[2], b[1], b[0], pl.ds(row, n_)] = self.parts[4][
                    pl.ds(row, n_)
                ]
            if s < 10:
                self.copy(cl, s).start()


def backward_kernel(
    count,
    dmid_ref,
    x_ref,
    mask_ref,
    gain_ref,
    a1_ref,
    q_ref,
    keys_ref,
    att_ref,
    iq_ref,
    ik_ref,
    io_ref,
    qa_ref,
    qb_ref,
    ka_ref,
    kb_ref,
    oa_ref,
    ob_ref,
    gga_hbm,
    ggb_hbm,
    gda_hbm,
    gdb_hbm,
    prob_hbm,
    wq_all,
    wk_all,
    wo_all,
    dx_ref,
    oqa_ref,
    oqb_ref,
    oka_ref,
    okb_ref,
    ooa_ref,
    oob_ref,
    oga_ref,
    ogb_ref,
    oda_ref,
    odb_ref,
    one,
    two,
    pa0,
    pa1,
    pa2,
    pa3,
    pa4,
    pb0,
    pb1,
    pb2,
    pb3,
    pb4,
    wbuf,
    pbuf,
    grad_s,
    small_s,
    dkv_s,
    acc,
    hout,
    hin,
    wsem,
    psem,
    gsem,
    send1,
    recv1,
    send2,
    recv2,
    hsend,
    hrecv,
):
    rows, d = x_ref.shape
    width = rows // 2
    reach = WINDOW // width
    keys = keys_ref.shape[1]
    span = keys - width + SUB
    me = lax.axis_index("ctx")
    bits = bits_of(me)
    meet_all(count, me)
    flat_one = one.reshape(-1, 128)
    flat_two = two.reshape(-1, 128)
    hid_rows = gda_hbm.shape[0]
    gates = ggb_hbm.shape[0] * 128
    at_ggb = d
    at_gda = at_ggb + gates
    at_gdb = at_gda + hid_rows
    at_goa = at_gdb + d
    at_gob = at_goa + d
    at_qb, at_ka, at_kb = d, 2 * d, 3 * d

    def whole(ref):
        return ref.at[(slice(None),) * 7]

    loads = [
        pltpu.make_async_copy(wo_all, wbuf.at[(slice(None),) * 6 + (pl.ds(0, d),)], wsem.at[0])
    ]
    grads = [
        pltpu.make_async_copy(src.reshape(-1, 128), flat_one.at[pl.ds(at, n)], gsem.at[i])
        for i, (src, at, n) in enumerate(
            (
                (gga_hbm, 0, d),
                (ggb_hbm, at_ggb, gates),
                (gda_hbm, at_gda, hid_rows),
                (gdb_hbm, at_gdb, d),
            )
        )
    ]
    groups = HEADS // GROUP
    subs = width // SUB
    turns = [(w, s, g) for w in range(2) for s in range(subs) for g in range(groups)]

    def prob(n):
        w, s, g = turns[n]
        return pltpu.make_async_copy(
            prob_hbm.at[w, s, pl.ds(g * GROUP * SUB, GROUP * SUB)], pbuf.at[n % 2], psem.at[n % 2]
        )

    for copy in loads + grads + [prob(0), prob(1)]:
        copy.start()

    def beside(*xs):
        return jnp.concatenate(xs, axis=1)

    def weight(lo, n):
        return wbuf[:, :, :, :, :, :, lo : lo + n].reshape(-1, n)

    def store_tiles(flat, at, x):
        for j in range(x.shape[1] // 128):
            flat[pl.ds(at + j * 128, 128)] = x[:, j * 128 : (j + 1) * 128].astype(bf16)

    grad_s[...] = dmid_ref[...].astype(bf16)
    small_s[:, :128] = (dot(grad_s[...], ob_ref[...], NT) * mask_ref[...]).astype(bf16)
    flat_one[pl.ds(at_goa, d)] = dot(att_ref[...], small_s[:, :128], TN).astype(bf16)
    store_tiles(flat_one, at_gob, dot(io_ref[...], grad_s[...], TN))
    for copy in grads:
        copy.wait()
    first = Sum(me, one, (pa0, pa1, pa2, pa3, pa4), send1, recv1)
    second = Sum(me, two, (pb0, pb1, pb2, pb3, pb4), send2, recv2)
    first.begin()
    for copy in loads:
        copy.wait()
    acc[:, :d] = dot(
        beside(grad_s[...], small_s[:, :128]), beside(weight(0, d), oa_ref[...]), NT
    )
    grad_s[...] = acc[:, :d].astype(bf16)
    loads = [
        pltpu.make_async_copy(wq_all, wbuf.at[(slice(None),) * 6 + (pl.ds(0, d),)], wsem.at[0]),
        pltpu.make_async_copy(
            wk_all, wbuf.at[(slice(None),) * 6 + (pl.ds(d, 2 * HD),)], wsem.at[1]
        ),
    ]
    for copy in loads:
        copy.start()
    dkv_s[...] = jnp.zeros_like(dkv_s)
    first.advance()

    for n, (which, s, g) in enumerate(turns):
        base = s * SUB
        lines = slice(which * width + base, which * width + base + SUB)
        heads = slice(g * GROUP * HD, (g + 1) * GROUP * HD)
        k = keys_ref[which, base : base + span, :HD]
        v = keys_ref[which, base : base + span, HD:]
        q = heads_down(q_ref[lines, heads])
        do = heads_down(grad_s[lines, heads])
        o = heads_down(att_ref[lines, heads])
        delta = jnp.sum(do.astype(f32) * o.astype(f32), axis=1, keepdims=True)
        prob(n).wait()
        p = pbuf[n % 2]
        ds = (p.astype(f32) * (dot(do, v, NT) - delta)).astype(bf16)
        dkv_s[which, HD:, base : base + span] += dot(do.T, p)
        dkv_s[which, :HD, base : base + span] += dot(q.T, ds) * SCALE
        grad_s[lines, heads] = heads_across(dot(ds, k) * SCALE).astype(bf16)
        if n + 2 < len(turns):
            prob(n + 2).start()
        if n in ADVANCE:
            first.advance()

    def piece(which, j):
        lo = (reach - j) * width
        return dkv_s[which, :, lo : lo + width].T

    for j in range(1, reach + 1):
        for which in range(2):
            hout[which, j - 1] = piece(which, j).astype(bf16)

    def low(j):
        return pltpu.make_async_remote_copy(
            hout.at[0, j - 1],
            hin.at[0, j - 1],
            hsend.at[0, j],
            hrecv.at[0, j],
            device_id=(me - j,),
            device_id_type=MESH,
        )

    def high(j):
        block = 2 * count - 1 - me - j
        upper = block // count
        target = block + upper * (2 * count - 1 - 2 * block)
        copy = pltpu.make_async_remote_copy(
            hout.at[1, j - 1],
            hin.at[upper, j - 1],
            hsend.at[1, j],
            hrecv.at[upper, j],
            device_id=(target,),
            device_id_type=MESH,
        )
        return copy, target

    def incoming(half, j):
        return pltpu.make_async_remote_copy(
            hout.at[0, j - 1],
            hin.at[half, j - 1],
            hsend.at[0, j],
            hrecv.at[half, j],
            device_id=flip(me, bits, 0),
            device_id_type=MESH,
        )

    for j in range(1, reach + 1):
        pl.when(me >= j)(low(j).start)
        copy, target = high(j)
        pl.when(target != me)(copy.start)
    small_s[:, :128] = (dot(grad_s[...], qb_ref[...], NT) * mask_ref[...]).astype(bf16)
    flat_two[pl.ds(0, d)] = dot(a1_ref[...], small_s[:, :128], TN).astype(bf16)
    store_tiles(flat_two, at_qb, dot(iq_ref[...], grad_s[...], TN))
    used = 3 * d + 2 * HD
    spare = flat_two.shape[0] - used
    flat_two[pl.ds(used, spare)] = jnp.zeros((spare, 128), bf16)
    first.advance()
    for half in range(2):
        own = dkv_s[half, :, reach * width :].T
        acc[half * width : (half + 1) * width, : 2 * HD] = own
    for j in range(1, reach + 1):
        lower_self = 2 * me == 2 * count - 1 - j

        @pl.when(jnp.logical_not(lower_self))
        def _(j=j):
            incoming(0, j).wait_recv()
            acc[:width, : 2 * HD] += hin[0, j - 1].astype(f32)

        @pl.when(lower_self)
        def _(j=j):
            acc[:width, : 2 * HD] += hout[1, j - 1].astype(f32)

        @pl.when(me >= j)
        def _(j=j):
            incoming(1, j).wait_recv()
            acc[width:, : 2 * HD] += hin[1, j - 1].astype(f32)

    small_s[:, 128 : 128 + 2 * HD] = acc[:, : 2 * HD].astype(bf16)
    dkv = small_s[:, 128 : 128 + 2 * HD]
    small_s[:, 128 + 2 * HD :] = (dot(dkv, kb_ref[...], NT) * mask_ref[...]).astype(bf16)
    flat_two[pl.ds(at_ka, d)] = dot(a1_ref[...], small_s[:, 128 + 2 * HD :], TN).astype(bf16)
    store_tiles(flat_two, at_kb, dot(ik_ref[...], small_s[:, 128 : 128 + 2 * HD], TN))
    second.begin()
    first.advance()
    for copy in loads:
        copy.wait()
    acc[:, :d] = dot(
        beside(grad_s[...], small_s[...]),
        beside(weight(0, d), qa_ref[...], weight(d, 2 * HD), ka_ref[...]),
        NT,
    )
    second.advance()
    first.advance()

    def finish(r, unused):
        at = tile_at(r, 16)
        x = x_ref[at, :].astype(f32)
        e = acc[at, :d] * gain_ref[...]
        rr = lax.rsqrt(jnp.mean(x * x, axis=1, keepdims=True) + NORM_EPS)
        pull = (rr * rr * rr) * jnp.mean(e * x, axis=1, keepdims=True)
        dx_ref[at, :] = (dmid_ref[at, :] + rr * e - pull * x).astype(bf16)
        return unused

    lax.fori_loop(0, rows // 16, finish, 0, unroll=8)
    while first.queue:
        second.advance()
        first.advance()

    def take(out, flat, at, tiles):
        if tiles:
            for j in range(out.shape[1] // 128):
                out[:, j * 128 : (j + 1) * 128] = flat[pl.ds(at + j * 128, 128)]
        else:
            out[...] = flat[pl.ds(at, out.shape[0])]

    take(oga_ref, flat_one, 0, False)
    take(ogb_ref, flat_one, at_ggb, True)
    take(oda_ref, flat_one, at_gda, False)
    take(odb_ref, flat_one, at_gdb, True)
    take(ooa_ref, flat_one, at_goa, False)
    take(oob_ref, flat_one, at_gob, True)
    second.advance(40)
    take(oqa_ref, flat_two, 0, False)
    take(oqb_ref, flat_two, at_qb, True)
    take(oka_ref, flat_two, at_ka, False)
    take(okb_ref, flat_two, at_kb, True)
    for j in range(1, reach + 1):
        pl.when(me >= j)(low(j).wait_send)
        copy, target = high(j)
        pl.when(target != me)(copy.wait_send)


def backward(count, small, large):
    rows, d = small[0].shape
    gates, hid = large[1].shape[0] * 128, large[2].shape[0]
    keys = small[6].shape[1]
    span = keys - rows // 2 + SUB
    one = (2 * d + gates + hid + 2 * d) // 32
    two = -(-(3 * d + 2 * HD) // 512) * 16
    S = jax.ShapeDtypeStruct
    V = pltpu.VMEM
    DMA = pltpu.SemaphoreType.DMA
    five = (2,) * 5
    outs = [S((rows, d), bf16)]
    for a, b in ((d, d), (d, 2 * HD), (d, d), (d, gates), (hid, d)):
        outs += [S((a, 128), bf16), S((128, b), bf16)]
    return pl.pallas_call(
        functools.partial(backward_kernel, count),
        in_specs=[VMEM] * len(small) + [HBM] * len(large),
        out_specs=[VMEM] * len(outs),
        out_shape=outs,
        scratch_shapes=[V(five + (one, 128), bf16), V(five + (two, 128), bf16)]
        + [V((2,) * (4 - s) + (one, 128), bf16) for s in range(5)]
        + [V((2,) * (4 - s) + (two, 128), bf16) for s in range(5)]
        + [
            V(five + (d // 32, d + 2 * HD), bf16),
            V((2, GROUP * SUB, span), bf16),
            V((rows, d), bf16),
            V((rows, 256 + 2 * HD), bf16),
            V((2, 2 * HD, keys), f32),
            V((rows, d), f32),
            V((2, 4, rows // 2, 2 * HD), bf16),
            V((2, 4, rows // 2, 2 * HD), bf16),
            DMA((2,)),
            DMA((2,)),
            DMA((4,)),
            DMA((4, 10)),
            DMA((4, 10)),
            DMA((4, 10)),
            DMA((4, 10)),
            DMA((2, 5)),
            DMA((2, 5)),
        ],
        compiler_params=pltpu.CompilerParams(
            collective_id=1, has_side_effects=True, vmem_limit_bytes=63 << 20
        ),
        name="backward",
    )(*small, *large)


def local_own(
    tokens,
    cotangent,
    doc_lengths,
    adapter_ids,
    w_query,
    w_keyval,
    w_output,
    w_gateup,
    w_down,
    gain_attn,
    gain_mlp,
    query_a,
    query_b,
    keyval_a,
    keyval_b,
    output_a,
    output_b,
    gateup_a,
    gateup_b,
    down_a,
    down_b,
):
    count = lax.axis_size("ctx")
    device = lax.axis_index("ctx")
    local_rows = tokens.shape[0]
    width = local_rows // 2
    reach = (WINDOW + width - 1) // width
    half_rows = jnp.arange(width, dtype=jnp.int32)
    own_blocks = (device, 2 * count - 1 - device)
    positions = jnp.concatenate(
        [own_blocks[0] * width + half_rows, own_blocks[1] * width + half_rows]
    )
    segment, mask = adapter_mask(doc_lengths, adapter_ids, positions)
    key_blocks = [[block - reach + step for step in range(reach + 1)] for block in own_blocks]
    key_pos = jnp.stack(
        [jnp.concatenate([e * width + half_rows for e in blocks]) for blocks in key_blocks]
    )
    key_seg = segment_of(doc_lengths, key_pos.reshape(-1)).reshape(2, 1, -1)
    (
        result,
        grad_middle,
        act_one,
        query,
        keys,
        attention,
        inner_query,
        inner_keyval,
        inner_output,
        g_gateup_a,
        g_gateup_b,
        g_down_a,
        g_down_b,
        prob,
        full_query,
        full_keyval,
        full_output,
        unused_down,
        unused_gateup,
    ) = forward(
        count,
        (
            tokens,
            cotangent,
            mask,
            segment[:, None],
            key_seg,
            gain_attn[None, :],
            gain_mlp[None, :],
            query_a,
            query_b,
            keyval_a,
            keyval_b,
            output_a,
            output_b,
            gateup_a,
            gateup_b,
            down_a,
            down_b,
        ),
        (w_query, w_keyval, w_output, w_down, w_gateup),
    )
    grad_tokens, *sums = backward(
        count,
        (
            grad_middle,
            tokens,
            mask,
            gain_attn[None, :],
            act_one,
            query,
            keys,
            attention,
            inner_query,
            inner_keyval,
            inner_output,
            query_a,
            query_b,
            keyval_a,
            keyval_b,
            output_a,
            output_b,
        ),
        (
            g_gateup_a,
            g_gateup_b,
            g_down_a,
            g_down_b,
            prob,
            full_query,
            full_keyval,
            full_output,
        ),
    )
    return (result, grad_tokens, *(s.astype(f32) for s in sums))


def solution(mesh):
    in_specs = (
        P("ctx", None),
        P("ctx", None),
        P(),
        P(),
        P("ctx", None),
        P("ctx", None),
        P("ctx", None),
        P("ctx", None),
        P("ctx", None),
        P(),
        P(),
        P(),
        P(),
        P(),
        P(),
        P(),
        P(),
        P(),
        P(),
        P(),
        P(),
    )
    out_specs = (P("ctx", None), P("ctx", None), P(), P(), P(), P(), P(), P(), P(), P(), P(), P())
    local = local_own if mesh.shape["ctx"] == 32 else local_native
    return jax.shard_map(local, mesh=mesh, in_specs=in_specs, out_specs=out_specs, check_vma=False)
```

```python
import functools

import jax
import jax.numpy as jnp
from jax import lax
from jax.experimental import pallas as pl
from jax.experimental.pallas import tpu as pltpu
from jax.sharding import PartitionSpec as P

HEADS = 12
HD = 128
FF = 4608
WINDOW = 1024
RANK = 16
ADAPTERS = 8


NORM_EPS = 1e-06
MASKED = -1e30


MESH = pl.DeviceIdType.MESH
bf16 = jnp.bfloat16
f32 = jnp.float32
NN = (((1,), (0,)), ((), ()))
NT = (((1,), (1,)), ((), ()))
TN = (((0,), (0,)), ((), ()))
VMEM = pl.BlockSpec(memory_space=pltpu.VMEM)
HBM = pl.BlockSpec(memory_space=pl.ANY)
SMEM = pl.BlockSpec(memory_space=pltpu.SMEM)
ORD_A = (4, 3, 1, 2, 0)
ORD_A2 = (4, 3, 2, 1, 0)
ORD_B = (4, 1, 2, 3, 0)
ORD_B2 = (4, 2, 1, 3, 0)
ORD_C = (4, 2, 3, 1, 0)
ORD_C2 = (4, 1, 3, 2, 0)


def shifted(x, axis, by):
    size = lax.axis_size(axis)
    pairs = [(i, i + by) for i in range(size) if 0 <= i + by < size]
    return lax.ppermute(x, axis, pairs)


def segment_of(doc_lengths, positions):
    starts = jnp.cumsum(doc_lengths) - doc_lengths
    return jnp.sum((starts[None, :] <= positions[:, None]).astype(jnp.int32), axis=1) - 1


def adapter_mask(doc_lengths, adapter_ids, positions):
    segment = segment_of(doc_lengths, positions)
    owner = segment[:, None] == jnp.arange(doc_lengths.shape[0], dtype=jnp.int32)[None, :]
    chosen = jnp.sum(jnp.where(owner, adapter_ids[None, :], 0), axis=1)
    columns = jnp.arange(ADAPTERS * RANK, dtype=jnp.int32) // RANK
    return (segment, (columns[None, :] == chosen[:, None]).astype(jnp.float32))


def rms_scale(values, gain):
    return values * lax.rsqrt(jnp.mean(values * values, axis=-1, keepdims=True) + NORM_EPS) * gain


def by_rows(left, right):
    return lax.dot_general(
        left, right, (((0,), (0,)), ((), ())), preferred_element_type=jnp.float32
    )


def by_cols(left, right):
    return lax.dot_general(
        left, right, (((1,), (1,)), ((), ())), preferred_element_type=jnp.float32
    )


def adapted(inputs, weight, down_part, up_part, mask):
    inner = (jnp.dot(inputs, down_part, preferred_element_type=jnp.float32) * mask).astype(
        jnp.bfloat16
    )
    return (
        jnp.dot(inputs, weight, preferred_element_type=jnp.float32)
        + jnp.dot(inner, up_part, preferred_element_type=jnp.float32),
        inner,
    )


def adapter_back(grad_out, inputs, inner, up_part, mask):
    grad_up = by_rows(inner, grad_out)
    grad_inner = (by_cols(grad_out, up_part) * mask).astype(jnp.bfloat16)
    return (by_rows(inputs, grad_inner), grad_up, grad_inner)


def owner_of(block, count, width):
    device_of = jnp.where(block < count, block, 2 * count - 1 - block)
    return (device_of, jnp.where(block < count, 0, width))


def key_block(table, first_device, block, count, width):
    device_of, row_in = owner_of(block, count, width)
    piece = lax.dynamic_slice(
        table, (device_of - first_device, row_in, jnp.int32(0)), (1, width, table.shape[2])
    )
    return piece[0]


def block_scores(query, keys, allowed):
    rows = query.shape[0]
    heads = query.reshape(rows, HEADS, HD)
    raw = jnp.einsum(
        "rhd,kd->rhk", heads, keys[:, :HD], preferred_element_type=jnp.float32
    ) * HD ** (-0.5)
    return jnp.where(allowed[:, None, :], raw, MASKED)


def attend_forward(query, keys, allowed):
    scores = block_scores(query, keys, allowed)
    top = jnp.max(scores, axis=-1, keepdims=True)
    total = jnp.sum(jnp.exp(scores - top), axis=-1, keepdims=True)
    log_total = top + jnp.log(total)
    weights = jnp.exp(scores - log_total).astype(jnp.bfloat16)
    mixed = jnp.einsum("rhk,kd->rhd", weights, keys[:, HD:], preferred_element_type=jnp.float32)
    return (mixed.reshape(query.shape[0], -1), log_total)


def attend_backward(query, keys, allowed, log_total, grad_out):
    rows = query.shape[0]
    prob = jnp.exp(block_scores(query, keys, allowed) - log_total)
    grad_heads = grad_out.reshape(rows, HEADS, HD)
    grad_prob = jnp.einsum(
        "rhd,kd->rhk", grad_heads, keys[:, HD:], preferred_element_type=jnp.float32
    )
    delta = jnp.sum(prob * grad_prob, axis=-1, keepdims=True)
    grad_scores = (prob * (grad_prob - delta)).astype(jnp.bfloat16)
    scale = HD ** (-0.5)
    grad_query = (
        jnp.einsum("rhk,kd->rhd", grad_scores, keys[:, :HD], preferred_element_type=jnp.float32)
        * scale
    )
    grad_key = (
        jnp.einsum(
            "rhk,rhd->kd",
            grad_scores,
            query.reshape(rows, HEADS, HD),
            preferred_element_type=jnp.float32,
        )
        * scale
    )
    grad_value = jnp.einsum(
        "rhk,rhd->kd", prob.astype(jnp.bfloat16), grad_heads, preferred_element_type=jnp.float32
    )
    return (grad_query.reshape(rows, -1), jnp.concatenate([grad_key, grad_value], axis=1))


def local_native(
    tokens,
    cotangent,
    doc_lengths,
    adapter_ids,
    w_query,
    w_keyval,
    w_output,
    w_gateup,
    w_down,
    gain_attn,
    gain_mlp,
    query_a,
    query_b,
    keyval_a,
    keyval_b,
    output_a,
    output_b,
    gateup_a,
    gateup_b,
    down_a,
    down_b,
):
    count = lax.axis_size("ctx")
    device = lax.axis_index("ctx")
    local_rows = tokens.shape[0]
    width = local_rows // 2
    reach = (WINDOW + width - 1) // width
    key_width = w_keyval.shape[1]
    half_rows = jnp.arange(width, dtype=jnp.int32)
    own_blocks = (device, 2 * count - 1 - device)
    positions = jnp.concatenate(
        [own_blocks[0] * width + half_rows, own_blocks[1] * width + half_rows]
    )
    segment, mask = adapter_mask(doc_lengths, adapter_ids, positions)
    resid = tokens.astype(jnp.float32)
    act_one = rms_scale(resid, gain_attn).astype(jnp.bfloat16)
    full_query, full_keyval, full_output, full_gateup = (
        lax.all_gather(w_query, "ctx", axis=0, tiled=True),
        lax.all_gather(w_keyval, "ctx", axis=0, tiled=True),
        lax.all_gather(w_output, "ctx", axis=0, tiled=True),
        lax.all_gather(w_gateup, "ctx", axis=0, tiled=True),
    )
    query_full, inner_query = adapted(act_one, full_query, query_a, query_b, mask)
    keyval_full, inner_keyval = adapted(act_one, full_keyval, keyval_a, keyval_b, mask)
    query = query_full.astype(jnp.bfloat16)
    keyval = keyval_full.astype(jnp.bfloat16)
    stacked = [keyval]
    for offset in range(1, reach + 1):
        later = shifted(keyval, "ctx", -offset)
        prior = shifted(keyval, "ctx", offset)
        stacked = [prior] + stacked + [later]
    table = jnp.stack(stacked)
    first_device = device - reach
    kept = []
    mixed_parts = []
    for which in range(2):
        block = own_blocks[which]
        key_blocks = [block - reach + step for step in range(reach + 1)]
        keys = jnp.concatenate(
            [key_block(table, first_device, entry, count, width) for entry in key_blocks], axis=0
        )
        key_pos = jnp.concatenate([entry * width + half_rows for entry in key_blocks])
        key_seg = segment_of(doc_lengths, key_pos)
        query_pos = positions[which * width : (which + 1) * width]
        query_seg = segment[which * width : (which + 1) * width]
        allowed = (
            (key_pos[None, :] <= query_pos[:, None])
            & (query_pos[:, None] - key_pos[None, :] < WINDOW)
            & (key_seg[None, :] == query_seg[:, None])
        )
        mixed, log_total = attend_forward(query[which * width : (which + 1) * width], keys, allowed)
        kept.append((key_blocks, keys, allowed, log_total))
        mixed_parts.append(mixed)
    attention = jnp.concatenate(mixed_parts, axis=0).astype(jnp.bfloat16)
    branch_one, inner_output = adapted(attention, full_output, output_a, output_b, mask)
    middle = resid + branch_one
    act_two = rms_scale(middle, gain_mlp).astype(jnp.bfloat16)
    gate_up, inner_gateup = adapted(act_two, full_gateup, gateup_a, gateup_b, mask)
    gate = gate_up[:, :FF]
    upper = gate_up[:, FF:]
    hidden = (jax.nn.gelu(gate) * upper).astype(jnp.bfloat16)
    down_main = jnp.dot(
        hidden,
        lax.all_gather(w_down, "ctx", axis=0, tiled=True),
        preferred_element_type=jnp.float32,
    )
    inner_down = (jnp.dot(hidden, down_a, preferred_element_type=jnp.float32) * mask).astype(
        jnp.bfloat16
    )
    result = middle + (down_main + jnp.dot(inner_down, down_b, preferred_element_type=jnp.float32))
    grad_down_a, grad_down_b, d_inner_down = adapter_back(
        cotangent, hidden, inner_down, down_b, mask
    )
    grad_hidden = by_cols(cotangent, lax.all_gather(w_down, "ctx", axis=0, tiled=True)) + by_cols(
        d_inner_down, down_a
    )

    def gated(gate_part, up_part):
        return jax.nn.gelu(gate_part) * up_part

    unused, pull_glu = jax.vjp(gated, gate, upper)
    grad_gate, grad_up = pull_glu(grad_hidden)
    grad_gateup = jnp.concatenate([grad_gate, grad_up], axis=1).astype(jnp.bfloat16)
    grad_gateup_a, grad_gateup_b, d_inner_gateup = adapter_back(
        grad_gateup, act_two, inner_gateup, gateup_b, mask
    )
    grad_act_two = by_cols(grad_gateup, full_gateup) + by_cols(d_inner_gateup, gateup_a)
    unused, pull_two = jax.vjp(lambda values: rms_scale(values, gain_mlp), middle)
    grad_middle = cotangent.astype(jnp.float32) + pull_two(grad_act_two)[0]
    grad_branch = grad_middle.astype(jnp.bfloat16)
    grad_output_a, grad_output_b, d_inner_output = adapter_back(
        grad_branch, attention, inner_output, output_b, mask
    )
    grad_attention = (by_cols(grad_branch, full_output) + by_cols(d_inner_output, output_a)).astype(
        jnp.bfloat16
    )
    query_grads = []
    key_grads = []
    for which in range(2):
        key_blocks, keys, allowed, log_total = kept[which]
        rows_query = query[which * width : (which + 1) * width]
        rows_grad = grad_attention[which * width : (which + 1) * width]
        grad_rows, grad_keys = attend_backward(rows_query, keys, allowed, log_total, rows_grad)
        query_grads.append(grad_rows)
        for step, entry in enumerate(key_blocks):
            key_grads.append((entry, grad_keys[step * width : (step + 1) * width]))
    grad_query = jnp.concatenate(query_grads, axis=0).astype(jnp.bfloat16)
    slots = jnp.zeros((2 * reach + 1, local_rows, key_width), jnp.float32)
    for entry, piece in key_grads:
        device_of, row_in = owner_of(entry, count, width)
        slot = device_of - first_device
        current = lax.dynamic_slice(slots, (slot, row_in, jnp.int32(0)), (1, width, key_width))
        slots = lax.dynamic_update_slice(slots, current + piece[None], (slot, row_in, jnp.int32(0)))
    grad_keyval_full = slots[reach]
    for offset in range(1, reach + 1):
        from_lower = shifted(slots[reach + offset].astype(jnp.bfloat16), "ctx", offset).astype(
            jnp.float32
        )
        from_upper = shifted(slots[reach - offset].astype(jnp.bfloat16), "ctx", -offset).astype(
            jnp.float32
        )
        grad_keyval_full = grad_keyval_full + from_lower + from_upper
    grad_keyval = grad_keyval_full.astype(jnp.bfloat16)
    grad_query_a, grad_query_b, d_inner_query = adapter_back(
        grad_query, act_one, inner_query, query_b, mask
    )
    grad_keyval_a, grad_keyval_b, d_inner_keyval = adapter_back(
        grad_keyval, act_one, inner_keyval, keyval_b, mask
    )
    grad_act_one = (
        by_cols(grad_query, full_query)
        + by_cols(grad_keyval, full_keyval)
        + by_cols(d_inner_query, query_a)
        + by_cols(d_inner_keyval, keyval_a)
    )
    unused, pull_one = jax.vjp(lambda values: rms_scale(values, gain_attn), resid)
    grad_tokens = (grad_middle + pull_one(grad_act_one)[0]).astype(jnp.bfloat16)
    sums = lax.psum(
        (
            grad_query_a,
            grad_query_b,
            grad_keyval_a,
            grad_keyval_b,
            grad_output_a,
            grad_output_b,
            grad_gateup_a,
            grad_gateup_b,
            grad_down_a,
            grad_down_b,
        ),
        "ctx",
    )
    return (
        result.astype(jnp.bfloat16),
        grad_tokens,
        sums[0],
        sums[1],
        sums[2],
        sums[3],
        sums[4],
        sums[5],
        sums[6],
        sums[7],
        sums[8],
        sums[9],
    )


def flip(me, bits, b):
    return (me+(1-2*bits[b])*(1<<b),)
CHUNK = 512
UNIT = 256
SUB = 128
GROUP = 4
SCALE = HD ** (-0.5)
LAGS = (0, 2, 4, 6, 8)
SOFT_UNROLL = 8
AHEAD = 18 + LAGS[4]
KEYS_AT = 4 + LAGS[4]
ATT_STEPS = 11


def dot(a, b, dims=NN):
    return lax.dot_general(a, b, dims, preferred_element_type=f32)


def tile_at(i, size):
    return pl.ds(i * size if isinstance(i, int) else pl.multiple_of(i * size, size), size)


def even_odd(par, low, high):
    if par % 2:
        return ((low, 2, ORD_A2), (high, 1, ORD_C2), (high + 1, 1, ORD_B2))
    return ((low, 2, ORD_A), (high, 1, ORD_C), (high + 1, 1, ORD_B))


def bits_of(me):
    return [(me // (1 << b)) % 2 for b in range(5)]


def segment_at(lens_ref, pos):
    start = jnp.int32(0)
    seg = jnp.full(pos.shape, -1, jnp.int32)
    for i in range(lens_ref.shape[0]):
        seg += jnp.where(pos >= start, 1, 0)
        start += lens_ref[i]
    return seg


def mask_at(lens_ref, ids_ref, count, me, rows):
    width = rows // 2
    row = lax.broadcasted_iota(jnp.int32, (rows, ADAPTERS * RANK), 0)
    col = lax.broadcasted_iota(jnp.int32, (rows, ADAPTERS * RANK), 1)
    pos = row + jnp.where(row < width, me * width, (2 * count - 2 - me) * width)
    seg = segment_at(lens_ref, pos)
    chosen = jnp.zeros(pos.shape, jnp.int32)
    for i in range(ids_ref.shape[0]):
        chosen = jnp.where(seg == i, ids_ref[i], chosen)
    return jnp.where(col // RANK == chosen, 1.0, 0.0)


def meet_all(count, me):
    barrier = pltpu.get_barrier_semaphore()

    def greet(k, unused):
        pl.semaphore_signal(
            barrier, 1, device_id=(lax.rem(me + k, count),), device_id_type=MESH
        )
        return unused

    lax.fori_loop(1, count, greet, 0)
    pl.semaphore_wait(barrier, count - 1)


def heads_down(x):
    return jnp.concatenate([x[:, i * HD : (i + 1) * HD] for i in range(x.shape[1] // HD)], axis=0)


def heads_across(x):
    return jnp.concatenate([x[i * SUB : (i + 1) * SUB] for i in range(x.shape[0] // SUB)], axis=1)


def norm_rows(read, gain_ref, write, rows):
    def block(r, unused):
        at = tile_at(r, 16)
        x = read(at)
        scale = lax.rsqrt(jnp.mean(x * x, axis=1, keepdims=True) + NORM_EPS)
        write(at, (x * scale * gain_ref[...][None, :]).astype(bf16))
        return unused

    lax.fori_loop(0, rows // 16, block, 0, unroll=8)


def forward_kernel(
    count,
    x_ref,
    g_ref,
    lens_ref,
    ids_ref,
    gain1_ref,
    gain2_ref,
    qa_ref,
    qb_ref,
    ka_ref,
    kb_ref,
    oa_ref,
    ob_ref,
    ga_ref,
    gb_ref,
    da_ref,
    db_ref,
    wq_own,
    wk_own,
    wo_own,
    wd_own,
    wg_own,
    out_ref,
    dmid_ref,
    a1_ref,
    q_ref,
    keys_ref,
    att_ref,
    iq_ref,
    ik_ref,
    io_ref,
    gga_ref,
    ggb_ref,
    gda_ref,
    gdb_ref,
    prob_hbm,
    wq_all,
    wk_all,
    wo_all,
    wd_all,
    wg_all,
    held_q,
    held_k,
    held_o,
    held_d,
    held_g,
    wbuf,
    dbuf,
    pbuf,
    kv_own,
    a2_s,
    igu_s,
    did_s,
    mask_ref,
    acc_o,
    acc_a,
    gu_s,
    dh_s,
    hid_s,
    dgu_s,
    wsem,
    dsem,
    psem,
    own_sem,
    xsend,
    xrecv,
    hsend,
    hrecv,
):
    rows, d = x_ref.shape
    width = rows // 2
    reach = WINDOW // width
    keys = keys_ref.shape[1]
    span = keys - width + SUB
    ff = da_ref.shape[0]
    nu, nc = ff // UNIT, ff // CHUNK
    me = lax.axis_index("ctx")
    bits = bits_of(me)
    meet_all(count, me)
    here = (bits[4], bits[3], bits[2], bits[1], bits[0])
    own = (wq_own, wk_own, wo_own, wd_own, wg_own)
    held = (held_q, held_k, held_o, held_d, held_g)
    full = (wq_all, wk_all, wo_all, wd_all, wg_all)

    def where(bit_set):
        return tuple(pl.ds(0, 2) if b in bit_set else bits[b] for b in (4, 3, 2, 1, 0))

    def remote(src, dst, send, recv, bit):
        return pltpu.make_async_remote_copy(
            src, dst, send, recv, device_id=flip(me, bits, bit), device_id_type=MESH
        )

    units = []
    for u in range(3):
        units.append((0, 0, even_odd(u, 4 * u, 4 * u + 2)))
    units.append((1, 0, ((0, 1, ORD_A), (1, 1, ORD_C2))))
    for u in range(3):
        units.append((2, 0, even_odd(u, 4 * u, 4 * u + 2)))
    thick = wd_own.shape[0] // 3
    for u in range(9):
        units.append((3, u // 3 * thick, even_odd(u + 1, u % 3 * 4, u % 3 * 4 + 2)))
    first = len(units)

    def exchange(u, cl, k):
        w, row, split = units[u]
        tile, tiles, order = split[cl]
        lines = pl.ds(row, wq_own.shape[0])
        cols = pl.ds(tile * 128, tiles * 128)
        there = full[w].at[where(order[:k]) + (lines, cols)]
        return remote(
            there if k else own[w].at[lines, cols],
            there,
            xsend.at[u, cl, k],
            xrecv.at[u, cl, k],
            order[k],
        )

    def gate(v, par, cl, k):
        tile, tiles, order = even_odd(par, 0, ff // 128)[cl]
        at = tile * 128 + v * UNIT
        cols = pl.ds(at if isinstance(at, int) else pl.multiple_of(at, 128), tiles * 128)
        there = wg_all.at[where(order[:k]) + (slice(None), cols)]
        return remote(
            there if k else wg_own.at[:, cols],
            there,
            xsend.at[first + v, cl, k],
            xrecv.at[first + v, cl, k],
            order[k],
        )

    staged = [pltpu.make_async_copy(own[w], held[w], own_sem.at[w]) for w in range(5)]
    placed = [pltpu.make_async_copy(held[w], full[w].at[here], own_sem.at[w]) for w in range(5)]
    for copy in staged:
        copy.start()
    done_place = set()

    def place(w):
        if w not in done_place:
            done_place.add(w)
            placed[w].wait()

    order = []
    for t in range(AHEAD):
        for k in (4, 3, 2, 1, 0):
            u = t - LAGS[k]
            if 0 <= u < first + nu:
                order.append((t + (4 - k) / 5, u, k))

    def steps(n):
        while order and order[0][0] < n:
            unused, u, k = order.pop(0)
            w = units[u][0] if u < first else 4
            if k:
                place(w)
            for cl in range(2 if w == 1 else 3):
                at = (
                    functools.partial(exchange, u, cl)
                    if u < first
                    else functools.partial(gate, u - first, (u - first) % 2, cl)
                )
                if k:
                    at(k - 1).wait_recv()
                at(k).start()

    def loop_steps(c, point):
        for i in (2 * point, 2 * point + 1):
            t, k = i // 5, 4 - i % 5
            v = 2 * c + t + AHEAD - first - LAGS[k]
            par = (t + AHEAD - first - LAGS[k]) % 2

            @pl.when(v < nu)
            def _(v=v, par=par, k=k):
                for cl in range(3):
                    if k:
                        gate(v, par, cl, k - 1).wait_recv()
                    gate(v, par, cl, k).start()

    def arrived(weight_at):
        for u, unit in enumerate(units):
            if unit[0] == weight_at:
                for cl in range(len(unit[2])):
                    exchange(u, cl, 4).wait_recv()

    def load(w, lo, n, slot, at, sem):
        return pltpu.make_async_copy(
            full[w].at[(slice(None),) * 6 + (pl.ds(lo, n),)],
            wbuf.at[(slot,) + (slice(None),) * 6 + (pl.ds(at, n),)],
            wsem.at[slot, sem],
        )

    def weight(slot, lo, n):
        return wbuf[slot, :, :, :, :, :, :, lo : lo + n].reshape(-1, n)

    for w in range(5):
        staged[w].wait()
        placed[w].start()
    steps(4)
    mask_ref[...] = mask_at(lens_ref, ids_ref, count, me, rows)

    def read_x(at):
        return x_ref[at, :].astype(f32)

    def write_a1(at, y):
        a1_ref[at, :] = y

    norm_rows(read_x, gain1_ref, write_a1, rows)
    iq_ref[...] = (dot(a1_ref[...], qa_ref[...]) * mask_ref[...]).astype(bf16)
    ik_ref[...] = (dot(a1_ref[...], ka_ref[...]) * mask_ref[...]).astype(bf16)
    did_s[...] = (dot(g_ref[...], db_ref[...], NT) * mask_ref[...]).astype(bf16)
    steps(KEYS_AT)
    arrived(0)
    arrived(1)
    loads = [load(0, 0, 1024, 0, 0, 0), load(0, 1024, d - 1024, 1, 0, 0)]
    loads.append(load(1, 0, 2 * HD, 1, d - 1024, 1))
    for copy in loads:
        copy.start()
    for copy in loads:
        copy.wait()

    def beside(a, b):
        return jnp.concatenate([a, b], axis=1)

    def under(a, b):
        return jnp.concatenate([a, b], axis=0)

    kv_own[...] = dot(
        beside(a1_ref[...], ik_ref[...]), under(weight(1, d - 1024, 2 * HD), kb_ref[...])
    ).astype(bf16)
    keys_ref[0, pl.ds(reach * width, width)] = kv_own[pl.ds(0, width)]
    keys_ref[1, pl.ds(reach * width, width)] = kv_own[pl.ds(width, width)]

    def low(j):
        block = me + j
        upper = block // count
        target = block + upper * (2 * count - 1 - 2 * block)
        copy = pltpu.make_async_remote_copy(
            kv_own.at[pl.ds(0, width)],
            keys_ref.at[upper, pl.ds((reach - j) * width, width)],
            hsend.at[0, j],
            hrecv.at[upper, j],
            device_id=(target,),
            device_id_type=MESH,
        )
        return copy, target

    def high(j):
        return pltpu.make_async_remote_copy(
            kv_own.at[pl.ds(width, width)],
            keys_ref.at[1, pl.ds((reach - j) * width, width)],
            hsend.at[1, j],
            hrecv.at[1, j],
            device_id=(me - j,),
            device_id_type=MESH,
        )

    def incoming(which, j):
        return pltpu.make_async_remote_copy(
            kv_own.at[pl.ds(0, width)],
            keys_ref.at[which, pl.ds((reach - j) * width, width)],
            hsend.at[0, j],
            hrecv.at[which, j],
            device_id=flip(me, bits, 0),
            device_id_type=MESH,
        )

    for j in range(1, reach + 1):
        copy, target = low(j)
        pl.when(target != me)(copy.start)
        pl.when(me >= j)(high(j).start)

        @pl.when(target == me)
        def _(j=j):
            keys_ref[1, pl.ds((reach - j) * width, width)] = kv_own[pl.ds(0, width)]

        @pl.when(me < j)
        def _(j=j):
            keys_ref[0, pl.ds((reach - j) * width, width)] = jnp.zeros((width, 2 * HD), bf16)

    steps(KEYS_AT + 1)
    q_ref[:, :1024] = dot(
        beside(a1_ref[...], iq_ref[...]), under(weight(0, 0, 1024), qb_ref[:, :1024])
    ).astype(bf16)
    q_ref[:, 1024:] = dot(
        beside(a1_ref[...], iq_ref[...]), under(weight(1, 0, d - 1024), qb_ref[:, 1024:])
    ).astype(bf16)
    for j in range(1, reach + 1):
        pl.when(me >= j)(incoming(0, j).wait_recv)
        pl.when(2 * me != 2 * count - 1 - j)(incoming(1, j).wait_recv)
    steps(KEYS_AT + 2)

    groups = HEADS // GROUP
    subs = width // SUB
    turn = 0
    for which in range(2):
        for s in range(subs):
            block = me if which == 0 else 2 * count - 1 - me
            base = s * SUB
            lines = slice(which * width + base, which * width + base + SUB)
            row = lax.broadcasted_iota(jnp.int32, (SUB, span), 0)
            col = lax.broadcasted_iota(jnp.int32, (SUB, span), 1)
            ok = (
                (col <= row + (span - SUB))
                & (col > row + (span - SUB - WINDOW))
                & (
                    segment_at(lens_ref, block * width + base + col[:1] - reach * width)
                    == segment_at(lens_ref, block * width + base + row[:, :1])
                )
            )
            acc_a[:SUB, :span] = jnp.where(ok, 0.0, MASKED)

            for g in range(groups):
                heads = slice(g * GROUP * HD, (g + 1) * GROUP * HD)
                k = keys_ref[which, base : base + span, :HD]
                v = keys_ref[which, base : base + span, HD:]
                acc_o[: GROUP * SUB, :span] = dot(heads_down(q_ref[lines, heads]), k, NT)
                slot = turn % 2
                if turn >= 2:
                    pltpu.make_async_copy(
                        pbuf.at[slot], prob_hbm.at[0, 0, pl.ds(0, GROUP * SUB)], psem.at[slot]
                    ).wait()

                def soft(r, unused, slot=slot):
                    at = tile_at(r, 16)
                    bias = acc_a[tile_at(r % (SUB // 16), 16), :span]
                    sc = acc_o[at, :span] * SCALE + bias
                    e = jnp.exp(sc - jnp.max(sc, axis=1, keepdims=True))
                    inv = 1.0 / jnp.sum(e, axis=1, keepdims=True)
                    pbuf[slot, at, :] = (e * inv).astype(bf16)
                    return unused

                lax.fori_loop(0, GROUP * SUB // 16, soft, 0, unroll=SOFT_UNROLL)
                pltpu.make_async_copy(
                    pbuf.at[slot],
                    prob_hbm.at[which, s, pl.ds(g * GROUP * SUB, GROUP * SUB)],
                    psem.at[slot],
                ).start()
                att_ref[lines, heads] = heads_across(dot(pbuf[slot], v)).astype(bf16)
                turn += 1
                steps(KEYS_AT + 2 + ATT_STEPS * turn / (2 * subs * groups))
    for slot in range(2):
        pltpu.make_async_copy(
            pbuf.at[slot], prob_hbm.at[0, 0, pl.ds(0, GROUP * SUB)], psem.at[slot]
        ).wait()
    arrived(2)
    loads = [load(2, 0, 1024, 0, 0, 0), load(2, 1024, d - 1024, 1, 0, 0)]
    for copy in loads:
        copy.start()
    io_ref[...] = (dot(att_ref[...], oa_ref[...]) * mask_ref[...]).astype(bf16)
    for copy in loads:
        copy.wait()
    dmid_ref[:, :1024] = x_ref[:, :1024].astype(f32) + dot(
        beside(att_ref[...], io_ref[...]), under(weight(0, 0, 1024), ob_ref[:, :1024])
    )
    dmid_ref[:, 1024:] = x_ref[:, 1024:].astype(f32) + dot(
        beside(att_ref[...], io_ref[...]), under(weight(1, 0, d - 1024), ob_ref[:, 1024:])
    )
    steps(KEYS_AT + 2 + ATT_STEPS + 1)

    def read_mid(at):
        return dmid_ref[at, :]

    def write_a2(at, y):
        a2_s[at, :] = y

    norm_rows(read_mid, gain2_ref, write_a2, rows)
    igu_s[...] = (dot(a2_s[...], ga_ref[...]) * mask_ref[...]).astype(bf16)
    acc_o[...] = jnp.zeros_like(acc_o)
    acc_a[...] = jnp.zeros_like(acc_a)
    steps(AHEAD)
    arrived(3)

    def arrived_gate(c):
        for j in range(CHUNK // UNIT):
            for cl in range(3):
                gate(c * (CHUNK // UNIT) + j, j % 2, cl, 4).wait_recv()

    def down_rows(c):
        return wd_rows.at[tile_at(c, CHUNK)]

    wd_rows = wd_all.reshape(ff, d)

    def fetch(c, slot):
        cps = [
            pltpu.make_async_copy(
                wg_all.at[(slice(None),) * 6 + (tile_at_base(base, c),)],
                wbuf.at[(slot,) + (slice(None),) * 6 + (pl.ds(o, CHUNK),)],
                wsem.at[slot, i],
            )
            for i, (base, o) in enumerate(((0, 0), (ff, CHUNK)))
        ]
        cps.append(pltpu.make_async_copy(down_rows(c), dbuf.at[slot], dsem.at[slot]))
        return cps

    def tile_at_base(base, c):
        at = base + c * CHUNK
        return pl.ds(at if isinstance(at, int) else pl.multiple_of(at, 128), CHUNK)

    arrived_gate(0)
    for copy in fetch(0, 0):
        copy.start()
    for copy in fetch(0, 0):
        copy.wait()

    def chunk(c, unused):
        slot = c % 2
        loop_steps(c, 0)
        gbc = beside(gb_ref[:, tile_at_base(0, c)], gb_ref[:, tile_at_base(ff, c)])
        dac = da_ref[tile_at(c, CHUNK), :]

        def wx():
            return under(weight(slot, 0, 2 * CHUNK), gbc)

        def wdx():
            return beside(dbuf[slot], dac)

        gu_s[...] = dot(beside(a2_s[...], igu_s[...]), wx())
        loop_steps(c, 1)
        dh_s[...] = dot(beside(g_ref[...], did_s[...]), wdx(), NT)
        k0 = 0.7978845608028654

        def glu(r, unused):
            at = tile_at(r, 16)
            gate_v, up, dh = gu_s[at, :CHUNK], gu_s[at, CHUNK:], dh_s[at, :]
            sq = gate_v * gate_v
            th = jnp.tanh(gate_v * (k0 + (k0 * 0.044715) * sq))
            ht = 0.5 + 0.5 * th
            gl = gate_v * ht
            dgl = ht + (gate_v * (0.5 - 0.5 * th * th)) * (k0 + (3 * k0 * 0.044715) * sq)
            hid_s[at, :] = (gl * up).astype(bf16)
            dgu_s[at, :CHUNK] = (dh * up * dgl).astype(bf16)
            dgu_s[at, CHUNK:] = (dh * gl).astype(bf16)
            return unused

        loop_steps(c, 2)
        lax.fori_loop(0, rows // 16, glu, 0)
        loop_steps(c, 3)
        acc_o[...] += dot(hid_s[...], wdx())
        loop_steps(c, 4)
        gda_ref[tile_at(c, CHUNK), :] = dot(hid_s[...], did_s[...], TN).astype(bf16)
        r = dot(igu_s[...], dgu_s[...], TN).astype(bf16)
        for i in range(2):
            for j in range(CHUNK // 128):
                lo = i * CHUNK + j * 128
                ggb_ref[pl.ds(c * (CHUNK // 128) + (ff // 128) * i + j, 1)] = r[
                    None, :, lo : lo + 128
                ]

        @pl.when(c + 1 < nc)
        def _():
            arrived_gate(c + 1)
            for copy in fetch(c + 1, 1 - slot):
                copy.start()

        acc_a[...] += dot(dgu_s[...], wx(), NT)

        @pl.when(c + 1 < nc)
        def _():
            for copy in fetch(c + 1, 1 - slot):
                copy.wait()

        return unused

    lax.fori_loop(0, nc, chunk, 0)
    inner_d = (acc_o[:, d:] * mask_ref[...]).astype(bf16)
    acc_o[:, :d] += dot(inner_d, db_ref[...])
    r = dot(inner_d, g_ref[...], TN).astype(bf16)
    for j in range(d // 128):
        gdb_ref[j] = r[:, j * 128 : (j + 1) * 128]
    dgu = (acc_a[:, d:] * mask_ref[...]).astype(bf16)
    gga_ref[...] = dot(a2_s[...], dgu, TN).astype(bf16)
    acc_a[:, :d] += dot(dgu, ga_ref[...], NT)

    def finish(r, unused):
        at = tile_at(r, 16)
        mid = dmid_ref[at, :]
        out_ref[at, :] = (mid + acc_o[at, :d]).astype(bf16)
        e = acc_a[at, :d] * gain2_ref[...][None, :]
        rr = lax.rsqrt(jnp.mean(mid * mid, axis=1, keepdims=True) + NORM_EPS)
        pull = (rr * rr * rr) * jnp.mean(e * mid, axis=1, keepdims=True)
        dmid_ref[at, :] = g_ref[at, :].astype(f32) + rr * e - pull * mid
        return unused

    lax.fori_loop(0, rows // 16, finish, 0, unroll=8)
    for j in range(1, reach + 1):
        copy, target = low(j)
        pl.when(target != me)(copy.wait_send)
        pl.when(me >= j)(high(j).wait_send)
    for u, unit in enumerate(units):
        for cl in range(len(unit[2])):
            for k in range(5):
                exchange(u, cl, k).wait_send()

    def sent(v, unused):
        for par in range(2):
            for cl in range(3):
                for k in range(5):
                    gate(2 * v + par, par, cl, k).wait_send()
        return unused

    lax.fori_loop(0, nu // 2, sent, 0)


def forward(count, small, weights):
    x, g = small[0], small[1]
    rows, d = x.shape
    ff = weights[3].shape[0] * count
    width = rows // 2
    keys = WINDOW + width
    span = keys - width + SUB
    nu = ff // UNIT
    S = jax.ShapeDtypeStruct
    full = [S((2,) * 5 + w.shape, bf16) for w in weights]
    outs = [
        S((rows, d), bf16),
        S((rows, d), f32),
        S((rows, d), bf16),
        S((rows, d), bf16),
        S((2, keys, 2 * HD), bf16),
        S((rows, d), bf16),
        S((rows, 128), bf16),
        S((rows, 128), bf16),
        S((rows, 128), bf16),
        S((d, 128), bf16),
        S((2 * ff // 128, 128, 128), bf16),
        S((ff, 128), bf16),
        S((d // 128, 128, 128), bf16),
    ]
    DMA = pltpu.SemaphoreType.DMA
    return pl.pallas_call(
        functools.partial(forward_kernel, count),
        in_specs=[VMEM] * 2 + [SMEM] * 2 + [VMEM] * (len(small) - 4) + [HBM] * 5,
        out_specs=[VMEM] * len(outs) + [HBM] * 6,
        out_shape=outs + [S((2, width // SUB, HEADS * SUB, span), bf16)] + full,
        scratch_shapes=[pltpu.VMEM(w.shape, bf16) for w in weights]
        + [
            pltpu.VMEM((2,) * 6 + (weights[0].shape[0], 2 * CHUNK), bf16),
            pltpu.VMEM((2, CHUNK, d), bf16),
            pltpu.VMEM((2, GROUP * SUB, span), bf16),
            pltpu.VMEM((rows, 2 * HD), bf16),
            pltpu.VMEM((rows, d), bf16),
            pltpu.VMEM((rows, 128), bf16),
            pltpu.VMEM((rows, 128), bf16),
            pltpu.VMEM((rows, 128), f32),
            pltpu.VMEM((rows, d + 128), f32),
            pltpu.VMEM((rows, d + 128), f32),
            pltpu.VMEM((rows, 2 * CHUNK), f32),
            pltpu.VMEM((rows, CHUNK), f32),
            pltpu.VMEM((rows, CHUNK), bf16),
            pltpu.VMEM((rows, 2 * CHUNK), bf16),
            DMA((2, 2)),
            DMA((2,)),
            DMA((2,)),
            DMA((5,)),
            DMA((16 + nu, 3, 5)),
            DMA((16 + nu, 3, 5)),
            DMA((2, 5)),
            DMA((2, 5)),
        ],
        compiler_params=pltpu.CompilerParams(
            collective_id=0, has_side_effects=True, vmem_limit_bytes=63 << 20
        ),
        name="forward",
    )(*small, *weights)


ADVANCE = (6, 11)
POINTS = ()


class Sum:
    def __init__(self, me, buf, parts, send, recv):
        self.me, self.bits = me, bits_of(me)
        self.buf, self.parts, self.send, self.recv = buf, parts, send, recv
        tiles = buf.shape[5] // 16
        third, sixth = round(tiles / 3), round(tiles / 6)
        sizes = (third, third, sixth, tiles - 2 * third - sixth)
        self.split, row = [], 0
        for n, order in zip(sizes, (ORD_A, ORD_A2, ORD_B, ORD_B2)):
            self.split.append((row, n * 16, order))
            row += n * 16
        self.queue = [(s, cl) for s in range(1, 11) for cl in range(4)]

    def copy(self, cl, s):
        row, n, order = self.split[cl]
        lines = pl.ds(row, n)
        bits = self.bits
        if s < 5:
            red = order[::-1]
            bit = red[s]
            rem = [b for b in (4, 3, 2, 1, 0) if b not in red[:s]]
            src = self.buf if s == 0 else self.parts[s - 1]
            idx = tuple((1 - bits[b]) if b == bit else pl.ds(0, 2) for b in rem)
            src = src.at[idx + (lines,)]
            dst = self.parts[s].at[(pl.ds(0, 2),) * (4 - s) + (lines,)]
        else:
            bit, have = order[s - 5], order[: s - 5]
            idx = tuple(pl.ds(0, 2) if b in have else bits[b] for b in (4, 3, 2, 1, 0))
            src = dst = self.buf.at[idx + (lines,)]
        return pltpu.make_async_remote_copy(
            src,
            dst,
            self.send.at[cl, s],
            self.recv.at[cl, s],
            device_id=flip(self.me, bits, bit),
            device_id_type=MESH,
        )

    def add(self, cl, s):
        row, n, order = self.split[cl]
        red = order[::-1]
        rem = [b for b in (4, 3, 2, 1, 0) if b not in red[:s]]
        src, dst = (self.buf if s == 0 else self.parts[s - 1]), self.parts[s]
        lines = pl.ds(row, n)
        free = 4 - s

        def one(j, unused):
            at = [(j // (1 << (free - 1 - i))) % 2 for i in range(free)]
            rest = iter(at)
            idx = tuple(self.bits[b] if b == red[s] else next(rest) for b in rem)
            total = src[idx + (lines,)].astype(f32) + dst[tuple(at) + (lines,)].astype(f32)
            dst[tuple(at) + (lines,)] = total.astype(bf16)
            return unused

        lax.fori_loop(0, 1 << free, one, 0)

    def begin(self):
        for cl in range(4):
            self.copy(cl, 0).start()

    def advance(self, n=4):
        for unused in range(n):
            if not self.queue:
                return
            s, cl = self.queue.pop(0)
            before = self.copy(cl, s - 1)
            before.wait_recv()
            before.wait_send()
            if s <= 5:
                self.add(cl, s - 1)
            if s == 5:
                row, n_, unused_order = self.split[cl]
                b = self.bits
                self.buf[b[4], b[3], b[2], b[1], b[0], pl.ds(row, n_)] = self.parts[4][
                    pl.ds(row, n_)
                ]
            if s < 10:
                self.copy(cl, s).start()


def backward_kernel(
    count,
    dmid_ref,
    x_ref,
    lens_ref,
    ids_ref,
    gain_ref,
    a1_ref,
    q_ref,
    keys_ref,
    att_ref,
    iq_ref,
    ik_ref,
    io_ref,
    qa_ref,
    qb_ref,
    ka_ref,
    kb_ref,
    oa_ref,
    ob_ref,
    gga_hbm,
    ggb_hbm,
    gda_hbm,
    gdb_hbm,
    prob_hbm,
    wq_all,
    wk_all,
    wo_all,
    dx_ref,
    one,
    two,
    pa0,
    pa1,
    pa2,
    pa3,
    pa4,
    pb0,
    pb1,
    pb2,
    pb3,
    pb4,
    mask_ref,
    wbuf,
    pbuf,
    grad_s,
    small_s,
    dkv_s,
    acc,
    hout,
    hin,
    wsem,
    psem,
    gsem,
    send1,
    recv1,
    send2,
    recv2,
    hsend,
    hrecv,
):
    rows, d = x_ref.shape
    width = rows // 2
    reach = WINDOW // width
    keys = keys_ref.shape[1]
    span = keys - width + SUB
    me = lax.axis_index("ctx")
    bits = bits_of(me)
    meet_all(count, me)
    flat_one = one.reshape(-1, 128)
    flat_two = two.reshape(-1, 128)
    hid_rows = gda_hbm.shape[0]
    gates = ggb_hbm.shape[0] * 128
    at_ggb = d
    at_gda = at_ggb + gates
    at_gdb = at_gda + hid_rows
    at_goa = at_gdb + d
    at_gob = at_goa + d
    at_qb, at_ka, at_kb = d, 2 * d, 3 * d

    def whole(ref):
        return ref.at[(slice(None),) * 7]

    loads = [
        pltpu.make_async_copy(wo_all, wbuf.at[(slice(None),) * 6 + (pl.ds(0, d),)], wsem.at[0])
    ]
    grads = [
        pltpu.make_async_copy(src.reshape(-1, 128), flat_one.at[pl.ds(at, n)], gsem.at[i])
        for i, (src, at, n) in enumerate(
            (
                (gga_hbm, 0, d),
                (ggb_hbm, at_ggb, gates),
                (gda_hbm, at_gda, hid_rows),
                (gdb_hbm, at_gdb, d),
            )
        )
    ]
    groups = HEADS // GROUP
    subs = width // SUB
    turns = [(w, s, g) for w in range(2) for s in range(subs) for g in range(groups)]

    def prob(n):
        w, s, g = turns[n]
        return pltpu.make_async_copy(
            prob_hbm.at[w, s, pl.ds(g * GROUP * SUB, GROUP * SUB)], pbuf.at[n % 2], psem.at[n % 2]
        )

    for copy in loads + grads + [prob(0), prob(1)]:
        copy.start()

    def beside(*xs):
        return jnp.concatenate(xs, axis=1)

    def weight(lo, n):
        return wbuf[:, :, :, :, :, :, lo : lo + n].reshape(-1, n)

    def store_tiles(flat, at, x):
        for j in range(x.shape[1] // 128):
            flat[pl.ds(at + j * 128, 128)] = x[:, j * 128 : (j + 1) * 128].astype(bf16)

    mask_ref[...] = mask_at(lens_ref, ids_ref, count, me, rows)
    grad_s[...] = dmid_ref[...].astype(bf16)
    small_s[:, :128] = (dot(grad_s[...], ob_ref[...], NT) * mask_ref[...]).astype(bf16)
    flat_one[pl.ds(at_goa, d)] = dot(att_ref[...], small_s[:, :128], TN).astype(bf16)
    store_tiles(flat_one, at_gob, dot(io_ref[...], grad_s[...], TN))
    for copy in grads:
        copy.wait()
    first = Sum(me, one, (pa0, pa1, pa2, pa3, pa4), send1, recv1)
    second = Sum(me, two, (pb0, pb1, pb2, pb3, pb4), send2, recv2)
    first.begin()
    for copy in loads:
        copy.wait()
    acc[:, :d] = dot(
        beside(grad_s[...], small_s[:, :128]), beside(weight(0, d), oa_ref[...]), NT
    )
    grad_s[...] = acc[:, :d].astype(bf16)
    loads = [
        pltpu.make_async_copy(wq_all, wbuf.at[(slice(None),) * 6 + (pl.ds(0, d),)], wsem.at[0]),
        pltpu.make_async_copy(
            wk_all, wbuf.at[(slice(None),) * 6 + (pl.ds(d, 2 * HD),)], wsem.at[1]
        ),
    ]
    for copy in loads:
        copy.start()
    dkv_s[...] = jnp.zeros_like(dkv_s)
    first.advance()

    for n, (which, s, g) in enumerate(turns):
        base = s * SUB
        lines = slice(which * width + base, which * width + base + SUB)
        heads = slice(g * GROUP * HD, (g + 1) * GROUP * HD)
        k = keys_ref[which, base : base + span, :HD]
        v = keys_ref[which, base : base + span, HD:]
        q = heads_down(q_ref[lines, heads])
        do = heads_down(grad_s[lines, heads])
        o = heads_down(att_ref[lines, heads])
        delta = jnp.sum(do.astype(f32) * o.astype(f32), axis=1, keepdims=True)
        prob(n).wait()
        p = pbuf[n % 2]
        ds = (p.astype(f32) * (dot(do, v, NT) - delta)).astype(bf16)
        dkv_s[which, HD:, base : base + span] += dot(do.T, p)
        dkv_s[which, :HD, base : base + span] += dot(q.T, ds) * SCALE
        grad_s[lines, heads] = heads_across(dot(ds, k) * SCALE).astype(bf16)
        if n + 2 < len(turns):
            prob(n + 2).start()
        if n in ADVANCE:
            first.advance()

    def piece(which, j):
        lo = (reach - j) * width
        return dkv_s[which, :, lo : lo + width].T

    for j in range(1, reach + 1):
        for which in range(2):
            hout[which, j - 1] = piece(which, j).astype(bf16)

    def low(j):
        return pltpu.make_async_remote_copy(
            hout.at[0, j - 1],
            hin.at[0, j - 1],
            hsend.at[0, j],
            hrecv.at[0, j],
            device_id=(me - j,),
            device_id_type=MESH,
        )

    def high(j):
        block = 2 * count - 1 - me - j
        upper = block // count
        target = block + upper * (2 * count - 1 - 2 * block)
        copy = pltpu.make_async_remote_copy(
            hout.at[1, j - 1],
            hin.at[upper, j - 1],
            hsend.at[1, j],
            hrecv.at[upper, j],
            device_id=(target,),
            device_id_type=MESH,
        )
        return copy, target

    def incoming(half, j):
        return pltpu.make_async_remote_copy(
            hout.at[0, j - 1],
            hin.at[half, j - 1],
            hsend.at[0, j],
            hrecv.at[half, j],
            device_id=flip(me, bits, 0),
            device_id_type=MESH,
        )

    for j in range(1, reach + 1):
        pl.when(me >= j)(low(j).start)
        copy, target = high(j)
        pl.when(target != me)(copy.start)
    if 1 in POINTS:
        first.advance()
    small_s[:, :128] = (dot(grad_s[...], qb_ref[...], NT) * mask_ref[...]).astype(bf16)
    flat_two[pl.ds(0, d)] = dot(a1_ref[...], small_s[:, :128], TN).astype(bf16)
    store_tiles(flat_two, at_qb, dot(iq_ref[...], grad_s[...], TN))
    used = 3 * d + 2 * HD
    spare = flat_two.shape[0] - used
    flat_two[pl.ds(used, spare)] = jnp.zeros((spare, 128), bf16)
    first.advance()
    for half in range(2):
        own = dkv_s[half, :, reach * width :].T
        acc[half * width : (half + 1) * width, : 2 * HD] = own
    for j in range(1, reach + 1):
        lower_self = 2 * me == 2 * count - 1 - j

        @pl.when(jnp.logical_not(lower_self))
        def _(j=j):
            incoming(0, j).wait_recv()
            acc[:width, : 2 * HD] += hin[0, j - 1].astype(f32)

        @pl.when(lower_self)
        def _(j=j):
            acc[:width, : 2 * HD] += hout[1, j - 1].astype(f32)

        @pl.when(me >= j)
        def _(j=j):
            incoming(1, j).wait_recv()
            acc[width:, : 2 * HD] += hin[1, j - 1].astype(f32)

    if 2 in POINTS:
        first.advance()
    small_s[:, 128 : 128 + 2 * HD] = acc[:, : 2 * HD].astype(bf16)
    dkv = small_s[:, 128 : 128 + 2 * HD]
    small_s[:, 128 + 2 * HD :] = (dot(dkv, kb_ref[...], NT) * mask_ref[...]).astype(bf16)
    flat_two[pl.ds(at_ka, d)] = dot(a1_ref[...], small_s[:, 128 + 2 * HD :], TN).astype(bf16)
    store_tiles(flat_two, at_kb, dot(ik_ref[...], small_s[:, 128 : 128 + 2 * HD], TN))
    second.begin()
    first.advance()
    for copy in loads:
        copy.wait()
    acc[:, :d] = dot(
        beside(grad_s[...], small_s[...]),
        beside(weight(0, d), qa_ref[...], weight(d, 2 * HD), ka_ref[...]),
        NT,
    )
    second.advance()
    first.advance()

    def finish(r, unused):
        at = tile_at(r, 16)
        x = x_ref[at, :].astype(f32)
        e = acc[at, :d] * gain_ref[...][None, :]
        rr = lax.rsqrt(jnp.mean(x * x, axis=1, keepdims=True) + NORM_EPS)
        pull = (rr * rr * rr) * jnp.mean(e * x, axis=1, keepdims=True)
        dx_ref[at, :] = (dmid_ref[at, :] + rr * e - pull * x).astype(bf16)
        return unused

    lax.fori_loop(0, rows // 16, finish, 0, unroll=8)
    while first.queue:
        second.advance()
        first.advance()

    second.advance(40)
    for j in range(1, reach + 1):
        pl.when(me >= j)(low(j).wait_send)
        copy, target = high(j)
        pl.when(target != me)(copy.wait_send)


def backward(count, small, large):
    rows, d = small[0].shape
    gates, hid = large[1].shape[0] * 128, large[2].shape[0]
    keys = small[7].shape[1]
    span = keys - rows // 2 + SUB
    one = (2 * d + gates + hid + 2 * d) // 32
    two = -(-(3 * d + 2 * HD) // 512) * 16
    S = jax.ShapeDtypeStruct
    V = pltpu.VMEM
    DMA = pltpu.SemaphoreType.DMA
    five = (2,) * 5
    outs = [S((rows, d), bf16), S(five + (one, 128), bf16), S(five + (two, 128), bf16)]
    return pl.pallas_call(
        functools.partial(backward_kernel, count),
        in_specs=[VMEM] * 2 + [SMEM] * 2 + [VMEM] * (len(small) - 4) + [HBM] * len(large),
        out_specs=[VMEM] * len(outs),
        out_shape=outs,
        scratch_shapes=[V((2,) * (4 - s) + (one, 128), bf16) for s in range(5)]
        + [V((2,) * (4 - s) + (two, 128), bf16) for s in range(5)]
        + [
            V((rows, 128), f32),
            V(five + (d // 32, d + 2 * HD), bf16),
            V((2, GROUP * SUB, span), bf16),
            V((rows, d), bf16),
            V((rows, 256 + 2 * HD), bf16),
            V((2, 2 * HD, keys), f32),
            V((rows, d), f32),
            V((2, 4, rows // 2, 2 * HD), bf16),
            V((2, 4, rows // 2, 2 * HD), bf16),
            DMA((2,)),
            DMA((2,)),
            DMA((4,)),
            DMA((4, 10)),
            DMA((4, 10)),
            DMA((4, 10)),
            DMA((4, 10)),
            DMA((2, 5)),
            DMA((2, 5)),
        ],
        compiler_params=pltpu.CompilerParams(
            collective_id=1, has_side_effects=True, vmem_limit_bytes=63 << 20
        ),
        name="backward",
    )(*small, *large)


def unpack_kernel(places, one_hbm, two_hbm, *refs):
    n = len(places)
    outs, ins, wide = refs[:n], refs[n : 2 * n], refs[2 * n : 3 * n]
    in_sem, out_sem = refs[3 * n :]
    flat = [one_hbm.reshape(-1, 128), two_hbm.reshape(-1, 128)]
    reads = [
        pltpu.make_async_copy(flat[w].at[pl.ds(at, ins[i].shape[0])], ins[i], in_sem.at[i])
        for i, (w, at, tiled) in enumerate(places)
    ]
    writes = [pltpu.make_async_copy(wide[i], outs[i], out_sem.at[i]) for i in range(n)]
    for copy in reads:
        copy.start()
    for i, (w, at, tiled) in enumerate(places):
        reads[i].wait()
        if tiled:
            for j in range(wide[i].shape[1] // 128):
                wide[i][:, j * 128 : (j + 1) * 128] = ins[i][pl.ds(j * 128, 128)].astype(f32)
        else:
            wide[i][...] = ins[i][...].astype(f32)
        writes[i].start()
    for copy in writes:
        copy.wait()


def unpack(one, two, shapes, places):
    rows = [a * b // 128 for a, b in shapes]
    n = len(shapes)
    return pl.pallas_call(
        functools.partial(unpack_kernel, places),
        in_specs=[HBM] * 2,
        out_specs=[HBM] * n,
        out_shape=[jax.ShapeDtypeStruct(s, f32) for s in shapes],
        scratch_shapes=[pltpu.VMEM((r, 128), bf16) for r in rows]
        + [pltpu.VMEM(s, f32) for s in shapes]
        + [pltpu.SemaphoreType.DMA((n,)), pltpu.SemaphoreType.DMA((n,))],
        compiler_params=pltpu.CompilerParams(vmem_limit_bytes=40 << 20),
        name="unpack",
    )(one, two)


def local_own(
    tokens,
    cotangent,
    doc_lengths,
    adapter_ids,
    w_query,
    w_keyval,
    w_output,
    w_gateup,
    w_down,
    gain_attn,
    gain_mlp,
    query_a,
    query_b,
    keyval_a,
    keyval_b,
    output_a,
    output_b,
    gateup_a,
    gateup_b,
    down_a,
    down_b,
):
    count = lax.axis_size("ctx")
    (
        result,
        grad_middle,
        act_one,
        query,
        keys,
        attention,
        inner_query,
        inner_keyval,
        inner_output,
        g_gateup_a,
        g_gateup_b,
        g_down_a,
        g_down_b,
        prob,
        full_query,
        full_keyval,
        full_output,
        unused_down,
        unused_gateup,
    ) = forward(
        count,
        (
            tokens,
            cotangent,
            doc_lengths,
            adapter_ids,
            gain_attn,
            gain_mlp,
            query_a,
            query_b,
            keyval_a,
            keyval_b,
            output_a,
            output_b,
            gateup_a,
            gateup_b,
            down_a,
            down_b,
        ),
        (w_query, w_keyval, w_output, w_down, w_gateup),
    )
    grad_tokens, first, second = backward(
        count,
        (
            grad_middle,
            tokens,
            doc_lengths,
            adapter_ids,
            gain_attn,
            act_one,
            query,
            keys,
            attention,
            inner_query,
            inner_keyval,
            inner_output,
            query_a,
            query_b,
            keyval_a,
            keyval_b,
            output_a,
            output_b,
        ),
        (
            g_gateup_a,
            g_gateup_b,
            g_down_a,
            g_down_b,
            prob,
            full_query,
            full_keyval,
            full_output,
        ),
    )
    d, hid, gates = w_output.shape[1], down_a.shape[0], gateup_b.shape[1]
    kv = w_keyval.shape[1]
    shapes = [(d, 128), (128, d), (d, 128), (128, kv), (d, 128), (128, d)]
    shapes += [(d, 128), (128, gates), (hid, 128), (128, d)]
    places = [
        (1, 0, False),
        (1, d, True),
        (1, 2 * d, False),
        (1, 3 * d, True),
        (0, 2 * d + gates + hid, False),
        (0, 3 * d + gates + hid, True),
        (0, 0, False),
        (0, d, True),
        (0, d + gates, False),
        (0, d + gates + hid, True),
    ]
    sums = unpack(first, second, shapes, places)
    return (result, grad_tokens, *sums)


def solution(mesh):
    in_specs = (
        P("ctx", None),
        P("ctx", None),
        P(),
        P(),
        P("ctx", None),
        P("ctx", None),
        P("ctx", None),
        P("ctx", None),
        P("ctx", None),
        P(),
        P(),
        P(),
        P(),
        P(),
        P(),
        P(),
        P(),
        P(),
        P(),
        P(),
        P(),
    )
    out_specs = (P("ctx", None), P("ctx", None), P(), P(), P(), P(), P(), P(), P(), P(), P(), P())
    local = local_own if mesh.shape["ctx"] == 32 else local_native
    return jax.shard_map(local, mesh=mesh, in_specs=in_specs, out_specs=out_specs, check_vma=False)
```

```python
import functools

import jax
import jax.numpy as jnp
from jax import lax
from jax.experimental import pallas as pl
from jax.experimental.pallas import tpu as pltpu
from jax.sharding import PartitionSpec as P

HEADS = 12
HD = 128
FF = 4608
WINDOW = 1024
RANK = 16
ADAPTERS = 8


NORM_EPS = 1e-06
MASKED = -1e30


MESH = pl.DeviceIdType.MESH
bf16 = jnp.bfloat16
f32 = jnp.float32
NN = (((1,), (0,)), ((), ()))
NT = (((1,), (1,)), ((), ()))
TN = (((0,), (0,)), ((), ()))
VMEM = pl.BlockSpec(memory_space=pltpu.VMEM)
HBM = pl.BlockSpec(memory_space=pl.ANY)
SMEM = pl.BlockSpec(memory_space=pltpu.SMEM)
ORD_A = (4, 3, 1, 2, 0)
ORD_A2 = (4, 3, 2, 1, 0)
ORD_B = (4, 1, 2, 3, 0)
ORD_B2 = (4, 2, 1, 3, 0)
ORD_C = (4, 2, 3, 1, 0)
ORD_C2 = (4, 1, 3, 2, 0)


def shifted(x, axis, by):
    size = lax.axis_size(axis)
    pairs = [(i, i + by) for i in range(size) if 0 <= i + by < size]
    return lax.ppermute(x, axis, pairs)


def segment_of(doc_lengths, positions):
    starts = jnp.cumsum(doc_lengths) - doc_lengths
    return jnp.sum((starts[None, :] <= positions[:, None]).astype(jnp.int32), axis=1) - 1


def adapter_mask(doc_lengths, adapter_ids, positions):
    segment = segment_of(doc_lengths, positions)
    owner = segment[:, None] == jnp.arange(doc_lengths.shape[0], dtype=jnp.int32)[None, :]
    chosen = jnp.sum(jnp.where(owner, adapter_ids[None, :], 0), axis=1)
    columns = jnp.arange(ADAPTERS * RANK, dtype=jnp.int32) // RANK
    return (segment, (columns[None, :] == chosen[:, None]).astype(jnp.float32))


def rms_scale(values, gain):
    return values * lax.rsqrt(jnp.mean(values * values, axis=-1, keepdims=True) + NORM_EPS) * gain


def by_rows(left, right):
    return lax.dot_general(
        left, right, (((0,), (0,)), ((), ())), preferred_element_type=jnp.float32
    )


def by_cols(left, right):
    return lax.dot_general(
        left, right, (((1,), (1,)), ((), ())), preferred_element_type=jnp.float32
    )


def adapted(inputs, weight, down_part, up_part, mask):
    inner = (jnp.dot(inputs, down_part, preferred_element_type=jnp.float32) * mask).astype(
        jnp.bfloat16
    )
    return (
        jnp.dot(inputs, weight, preferred_element_type=jnp.float32)
        + jnp.dot(inner, up_part, preferred_element_type=jnp.float32),
        inner,
    )


def adapter_back(grad_out, inputs, inner, up_part, mask):
    grad_up = by_rows(inner, grad_out)
    grad_inner = (by_cols(grad_out, up_part) * mask).astype(jnp.bfloat16)
    return (by_rows(inputs, grad_inner), grad_up, grad_inner)


def owner_of(block, count, width):
    device_of = jnp.where(block < count, block, 2 * count - 1 - block)
    return (device_of, jnp.where(block < count, 0, width))


def key_block(table, first_device, block, count, width):
    device_of, row_in = owner_of(block, count, width)
    piece = lax.dynamic_slice(
        table, (device_of - first_device, row_in, jnp.int32(0)), (1, width, table.shape[2])
    )
    return piece[0]


def block_scores(query, keys, allowed):
    rows = query.shape[0]
    heads = query.reshape(rows, HEADS, HD)
    raw = jnp.einsum(
        "rhd,kd->rhk", heads, keys[:, :HD], preferred_element_type=jnp.float32
    ) * HD ** (-0.5)
    return jnp.where(allowed[:, None, :], raw, MASKED)


def attend_forward(query, keys, allowed):
    scores = block_scores(query, keys, allowed)
    top = jnp.max(scores, axis=-1, keepdims=True)
    total = jnp.sum(jnp.exp(scores - top), axis=-1, keepdims=True)
    log_total = top + jnp.log(total)
    weights = jnp.exp(scores - log_total).astype(jnp.bfloat16)
    mixed = jnp.einsum("rhk,kd->rhd", weights, keys[:, HD:], preferred_element_type=jnp.float32)
    return (mixed.reshape(query.shape[0], -1), log_total)


def attend_backward(query, keys, allowed, log_total, grad_out):
    rows = query.shape[0]
    prob = jnp.exp(block_scores(query, keys, allowed) - log_total)
    grad_heads = grad_out.reshape(rows, HEADS, HD)
    grad_prob = jnp.einsum(
        "rhd,kd->rhk", grad_heads, keys[:, HD:], preferred_element_type=jnp.float32
    )
    delta = jnp.sum(prob * grad_prob, axis=-1, keepdims=True)
    grad_scores = (prob * (grad_prob - delta)).astype(jnp.bfloat16)
    scale = HD ** (-0.5)
    grad_query = (
        jnp.einsum("rhk,kd->rhd", grad_scores, keys[:, :HD], preferred_element_type=jnp.float32)
        * scale
    )
    grad_key = (
        jnp.einsum(
            "rhk,rhd->kd",
            grad_scores,
            query.reshape(rows, HEADS, HD),
            preferred_element_type=jnp.float32,
        )
        * scale
    )
    grad_value = jnp.einsum(
        "rhk,rhd->kd", prob.astype(jnp.bfloat16), grad_heads, preferred_element_type=jnp.float32
    )
    return (grad_query.reshape(rows, -1), jnp.concatenate([grad_key, grad_value], axis=1))


def local_native(
    tokens,
    cotangent,
    doc_lengths,
    adapter_ids,
    w_query,
    w_keyval,
    w_output,
    w_gateup,
    w_down,
    gain_attn,
    gain_mlp,
    query_a,
    query_b,
    keyval_a,
    keyval_b,
    output_a,
    output_b,
    gateup_a,
    gateup_b,
    down_a,
    down_b,
):
    count = lax.axis_size("ctx")
    device = lax.axis_index("ctx")
    local_rows = tokens.shape[0]
    width = local_rows // 2
    reach = (WINDOW + width - 1) // width
    key_width = w_keyval.shape[1]
    half_rows = jnp.arange(width, dtype=jnp.int32)
    own_blocks = (device, 2 * count - 1 - device)
    positions = jnp.concatenate(
        [own_blocks[0] * width + half_rows, own_blocks[1] * width + half_rows]
    )
    segment, mask = adapter_mask(doc_lengths, adapter_ids, positions)
    resid = tokens.astype(jnp.float32)
    act_one = rms_scale(resid, gain_attn).astype(jnp.bfloat16)
    full_query, full_keyval, full_output, full_gateup = (
        lax.all_gather(w_query, "ctx", axis=0, tiled=True),
        lax.all_gather(w_keyval, "ctx", axis=0, tiled=True),
        lax.all_gather(w_output, "ctx", axis=0, tiled=True),
        lax.all_gather(w_gateup, "ctx", axis=0, tiled=True),
    )
    query_full, inner_query = adapted(act_one, full_query, query_a, query_b, mask)
    keyval_full, inner_keyval = adapted(act_one, full_keyval, keyval_a, keyval_b, mask)
    query = query_full.astype(jnp.bfloat16)
    keyval = keyval_full.astype(jnp.bfloat16)
    stacked = [keyval]
    for offset in range(1, reach + 1):
        later = shifted(keyval, "ctx", -offset)
        prior = shifted(keyval, "ctx", offset)
        stacked = [prior] + stacked + [later]
    table = jnp.stack(stacked)
    first_device = device - reach
    kept = []
    mixed_parts = []
    for which in range(2):
        block = own_blocks[which]
        key_blocks = [block - reach + step for step in range(reach + 1)]
        keys = jnp.concatenate(
            [key_block(table, first_device, entry, count, width) for entry in key_blocks], axis=0
        )
        key_pos = jnp.concatenate([entry * width + half_rows for entry in key_blocks])
        key_seg = segment_of(doc_lengths, key_pos)
        query_pos = positions[which * width : (which + 1) * width]
        query_seg = segment[which * width : (which + 1) * width]
        allowed = (
            (key_pos[None, :] <= query_pos[:, None])
            & (query_pos[:, None] - key_pos[None, :] < WINDOW)
            & (key_seg[None, :] == query_seg[:, None])
        )
        mixed, log_total = attend_forward(query[which * width : (which + 1) * width], keys, allowed)
        kept.append((key_blocks, keys, allowed, log_total))
        mixed_parts.append(mixed)
    attention = jnp.concatenate(mixed_parts, axis=0).astype(jnp.bfloat16)
    branch_one, inner_output = adapted(attention, full_output, output_a, output_b, mask)
    middle = resid + branch_one
    act_two = rms_scale(middle, gain_mlp).astype(jnp.bfloat16)
    gate_up, inner_gateup = adapted(act_two, full_gateup, gateup_a, gateup_b, mask)
    gate = gate_up[:, :FF]
    upper = gate_up[:, FF:]
    hidden = (jax.nn.gelu(gate) * upper).astype(jnp.bfloat16)
    down_main = jnp.dot(
        hidden,
        lax.all_gather(w_down, "ctx", axis=0, tiled=True),
        preferred_element_type=jnp.float32,
    )
    inner_down = (jnp.dot(hidden, down_a, preferred_element_type=jnp.float32) * mask).astype(
        jnp.bfloat16
    )
    result = middle + (down_main + jnp.dot(inner_down, down_b, preferred_element_type=jnp.float32))
    grad_down_a, grad_down_b, d_inner_down = adapter_back(
        cotangent, hidden, inner_down, down_b, mask
    )
    grad_hidden = by_cols(cotangent, lax.all_gather(w_down, "ctx", axis=0, tiled=True)) + by_cols(
        d_inner_down, down_a
    )

    def gated(gate_part, up_part):
        return jax.nn.gelu(gate_part) * up_part

    unused, pull_glu = jax.vjp(gated, gate, upper)
    grad_gate, grad_up = pull_glu(grad_hidden)
    grad_gateup = jnp.concatenate([grad_gate, grad_up], axis=1).astype(jnp.bfloat16)
    grad_gateup_a, grad_gateup_b, d_inner_gateup = adapter_back(
        grad_gateup, act_two, inner_gateup, gateup_b, mask
    )
    grad_act_two = by_cols(grad_gateup, full_gateup) + by_cols(d_inner_gateup, gateup_a)
    unused, pull_two = jax.vjp(lambda values: rms_scale(values, gain_mlp), middle)
    grad_middle = cotangent.astype(jnp.float32) + pull_two(grad_act_two)[0]
    grad_branch = grad_middle.astype(jnp.bfloat16)
    grad_output_a, grad_output_b, d_inner_output = adapter_back(
        grad_branch, attention, inner_output, output_b, mask
    )
    grad_attention = (by_cols(grad_branch, full_output) + by_cols(d_inner_output, output_a)).astype(
        jnp.bfloat16
    )
    query_grads = []
    key_grads = []
    for which in range(2):
        key_blocks, keys, allowed, log_total = kept[which]
        rows_query = query[which * width : (which + 1) * width]
        rows_grad = grad_attention[which * width : (which + 1) * width]
        grad_rows, grad_keys = attend_backward(rows_query, keys, allowed, log_total, rows_grad)
        query_grads.append(grad_rows)
        for step, entry in enumerate(key_blocks):
            key_grads.append((entry, grad_keys[step * width : (step + 1) * width]))
    grad_query = jnp.concatenate(query_grads, axis=0).astype(jnp.bfloat16)
    slots = jnp.zeros((2 * reach + 1, local_rows, key_width), jnp.float32)
    for entry, piece in key_grads:
        device_of, row_in = owner_of(entry, count, width)
        slot = device_of - first_device
        current = lax.dynamic_slice(slots, (slot, row_in, jnp.int32(0)), (1, width, key_width))
        slots = lax.dynamic_update_slice(slots, current + piece[None], (slot, row_in, jnp.int32(0)))
    grad_keyval_full = slots[reach]
    for offset in range(1, reach + 1):
        from_lower = shifted(slots[reach + offset].astype(jnp.bfloat16), "ctx", offset).astype(
            jnp.float32
        )
        from_upper = shifted(slots[reach - offset].astype(jnp.bfloat16), "ctx", -offset).astype(
            jnp.float32
        )
        grad_keyval_full = grad_keyval_full + from_lower + from_upper
    grad_keyval = grad_keyval_full.astype(jnp.bfloat16)
    grad_query_a, grad_query_b, d_inner_query = adapter_back(
        grad_query, act_one, inner_query, query_b, mask
    )
    grad_keyval_a, grad_keyval_b, d_inner_keyval = adapter_back(
        grad_keyval, act_one, inner_keyval, keyval_b, mask
    )
    grad_act_one = (
        by_cols(grad_query, full_query)
        + by_cols(grad_keyval, full_keyval)
        + by_cols(d_inner_query, query_a)
        + by_cols(d_inner_keyval, keyval_a)
    )
    unused, pull_one = jax.vjp(lambda values: rms_scale(values, gain_attn), resid)
    grad_tokens = (grad_middle + pull_one(grad_act_one)[0]).astype(jnp.bfloat16)
    sums = lax.psum(
        (
            grad_query_a,
            grad_query_b,
            grad_keyval_a,
            grad_keyval_b,
            grad_output_a,
            grad_output_b,
            grad_gateup_a,
            grad_gateup_b,
            grad_down_a,
            grad_down_b,
        ),
        "ctx",
    )
    return (
        result.astype(jnp.bfloat16),
        grad_tokens,
        sums[0],
        sums[1],
        sums[2],
        sums[3],
        sums[4],
        sums[5],
        sums[6],
        sums[7],
        sums[8],
        sums[9],
    )


def flip(me, bits, b):
    return (me+(1-2*bits[b])*(1<<b),)
CHUNK = 512
UNIT = 256
SUB = 128
GROUP = 4
SCALE = HD ** (-0.5)
LAGS = (0, 2, 4, 6, 8)
SOFT_UNROLL = 8
AHEAD = 18 + LAGS[4]
KEYS_AT = 4 + LAGS[4]
ATT_STEPS = 11


def dot(a, b, dims=NN):
    return lax.dot_general(a, b, dims, preferred_element_type=f32)


def tile_at(i, size):
    return pl.ds(i * size if isinstance(i, int) else pl.multiple_of(i * size, size), size)


def even_odd(par, low, high):
    if par % 2:
        return ((low, 2, ORD_A2), (high, 1, ORD_C2), (high + 1, 1, ORD_B2))
    return ((low, 2, ORD_A), (high, 1, ORD_C), (high + 1, 1, ORD_B))


def bits_of(me):
    return [(me // (1 << b)) % 2 for b in range(5)]


def segment_at(lens_ref, pos):
    start = jnp.int32(0)
    seg = jnp.full(pos.shape, -1, jnp.int32)
    for i in range(lens_ref.shape[0]):
        seg += jnp.where(pos >= start, 1, 0)
        start += lens_ref[i]
    return seg


def mask_at(lens_ref, ids_ref, count, me, rows):
    width = rows // 2
    row = lax.broadcasted_iota(jnp.int32, (rows, ADAPTERS * RANK), 0)
    col = lax.broadcasted_iota(jnp.int32, (rows, ADAPTERS * RANK), 1)
    pos = row + jnp.where(row < width, me * width, (2 * count - 2 - me) * width)
    seg = segment_at(lens_ref, pos)
    chosen = jnp.zeros(pos.shape, jnp.int32)
    for i in range(ids_ref.shape[0]):
        chosen = jnp.where(seg == i, ids_ref[i], chosen)
    return jnp.where(col // RANK == chosen, 1.0, 0.0)


def meet_all(count, me):
    barrier = pltpu.get_barrier_semaphore()

    def greet(k, unused):
        pl.semaphore_signal(
            barrier, 1, device_id=(lax.rem(me + k, count),), device_id_type=MESH
        )
        return unused

    lax.fori_loop(1, count, greet, 0)
    pl.semaphore_wait(barrier, count - 1)


def heads_down(x):
    return jnp.concatenate([x[:, i * HD : (i + 1) * HD] for i in range(x.shape[1] // HD)], axis=0)


def heads_across(x):
    return jnp.concatenate([x[i * SUB : (i + 1) * SUB] for i in range(x.shape[0] // SUB)], axis=1)


def norm_rows(read, gain_ref, write, rows):
    def block(r, unused):
        at = tile_at(r, 16)
        x = read(at)
        scale = lax.rsqrt(jnp.mean(x * x, axis=1, keepdims=True) + NORM_EPS)
        write(at, (x * scale * gain_ref[...][None, :]).astype(bf16))
        return unused

    lax.fori_loop(0, rows // 16, block, 0, unroll=8)


def forward_kernel(
    count,
    x_ref,
    g_ref,
    lens_ref,
    ids_ref,
    gain1_ref,
    gain2_ref,
    qa_ref,
    qb_ref,
    ka_ref,
    kb_ref,
    oa_ref,
    ob_ref,
    ga_ref,
    gb_hbm,
    da_hbm,
    db_ref,
    wq_own,
    wk_own,
    wo_own,
    wd_own,
    wg_own,
    out_ref,
    dmid_ref,
    a1_hbm,
    q_hbm,
    keys_hbm,
    att_hbm,
    iq_ref,
    ik_ref,
    io_ref,
    gga_ref,
    ggb_ref,
    gda_ref,
    gdb_ref,
    prob_hbm,
    wq_all,
    wk_all,
    wo_all,
    wd_all,
    wg_all,
    held_q,
    held_k,
    held_o,
    held_d,
    held_g,
    wbuf,
    dbuf,
    pbuf,
    kv_own,
    a2_s,
    igu_s,
    did_s,
    a1_ref,
    q_ref,
    keys_ref,
    att_ref,
    gb_ref,
    da_ref,
    mask_ref,
    acc_o,
    acc_a,
    gu_s,
    dh_s,
    hid_s,
    dgu_s,
    wsem,
    dsem,
    psem,
    own_sem,
    xsend,
    xrecv,
    hsend,
    hrecv,
    late_sem,
):
    rows, d = x_ref.shape
    width = rows // 2
    reach = WINDOW // width
    keys = keys_ref.shape[1]
    span = keys - width + SUB
    ff = da_hbm.shape[0]
    nu, nc = ff // UNIT, ff // CHUNK
    me = lax.axis_index("ctx")
    bits = bits_of(me)
    meet_all(count, me)
    here = (bits[4], bits[3], bits[2], bits[1], bits[0])
    own = (wq_own, wk_own, wo_own, wd_own, wg_own)
    held = (held_q, held_k, held_o, held_d, held_g)
    full = (wq_all, wk_all, wo_all, wd_all, wg_all)

    def where(bit_set):
        return tuple(pl.ds(0, 2) if b in bit_set else bits[b] for b in (4, 3, 2, 1, 0))

    def remote(src, dst, send, recv, bit):
        return pltpu.make_async_remote_copy(
            src, dst, send, recv, device_id=flip(me, bits, bit), device_id_type=MESH
        )

    units = []
    for u in range(3):
        units.append((0, 0, even_odd(u, 4 * u, 4 * u + 2)))
    units.append((1, 0, ((0, 1, ORD_A), (1, 1, ORD_C2))))
    for u in range(3):
        units.append((2, 0, even_odd(u, 4 * u, 4 * u + 2)))
    thick = wd_own.shape[0] // 3
    for u in range(9):
        units.append((3, u // 3 * thick, even_odd(u + 1, u % 3 * 4, u % 3 * 4 + 2)))
    first = len(units)

    def exchange(u, cl, k):
        w, row, split = units[u]
        tile, tiles, order = split[cl]
        lines = pl.ds(row, wq_own.shape[0])
        cols = pl.ds(tile * 128, tiles * 128)
        there = full[w].at[where(order[:k]) + (lines, cols)]
        return remote(
            there if k else own[w].at[lines, cols],
            there,
            xsend.at[u, cl, k],
            xrecv.at[u, cl, k],
            order[k],
        )

    def gate(v, par, cl, k):
        tile, tiles, order = even_odd(par, 0, ff // 128)[cl]
        at = tile * 128 + v * UNIT
        cols = pl.ds(at if isinstance(at, int) else pl.multiple_of(at, 128), tiles * 128)
        there = wg_all.at[where(order[:k]) + (slice(None), cols)]
        return remote(
            there if k else wg_own.at[:, cols],
            there,
            xsend.at[first + v, cl, k],
            xrecv.at[first + v, cl, k],
            order[k],
        )

    staged = [pltpu.make_async_copy(own[w], held[w], own_sem.at[w]) for w in range(5)]
    placed = [pltpu.make_async_copy(held[w], full[w].at[here], own_sem.at[w]) for w in range(5)]
    for copy in staged:
        copy.start()
    late = [
        pltpu.make_async_copy(src, dst, late_sem.at[i])
        for i, (src, dst) in enumerate(
            (
                (gb_hbm, gb_ref),
                (da_hbm, da_ref),
                (a1_ref, a1_hbm),
                (q_ref, q_hbm),
                (keys_ref, keys_hbm),
                (att_ref, att_hbm),
            )
        )
    ]
    late[0].start()
    late[1].start()
    done_place = set()

    def place(w):
        if w not in done_place:
            done_place.add(w)
            placed[w].wait()

    order = []
    for t in range(AHEAD):
        for k in (4, 3, 2, 1, 0):
            u = t - LAGS[k]
            if 0 <= u < first + nu:
                order.append((t + (4 - k) / 5, u, k))

    def steps(n):
        while order and order[0][0] < n:
            unused, u, k = order.pop(0)
            w = units[u][0] if u < first else 4
            if k:
                place(w)
            for cl in range(2 if w == 1 else 3):
                at = (
                    functools.partial(exchange, u, cl)
                    if u < first
                    else functools.partial(gate, u - first, (u - first) % 2, cl)
                )
                if k:
                    at(k - 1).wait_recv()
                at(k).start()

    def loop_steps(c, point):
        for i in (2 * point, 2 * point + 1):
            t, k = i // 5, 4 - i % 5
            v = 2 * c + t + AHEAD - first - LAGS[k]
            par = (t + AHEAD - first - LAGS[k]) % 2

            @pl.when(v < nu)
            def _(v=v, par=par, k=k):
                for cl in range(3):
                    if k:
                        gate(v, par, cl, k - 1).wait_recv()
                    gate(v, par, cl, k).start()

    def arrived(weight_at):
        for u, unit in enumerate(units):
            if unit[0] == weight_at:
                for cl in range(len(unit[2])):
                    exchange(u, cl, 4).wait_recv()

    def load(w, lo, n, slot, at, sem):
        return pltpu.make_async_copy(
            full[w].at[(slice(None),) * 6 + (pl.ds(lo, n),)],
            wbuf.at[(slot,) + (slice(None),) * 6 + (pl.ds(at, n),)],
            wsem.at[slot, sem],
        )

    def weight(slot, lo, n):
        return wbuf[slot, :, :, :, :, :, :, lo : lo + n].reshape(-1, n)

    for w in range(5):
        staged[w].wait()
        placed[w].start()
    steps(4)
    mask_ref[...] = mask_at(lens_ref, ids_ref, count, me, rows)

    def read_x(at):
        return x_ref[at, :].astype(f32)

    def write_a1(at, y):
        a1_ref[at, :] = y

    norm_rows(read_x, gain1_ref, write_a1, rows)
    iq_ref[...] = (dot(a1_ref[...], qa_ref[...]) * mask_ref[...]).astype(bf16)
    ik_ref[...] = (dot(a1_ref[...], ka_ref[...]) * mask_ref[...]).astype(bf16)
    did_s[...] = (dot(g_ref[...], db_ref[...], NT) * mask_ref[...]).astype(bf16)
    late[2].start()
    steps(KEYS_AT)
    arrived(0)
    arrived(1)
    loads = [load(0, 0, 1024, 0, 0, 0), load(0, 1024, d - 1024, 1, 0, 0)]
    loads.append(load(1, 0, 2 * HD, 1, d - 1024, 1))
    for copy in loads:
        copy.start()
    for copy in loads:
        copy.wait()

    def beside(a, b):
        return jnp.concatenate([a, b], axis=1)

    def under(a, b):
        return jnp.concatenate([a, b], axis=0)

    kv_own[...] = dot(
        beside(a1_ref[...], ik_ref[...]), under(weight(1, d - 1024, 2 * HD), kb_ref[...])
    ).astype(bf16)
    keys_ref[0, pl.ds(reach * width, width)] = kv_own[pl.ds(0, width)]
    keys_ref[1, pl.ds(reach * width, width)] = kv_own[pl.ds(width, width)]

    def low(j):
        block = me + j
        upper = block // count
        target = block + upper * (2 * count - 1 - 2 * block)
        copy = pltpu.make_async_remote_copy(
            kv_own.at[pl.ds(0, width)],
            keys_ref.at[upper, pl.ds((reach - j) * width, width)],
            hsend.at[0, j],
            hrecv.at[upper, j],
            device_id=(target,),
            device_id_type=MESH,
        )
        return copy, target

    def high(j):
        return pltpu.make_async_remote_copy(
            kv_own.at[pl.ds(width, width)],
            keys_ref.at[1, pl.ds((reach - j) * width, width)],
            hsend.at[1, j],
            hrecv.at[1, j],
            device_id=(me - j,),
            device_id_type=MESH,
        )

    def incoming(which, j):
        return pltpu.make_async_remote_copy(
            kv_own.at[pl.ds(0, width)],
            keys_ref.at[which, pl.ds((reach - j) * width, width)],
            hsend.at[0, j],
            hrecv.at[which, j],
            device_id=flip(me, bits, 0),
            device_id_type=MESH,
        )

    for j in range(1, reach + 1):
        copy, target = low(j)
        pl.when(target != me)(copy.start)
        pl.when(me >= j)(high(j).start)

        @pl.when(target == me)
        def _(j=j):
            keys_ref[1, pl.ds((reach - j) * width, width)] = kv_own[pl.ds(0, width)]

        @pl.when(me < j)
        def _(j=j):
            keys_ref[0, pl.ds((reach - j) * width, width)] = jnp.zeros((width, 2 * HD), bf16)

    steps(KEYS_AT + 1)
    q_ref[:, :1024] = dot(
        beside(a1_ref[...], iq_ref[...]), under(weight(0, 0, 1024), qb_ref[:, :1024])
    ).astype(bf16)
    q_ref[:, 1024:] = dot(
        beside(a1_ref[...], iq_ref[...]), under(weight(1, 0, d - 1024), qb_ref[:, 1024:])
    ).astype(bf16)
    for j in range(1, reach + 1):
        pl.when(me >= j)(incoming(0, j).wait_recv)
        pl.when(2 * me != 2 * count - 1 - j)(incoming(1, j).wait_recv)
    late[3].start()
    late[4].start()
    steps(KEYS_AT + 2)

    groups = HEADS // GROUP
    subs = width // SUB
    turn = 0
    for which in range(2):
        for s in range(subs):
            block = me if which == 0 else 2 * count - 1 - me
            base = s * SUB
            lines = slice(which * width + base, which * width + base + SUB)
            row = lax.broadcasted_iota(jnp.int32, (SUB, span), 0)
            col = lax.broadcasted_iota(jnp.int32, (SUB, span), 1)
            ok = (
                (col <= row + (span - SUB))
                & (col > row + (span - SUB - WINDOW))
                & (
                    segment_at(lens_ref, block * width + base + col[:1] - reach * width)
                    == segment_at(lens_ref, block * width + base + row[:, :1])
                )
            )
            acc_a[:SUB, :span] = jnp.where(ok, 0.0, MASKED)

            for g in range(groups):
                heads = slice(g * GROUP * HD, (g + 1) * GROUP * HD)
                k = keys_ref[which, base : base + span, :HD]
                v = keys_ref[which, base : base + span, HD:]
                acc_o[: GROUP * SUB, :span] = dot(heads_down(q_ref[lines, heads]), k, NT)
                slot = turn % 2
                if turn >= 2:
                    pltpu.make_async_copy(
                        pbuf.at[slot], prob_hbm.at[0, 0, pl.ds(0, GROUP * SUB)], psem.at[slot]
                    ).wait()

                def soft(r, unused, slot=slot):
                    at = tile_at(r, 16)
                    bias = acc_a[tile_at(r % (SUB // 16), 16), :span]
                    sc = acc_o[at, :span] * SCALE + bias
                    e = jnp.exp(sc - jnp.max(sc, axis=1, keepdims=True))
                    inv = 1.0 / jnp.sum(e, axis=1, keepdims=True)
                    pbuf[slot, at, :] = (e * inv).astype(bf16)
                    return unused

                lax.fori_loop(0, GROUP * SUB // 16, soft, 0, unroll=SOFT_UNROLL)
                pltpu.make_async_copy(
                    pbuf.at[slot],
                    prob_hbm.at[which, s, pl.ds(g * GROUP * SUB, GROUP * SUB)],
                    psem.at[slot],
                ).start()
                att_ref[lines, heads] = heads_across(dot(pbuf[slot], v)).astype(bf16)
                turn += 1
                steps(KEYS_AT + 2 + ATT_STEPS * turn / (2 * subs * groups))
    for slot in range(2):
        pltpu.make_async_copy(
            pbuf.at[slot], prob_hbm.at[0, 0, pl.ds(0, GROUP * SUB)], psem.at[slot]
        ).wait()
    late[5].start()
    arrived(2)
    loads = [load(2, 0, 1024, 0, 0, 0), load(2, 1024, d - 1024, 1, 0, 0)]
    for copy in loads:
        copy.start()
    io_ref[...] = (dot(att_ref[...], oa_ref[...]) * mask_ref[...]).astype(bf16)
    for copy in loads:
        copy.wait()
    dmid_ref[:, :1024] = x_ref[:, :1024].astype(f32) + dot(
        beside(att_ref[...], io_ref[...]), under(weight(0, 0, 1024), ob_ref[:, :1024])
    )
    dmid_ref[:, 1024:] = x_ref[:, 1024:].astype(f32) + dot(
        beside(att_ref[...], io_ref[...]), under(weight(1, 0, d - 1024), ob_ref[:, 1024:])
    )
    steps(KEYS_AT + 2 + ATT_STEPS + 1)

    def read_mid(at):
        return dmid_ref[at, :]

    def write_a2(at, y):
        a2_s[at, :] = y

    norm_rows(read_mid, gain2_ref, write_a2, rows)
    igu_s[...] = (dot(a2_s[...], ga_ref[...]) * mask_ref[...]).astype(bf16)
    acc_o[...] = jnp.zeros_like(acc_o)
    acc_a[...] = jnp.zeros_like(acc_a)
    steps(AHEAD)
    arrived(3)

    def arrived_gate(c):
        for j in range(CHUNK // UNIT):
            for cl in range(3):
                gate(c * (CHUNK // UNIT) + j, j % 2, cl, 4).wait_recv()

    def down_rows(c):
        return wd_rows.at[tile_at(c, CHUNK)]

    wd_rows = wd_all.reshape(ff, d)

    def fetch(c, slot):
        cps = [
            pltpu.make_async_copy(
                wg_all.at[(slice(None),) * 6 + (tile_at_base(base, c),)],
                wbuf.at[(slot,) + (slice(None),) * 6 + (pl.ds(o, CHUNK),)],
                wsem.at[slot, i],
            )
            for i, (base, o) in enumerate(((0, 0), (ff, CHUNK)))
        ]
        cps.append(pltpu.make_async_copy(down_rows(c), dbuf.at[slot], dsem.at[slot]))
        return cps

    def tile_at_base(base, c):
        at = base + c * CHUNK
        return pl.ds(at if isinstance(at, int) else pl.multiple_of(at, 128), CHUNK)

    late[0].wait()
    late[1].wait()
    arrived_gate(0)
    for copy in fetch(0, 0):
        copy.start()
    for copy in fetch(0, 0):
        copy.wait()

    def chunk(c, unused):
        slot = c % 2
        loop_steps(c, 0)
        gbc = beside(gb_ref[:, tile_at_base(0, c)], gb_ref[:, tile_at_base(ff, c)])
        dac = da_ref[tile_at(c, CHUNK), :]

        def wx():
            return under(weight(slot, 0, 2 * CHUNK), gbc)

        def wdx():
            return beside(dbuf[slot], dac)

        gu_s[...] = dot(beside(a2_s[...], igu_s[...]), wx())
        loop_steps(c, 1)
        dh_s[...] = dot(beside(g_ref[...], did_s[...]), wdx(), NT)
        k0 = 0.7978845608028654

        def glu(r, unused):
            at = tile_at(r, 16)
            gate_v, up, dh = gu_s[at, :CHUNK], gu_s[at, CHUNK:], dh_s[at, :]
            sq = gate_v * gate_v
            th = jnp.tanh(gate_v * (k0 + (k0 * 0.044715) * sq))
            ht = 0.5 + 0.5 * th
            gl = gate_v * ht
            dgl = ht + (gate_v * (0.5 - 0.5 * th * th)) * (k0 + (3 * k0 * 0.044715) * sq)
            hid_s[at, :] = (gl * up).astype(bf16)
            dgu_s[at, :CHUNK] = (dh * up * dgl).astype(bf16)
            dgu_s[at, CHUNK:] = (dh * gl).astype(bf16)
            return unused

        loop_steps(c, 2)
        lax.fori_loop(0, rows // 16, glu, 0)
        loop_steps(c, 3)
        acc_o[...] += dot(hid_s[...], wdx())
        loop_steps(c, 4)
        gda_ref[tile_at(c, CHUNK), :] = dot(hid_s[...], did_s[...], TN).astype(bf16)
        r = dot(igu_s[...], dgu_s[...], TN).astype(bf16)
        for i in range(2):
            for j in range(CHUNK // 128):
                lo = i * CHUNK + j * 128
                ggb_ref[pl.ds(c * (CHUNK // 128) + (ff // 128) * i + j, 1)] = r[
                    None, :, lo : lo + 128
                ]

        @pl.when(c + 1 < nc)
        def _():
            arrived_gate(c + 1)
            for copy in fetch(c + 1, 1 - slot):
                copy.start()

        acc_a[...] += dot(dgu_s[...], wx(), NT)

        @pl.when(c + 1 < nc)
        def _():
            for copy in fetch(c + 1, 1 - slot):
                copy.wait()

        return unused

    lax.fori_loop(0, nc, chunk, 0)
    inner_d = (acc_o[:, d:] * mask_ref[...]).astype(bf16)
    acc_o[:, :d] += dot(inner_d, db_ref[...])
    r = dot(inner_d, g_ref[...], TN).astype(bf16)
    for j in range(d // 128):
        gdb_ref[j] = r[:, j * 128 : (j + 1) * 128]
    dgu = (acc_a[:, d:] * mask_ref[...]).astype(bf16)
    gga_ref[...] = dot(a2_s[...], dgu, TN).astype(bf16)
    acc_a[:, :d] += dot(dgu, ga_ref[...], NT)

    def finish(r, unused):
        at = tile_at(r, 16)
        mid = dmid_ref[at, :]
        out_ref[at, :] = (mid + acc_o[at, :d]).astype(bf16)
        e = acc_a[at, :d] * gain2_ref[...][None, :]
        rr = lax.rsqrt(jnp.mean(mid * mid, axis=1, keepdims=True) + NORM_EPS)
        pull = (rr * rr * rr) * jnp.mean(e * mid, axis=1, keepdims=True)
        dmid_ref[at, :] = g_ref[at, :].astype(f32) + rr * e - pull * mid
        return unused

    lax.fori_loop(0, rows // 16, finish, 0, unroll=8)
    for j in range(1, reach + 1):
        copy, target = low(j)
        pl.when(target != me)(copy.wait_send)
        pl.when(me >= j)(high(j).wait_send)
    for copy in late[2:]:
        copy.wait()
    for u, unit in enumerate(units):
        for cl in range(len(unit[2])):
            for k in range(5):
                exchange(u, cl, k).wait_send()

    def sent(v, unused):
        for par in range(2):
            for cl in range(3):
                for k in range(5):
                    gate(2 * v + par, par, cl, k).wait_send()
        return unused

    lax.fori_loop(0, nu // 2, sent, 0)


def forward(count, small, weights):
    x, g = small[0], small[1]
    rows, d = x.shape
    ff = weights[3].shape[0] * count
    width = rows // 2
    keys = WINDOW + width
    span = keys - width + SUB
    nu = ff // UNIT
    S = jax.ShapeDtypeStruct
    full = [S((2,) * 5 + w.shape, bf16) for w in weights]
    outs = [
        S((rows, d), bf16),
        S((rows, d), f32),
        S((rows, d), bf16),
        S((rows, d), bf16),
        S((2, keys, 2 * HD), bf16),
        S((rows, d), bf16),
        S((rows, 128), bf16),
        S((rows, 128), bf16),
        S((rows, 128), bf16),
        S((d, 128), bf16),
        S((2 * ff // 128, 128, 128), bf16),
        S((ff, 128), bf16),
        S((d // 128, 128, 128), bf16),
    ]
    DMA = pltpu.SemaphoreType.DMA
    return pl.pallas_call(
        functools.partial(forward_kernel, count),
        in_specs=[VMEM] * 2
        + [SMEM] * 2
        + [VMEM] * (len(small) - 7)
        + [HBM] * 2
        + [VMEM]
        + [HBM] * 5,
        out_specs=[VMEM] * 2 + [HBM] * 4 + [VMEM] * (len(outs) - 6) + [HBM] * 6,
        out_shape=outs + [S((2, width // SUB, HEADS * SUB, span), bf16)] + full,
        scratch_shapes=[pltpu.VMEM(w.shape, bf16) for w in weights]
        + [
            pltpu.VMEM((2,) * 6 + (weights[0].shape[0], 2 * CHUNK), bf16),
            pltpu.VMEM((2, CHUNK, d), bf16),
            pltpu.VMEM((2, GROUP * SUB, span), bf16),
            pltpu.VMEM((rows, 2 * HD), bf16),
            pltpu.VMEM((rows, d), bf16),
            pltpu.VMEM((rows, 128), bf16),
            pltpu.VMEM((rows, 128), bf16),
            pltpu.VMEM((rows, d), bf16),
            pltpu.VMEM((rows, d), bf16),
            pltpu.VMEM((2, keys, 2 * HD), bf16),
            pltpu.VMEM((rows, d), bf16),
            pltpu.VMEM((128, 2 * ff), bf16),
            pltpu.VMEM((ff, 128), bf16),
            pltpu.VMEM((rows, 128), f32),
            pltpu.VMEM((rows, d + 128), f32),
            pltpu.VMEM((rows, d + 128), f32),
            pltpu.VMEM((rows, 2 * CHUNK), f32),
            pltpu.VMEM((rows, CHUNK), f32),
            pltpu.VMEM((rows, CHUNK), bf16),
            pltpu.VMEM((rows, 2 * CHUNK), bf16),
            DMA((2, 2)),
            DMA((2,)),
            DMA((2,)),
            DMA((5,)),
            DMA((16 + nu, 3, 5)),
            DMA((16 + nu, 3, 5)),
            DMA((2, 5)),
            DMA((2, 5)),
            DMA((6,)),
        ],
        compiler_params=pltpu.CompilerParams(
            collective_id=0, has_side_effects=True, vmem_limit_bytes=63 << 20
        ),
        name="forward",
    )(*small, *weights)


ADVANCE = (6, 11)
POINTS = ()


class Sum:
    def __init__(self, me, buf, parts, send, recv):
        self.me, self.bits = me, bits_of(me)
        self.buf, self.parts, self.send, self.recv = buf, parts, send, recv
        tiles = buf.shape[5] // 16
        third, sixth = round(tiles / 3), round(tiles / 6)
        sizes = (third, third, sixth, tiles - 2 * third - sixth)
        self.split, row = [], 0
        for n, order in zip(sizes, (ORD_A, ORD_A2, ORD_B, ORD_B2)):
            self.split.append((row, n * 16, order))
            row += n * 16
        self.queue = [(s, cl) for s in range(1, 11) for cl in range(4)]

    def copy(self, cl, s):
        row, n, order = self.split[cl]
        lines = pl.ds(row, n)
        bits = self.bits
        if s < 5:
            red = order[::-1]
            bit = red[s]
            rem = [b for b in (4, 3, 2, 1, 0) if b not in red[:s]]
            src = self.buf if s == 0 else self.parts[s - 1]
            idx = tuple((1 - bits[b]) if b == bit else pl.ds(0, 2) for b in rem)
            src = src.at[idx + (lines,)]
            dst = self.parts[s].at[(pl.ds(0, 2),) * (4 - s) + (lines,)]
        else:
            bit, have = order[s - 5], order[: s - 5]
            idx = tuple(pl.ds(0, 2) if b in have else bits[b] for b in (4, 3, 2, 1, 0))
            src = dst = self.buf.at[idx + (lines,)]
        return pltpu.make_async_remote_copy(
            src,
            dst,
            self.send.at[cl, s],
            self.recv.at[cl, s],
            device_id=flip(self.me, bits, bit),
            device_id_type=MESH,
        )

    def add(self, cl, s):
        row, n, order = self.split[cl]
        red = order[::-1]
        rem = [b for b in (4, 3, 2, 1, 0) if b not in red[:s]]
        src, dst = (self.buf if s == 0 else self.parts[s - 1]), self.parts[s]
        lines = pl.ds(row, n)
        free = 4 - s

        def one(j, unused):
            at = [(j // (1 << (free - 1 - i))) % 2 for i in range(free)]
            rest = iter(at)
            idx = tuple(self.bits[b] if b == red[s] else next(rest) for b in rem)
            total = src[idx + (lines,)].astype(f32) + dst[tuple(at) + (lines,)].astype(f32)
            dst[tuple(at) + (lines,)] = total.astype(bf16)
            return unused

        lax.fori_loop(0, 1 << free, one, 0)

    def begin(self):
        for cl in range(4):
            self.copy(cl, 0).start()

    def advance(self, n=4):
        for unused in range(n):
            if not self.queue:
                return
            s, cl = self.queue.pop(0)
            before = self.copy(cl, s - 1)
            before.wait_recv()
            before.wait_send()
            if s <= 5:
                self.add(cl, s - 1)
            if s == 5:
                row, n_, unused_order = self.split[cl]
                b = self.bits
                self.buf[b[4], b[3], b[2], b[1], b[0], pl.ds(row, n_)] = self.parts[4][
                    pl.ds(row, n_)
                ]
            if s < 10:
                self.copy(cl, s).start()


def backward_kernel(
    count,
    dmid_ref,
    x_ref,
    lens_ref,
    ids_ref,
    gain_ref,
    a1_ref,
    q_ref,
    keys_ref,
    att_ref,
    iq_ref,
    ik_ref,
    io_ref,
    qa_ref,
    qb_ref,
    ka_ref,
    kb_ref,
    oa_ref,
    ob_ref,
    gga_hbm,
    ggb_hbm,
    gda_hbm,
    gdb_hbm,
    prob_hbm,
    wq_all,
    wk_all,
    wo_all,
    dx_ref,
    one,
    two,
    pa0,
    pa1,
    pa2,
    pa3,
    pa4,
    pb0,
    pb1,
    pb2,
    pb3,
    pb4,
    mask_ref,
    wbuf,
    pbuf,
    grad_s,
    small_s,
    dkv_s,
    acc,
    hout,
    hin,
    wsem,
    psem,
    gsem,
    send1,
    recv1,
    send2,
    recv2,
    hsend,
    hrecv,
):
    rows, d = x_ref.shape
    width = rows // 2
    reach = WINDOW // width
    keys = keys_ref.shape[1]
    span = keys - width + SUB
    me = lax.axis_index("ctx")
    bits = bits_of(me)
    meet_all(count, me)
    flat_one = one.reshape(-1, 128)
    flat_two = two.reshape(-1, 128)
    hid_rows = gda_hbm.shape[0]
    gates = ggb_hbm.shape[0] * 128
    at_ggb = d
    at_gda = at_ggb + gates
    at_gdb = at_gda + hid_rows
    at_goa = at_gdb + d
    at_gob = at_goa + d
    at_qb, at_ka, at_kb = d, 2 * d, 3 * d

    def whole(ref):
        return ref.at[(slice(None),) * 7]

    loads = [
        pltpu.make_async_copy(wo_all, wbuf.at[(slice(None),) * 6 + (pl.ds(0, d),)], wsem.at[0])
    ]
    grads = [
        pltpu.make_async_copy(src.reshape(-1, 128), flat_one.at[pl.ds(at, n)], gsem.at[i])
        for i, (src, at, n) in enumerate(
            (
                (gga_hbm, 0, d),
                (ggb_hbm, at_ggb, gates),
                (gda_hbm, at_gda, hid_rows),
                (gdb_hbm, at_gdb, d),
            )
        )
    ]
    groups = HEADS // GROUP
    subs = width // SUB
    turns = [(w, s, g) for w in range(2) for s in range(subs) for g in range(groups)]

    def prob(n):
        w, s, g = turns[n]
        return pltpu.make_async_copy(
            prob_hbm.at[w, s, pl.ds(g * GROUP * SUB, GROUP * SUB)], pbuf.at[n % 2], psem.at[n % 2]
        )

    for copy in loads + grads + [prob(0), prob(1)]:
        copy.start()

    def beside(*xs):
        return jnp.concatenate(xs, axis=1)

    def weight(lo, n):
        return wbuf[:, :, :, :, :, :, lo : lo + n].reshape(-1, n)

    def store_tiles(flat, at, x):
        for j in range(x.shape[1] // 128):
            flat[pl.ds(at + j * 128, 128)] = x[:, j * 128 : (j + 1) * 128].astype(bf16)

    mask_ref[...] = mask_at(lens_ref, ids_ref, count, me, rows)
    grad_s[...] = dmid_ref[...].astype(bf16)
    small_s[:, :128] = (dot(grad_s[...], ob_ref[...], NT) * mask_ref[...]).astype(bf16)
    flat_one[pl.ds(at_goa, d)] = dot(att_ref[...], small_s[:, :128], TN).astype(bf16)
    store_tiles(flat_one, at_gob, dot(io_ref[...], grad_s[...], TN))
    for copy in grads:
        copy.wait()
    first = Sum(me, one, (pa0, pa1, pa2, pa3, pa4), send1, recv1)
    second = Sum(me, two, (pb0, pb1, pb2, pb3, pb4), send2, recv2)
    first.begin()
    for copy in loads:
        copy.wait()
    acc[:, :d] = dot(
        beside(grad_s[...], small_s[:, :128]), beside(weight(0, d), oa_ref[...]), NT
    )
    grad_s[...] = acc[:, :d].astype(bf16)
    loads = [
        pltpu.make_async_copy(wq_all, wbuf.at[(slice(None),) * 6 + (pl.ds(0, d),)], wsem.at[0]),
        pltpu.make_async_copy(
            wk_all, wbuf.at[(slice(None),) * 6 + (pl.ds(d, 2 * HD),)], wsem.at[1]
        ),
    ]
    for copy in loads:
        copy.start()
    dkv_s[...] = jnp.zeros_like(dkv_s)
    first.advance()

    for n, (which, s, g) in enumerate(turns):
        base = s * SUB
        lines = slice(which * width + base, which * width + base + SUB)
        heads = slice(g * GROUP * HD, (g + 1) * GROUP * HD)
        k = keys_ref[which, base : base + span, :HD]
        v = keys_ref[which, base : base + span, HD:]
        q = heads_down(q_ref[lines, heads])
        do = heads_down(grad_s[lines, heads])
        o = heads_down(att_ref[lines, heads])
        delta = jnp.sum(do.astype(f32) * o.astype(f32), axis=1, keepdims=True)
        prob(n).wait()
        p = pbuf[n % 2]
        ds = (p.astype(f32) * (dot(do, v, NT) - delta)).astype(bf16)
        dkv_s[which, HD:, base : base + span] += dot(do.T, p)
        dkv_s[which, :HD, base : base + span] += dot(q.T, ds) * SCALE
        grad_s[lines, heads] = heads_across(dot(ds, k) * SCALE).astype(bf16)
        if n + 2 < len(turns):
            prob(n + 2).start()
        if n in ADVANCE:
            first.advance()

    def piece(which, j):
        lo = (reach - j) * width
        return dkv_s[which, :, lo : lo + width].T

    for j in range(1, reach + 1):
        for which in range(2):
            hout[which, j - 1] = piece(which, j).astype(bf16)

    def low(j):
        return pltpu.make_async_remote_copy(
            hout.at[0, j - 1],
            hin.at[0, j - 1],
            hsend.at[0, j],
            hrecv.at[0, j],
            device_id=(me - j,),
            device_id_type=MESH,
        )

    def high(j):
        block = 2 * count - 1 - me - j
        upper = block // count
        target = block + upper * (2 * count - 1 - 2 * block)
        copy = pltpu.make_async_remote_copy(
            hout.at[1, j - 1],
            hin.at[upper, j - 1],
            hsend.at[1, j],
            hrecv.at[upper, j],
            device_id=(target,),
            device_id_type=MESH,
        )
        return copy, target

    def incoming(half, j):
        return pltpu.make_async_remote_copy(
            hout.at[0, j - 1],
            hin.at[half, j - 1],
            hsend.at[0, j],
            hrecv.at[half, j],
            device_id=flip(me, bits, 0),
            device_id_type=MESH,
        )

    for j in range(1, reach + 1):
        pl.when(me >= j)(low(j).start)
        copy, target = high(j)
        pl.when(target != me)(copy.start)
    if 1 in POINTS:
        first.advance()
    small_s[:, :128] = (dot(grad_s[...], qb_ref[...], NT) * mask_ref[...]).astype(bf16)
    flat_two[pl.ds(0, d)] = dot(a1_ref[...], small_s[:, :128], TN).astype(bf16)
    store_tiles(flat_two, at_qb, dot(iq_ref[...], grad_s[...], TN))
    used = 3 * d + 2 * HD
    spare = flat_two.shape[0] - used
    flat_two[pl.ds(used, spare)] = jnp.zeros((spare, 128), bf16)
    first.advance()
    for half in range(2):
        own = dkv_s[half, :, reach * width :].T
        acc[half * width : (half + 1) * width, : 2 * HD] = own
    for j in range(1, reach + 1):
        lower_self = 2 * me == 2 * count - 1 - j

        @pl.when(jnp.logical_not(lower_self))
        def _(j=j):
            incoming(0, j).wait_recv()
            acc[:width, : 2 * HD] += hin[0, j - 1].astype(f32)

        @pl.when(lower_self)
        def _(j=j):
            acc[:width, : 2 * HD] += hout[1, j - 1].astype(f32)

        @pl.when(me >= j)
        def _(j=j):
            incoming(1, j).wait_recv()
            acc[width:, : 2 * HD] += hin[1, j - 1].astype(f32)

    if 2 in POINTS:
        first.advance()
    small_s[:, 128 : 128 + 2 * HD] = acc[:, : 2 * HD].astype(bf16)
    dkv = small_s[:, 128 : 128 + 2 * HD]
    small_s[:, 128 + 2 * HD :] = (dot(dkv, kb_ref[...], NT) * mask_ref[...]).astype(bf16)
    flat_two[pl.ds(at_ka, d)] = dot(a1_ref[...], small_s[:, 128 + 2 * HD :], TN).astype(bf16)
    store_tiles(flat_two, at_kb, dot(ik_ref[...], small_s[:, 128 : 128 + 2 * HD], TN))
    second.begin()
    first.advance()
    for copy in loads:
        copy.wait()
    acc[:, :d] = dot(
        beside(grad_s[...], small_s[...]),
        beside(weight(0, d), qa_ref[...], weight(d, 2 * HD), ka_ref[...]),
        NT,
    )
    second.advance()
    first.advance()

    def finish(r, unused):
        at = tile_at(r, 16)
        x = x_ref[at, :].astype(f32)
        e = acc[at, :d] * gain_ref[...][None, :]
        rr = lax.rsqrt(jnp.mean(x * x, axis=1, keepdims=True) + NORM_EPS)
        pull = (rr * rr * rr) * jnp.mean(e * x, axis=1, keepdims=True)
        dx_ref[at, :] = (dmid_ref[at, :] + rr * e - pull * x).astype(bf16)
        return unused

    lax.fori_loop(0, rows // 16, finish, 0, unroll=8)
    while first.queue:
        second.advance()
        first.advance()

    second.advance(40)
    for j in range(1, reach + 1):
        pl.when(me >= j)(low(j).wait_send)
        copy, target = high(j)
        pl.when(target != me)(copy.wait_send)


def backward(count, small, large):
    rows, d = small[0].shape
    gates, hid = large[1].shape[0] * 128, large[2].shape[0]
    keys = small[7].shape[1]
    span = keys - rows // 2 + SUB
    one = (2 * d + gates + hid + 2 * d) // 32
    two = -(-(3 * d + 2 * HD) // 512) * 16
    S = jax.ShapeDtypeStruct
    V = pltpu.VMEM
    DMA = pltpu.SemaphoreType.DMA
    five = (2,) * 5
    outs = [S((rows, d), bf16), S(five + (one, 128), bf16), S(five + (two, 128), bf16)]
    return pl.pallas_call(
        functools.partial(backward_kernel, count),
        in_specs=[VMEM] * 2 + [SMEM] * 2 + [VMEM] * (len(small) - 4) + [HBM] * len(large),
        out_specs=[VMEM] * len(outs),
        out_shape=outs,
        scratch_shapes=[V((2,) * (4 - s) + (one, 128), bf16) for s in range(5)]
        + [V((2,) * (4 - s) + (two, 128), bf16) for s in range(5)]
        + [
            V((rows, 128), f32),
            V(five + (d // 32, d + 2 * HD), bf16),
            V((2, GROUP * SUB, span), bf16),
            V((rows, d), bf16),
            V((rows, 256 + 2 * HD), bf16),
            V((2, 2 * HD, keys), f32),
            V((rows, d), f32),
            V((2, 4, rows // 2, 2 * HD), bf16),
            V((2, 4, rows // 2, 2 * HD), bf16),
            DMA((2,)),
            DMA((2,)),
            DMA((4,)),
            DMA((4, 10)),
            DMA((4, 10)),
            DMA((4, 10)),
            DMA((4, 10)),
            DMA((2, 5)),
            DMA((2, 5)),
        ],
        compiler_params=pltpu.CompilerParams(
            collective_id=1, has_side_effects=True, vmem_limit_bytes=63 << 20
        ),
        name="backward",
    )(*small, *large)


def unpack_kernel(places, one_hbm, two_hbm, *refs):
    n = len(places)
    outs, ins, wide = refs[:n], refs[n : 2 * n], refs[2 * n : 3 * n]
    in_sem, out_sem = refs[3 * n :]
    flat = [one_hbm.reshape(-1, 128), two_hbm.reshape(-1, 128)]
    reads = [
        pltpu.make_async_copy(flat[w].at[pl.ds(at, ins[i].shape[0])], ins[i], in_sem.at[i])
        for i, (w, at, tiled) in enumerate(places)
    ]
    writes = [pltpu.make_async_copy(wide[i], outs[i], out_sem.at[i]) for i in range(n)]
    for copy in reads:
        copy.start()
    for i, (w, at, tiled) in enumerate(places):
        reads[i].wait()
        if tiled:
            for j in range(wide[i].shape[1] // 128):
                wide[i][:, j * 128 : (j + 1) * 128] = ins[i][pl.ds(j * 128, 128)].astype(f32)
        else:
            wide[i][...] = ins[i][...].astype(f32)
        writes[i].start()
    for copy in writes:
        copy.wait()


def unpack(one, two, shapes, places):
    rows = [a * b // 128 for a, b in shapes]
    n = len(shapes)
    return pl.pallas_call(
        functools.partial(unpack_kernel, places),
        in_specs=[HBM] * 2,
        out_specs=[HBM] * n,
        out_shape=[jax.ShapeDtypeStruct(s, f32) for s in shapes],
        scratch_shapes=[pltpu.VMEM((r, 128), bf16) for r in rows]
        + [pltpu.VMEM(s, f32) for s in shapes]
        + [pltpu.SemaphoreType.DMA((n,)), pltpu.SemaphoreType.DMA((n,))],
        compiler_params=pltpu.CompilerParams(vmem_limit_bytes=40 << 20),
        name="unpack",
    )(one, two)


def local_own(
    tokens,
    cotangent,
    doc_lengths,
    adapter_ids,
    w_query,
    w_keyval,
    w_output,
    w_gateup,
    w_down,
    gain_attn,
    gain_mlp,
    query_a,
    query_b,
    keyval_a,
    keyval_b,
    output_a,
    output_b,
    gateup_a,
    gateup_b,
    down_a,
    down_b,
):
    count = lax.axis_size("ctx")
    (
        result,
        grad_middle,
        act_one,
        query,
        keys,
        attention,
        inner_query,
        inner_keyval,
        inner_output,
        g_gateup_a,
        g_gateup_b,
        g_down_a,
        g_down_b,
        prob,
        full_query,
        full_keyval,
        full_output,
        unused_down,
        unused_gateup,
    ) = forward(
        count,
        (
            tokens,
            cotangent,
            doc_lengths,
            adapter_ids,
            gain_attn,
            gain_mlp,
            query_a,
            query_b,
            keyval_a,
            keyval_b,
            output_a,
            output_b,
            gateup_a,
            gateup_b,
            down_a,
            down_b,
        ),
        (w_query, w_keyval, w_output, w_down, w_gateup),
    )
    grad_tokens, first, second = backward(
        count,
        (
            grad_middle,
            tokens,
            doc_lengths,
            adapter_ids,
            gain_attn,
            act_one,
            query,
            keys,
            attention,
            inner_query,
            inner_keyval,
            inner_output,
            query_a,
            query_b,
            keyval_a,
            keyval_b,
            output_a,
            output_b,
        ),
        (
            g_gateup_a,
            g_gateup_b,
            g_down_a,
            g_down_b,
            prob,
            full_query,
            full_keyval,
            full_output,
        ),
    )
    d, hid, gates = w_output.shape[1], down_a.shape[0], gateup_b.shape[1]
    kv = w_keyval.shape[1]
    shapes = [(d, 128), (128, d), (d, 128), (128, kv), (d, 128), (128, d)]
    shapes += [(d, 128), (128, gates), (hid, 128), (128, d)]
    places = [
        (1, 0, False),
        (1, d, True),
        (1, 2 * d, False),
        (1, 3 * d, True),
        (0, 2 * d + gates + hid, False),
        (0, 3 * d + gates + hid, True),
        (0, 0, False),
        (0, d, True),
        (0, d + gates, False),
        (0, d + gates + hid, True),
    ]
    sums = unpack(first, second, shapes, places)
    return (result, grad_tokens, *sums)


def solution(mesh):
    in_specs = (
        P("ctx", None),
        P("ctx", None),
        P(),
        P(),
        P("ctx", None),
        P("ctx", None),
        P("ctx", None),
        P("ctx", None),
        P("ctx", None),
        P(),
        P(),
        P(),
        P(),
        P(),
        P(),
        P(),
        P(),
        P(),
        P(),
        P(),
        P(),
    )
    out_specs = (P("ctx", None), P("ctx", None), P(), P(), P(), P(), P(), P(), P(), P(), P(), P())
    local = local_own if mesh.shape["ctx"] == 32 else local_native
    return jax.shard_map(local, mesh=mesh, in_specs=in_specs, out_specs=out_specs, check_vma=False)
```
